32 devices in a mesh: grp: 2 (over x), seq: 16 (over z, y, core).
Axes of the slice: x: 2, y: 2, z: 4, core: 2. Of those that a mesh axis runs over, the one named last changes fastest.
Arguments:
- queries: bfloat16 [6144, 4096], P(('grp', 'seq')), parts along dimension 0, may hold values from -6 to 6
- keys: bfloat16 [6144, 4096], P(('grp', 'seq')), parts along dimension 0, may hold values from -6 to 6
- values: bfloat16 [6144, 4096], P(('grp', 'seq')), parts along dimension 0, may hold values from -6 to 6
- latent_in: float32 [6144, 64], P(('grp', 'seq')), parts along dimension 0, may hold values from -6 to 6
- mod_table: float32 [16, 2, 4096], replicated, may hold values from -3 to 3
- step_size: float32 [16], replicated, may hold values from 0.25 to 1
- timestep: int32 [64], P('grp'), parts along dimension 0, may hold values from 0 to 15
- head_weight: float32 [4096, 64], replicated, may hold values from -0.09375 to 0.09375
- conv_in_weight: bfloat16 [27, 16, 384], replicated, may hold values from -0.3125 to 0.3125
- conv_in_bias: float32 [384], replicated, may hold values from -3 to 3
- norm_gain: float32 [384], replicated, may hold values from 0.1 to 1.9
- conv_weight: bfloat16 [27, 384, 384], replicated, may hold values from -0.0625 to 0.0625
- conv_bias: float32 [384], replicated, may hold values from -3 to 3
- patch_weight: bfloat16 [1536, 1024], replicated, may hold values from -0.15625 to 0.15625
- patch_gain: float32 [1024], replicated, may hold values from 0.1 to 1.9
- post_gain: float32 [1024], replicated, may hold values from 0.1 to 1.9
- proj_weight: float32 [1024, 768], replicated, may hold values from -0.1875 to 0.1875
- text_table: bfloat16 [24704, 768], P(None, 'seq'), may hold values from -6 to 6
- prompt_ids: int32 [154], P('grp'), parts along dimension 0, may hold values from 0 to 24703
- frame_order: int32 [64], P('grp'), parts along dimension 0, may hold values from 0 to 31, each once
Outputs:
- latent_next: float32 [6144, 64], P(('grp', 'seq')), parts along dimension 0
- decoded: bfloat16 [64, 16, 24, 384], P(('grp', 'seq')), parts along dimension 0
- image_embed: float32 [64, 768], P(('grp', 'seq')), parts along dimension 0
- scores: float32 [64], P(('grp', 'seq')), parts along dimension 0
The draws below stay inside these ranges and needn't reach their ends.
There are 2 independent parts, one for each index of `grp`. The reference program is written for one: setup_inputs(seed, part) draws one part's arguments, and reference() takes and returns one part's arrays. A program takes and returns all parts, laid end to end along the dimension named above; an argument that names none is the same for every part. Nothing has to cross between parts.
All inputs are finite; a program needn't handle non-finite values.
Results may differ from the reference program's by a relative error of at most 0.009.
Values may be sent and summed in bfloat16 or wider, within the bound.
A program may use at most 128 MiB of HBM per device.

```python
import jax
import jax.numpy as jnp
from jax import lax

GRID_H = 8
GRID_W = 12
HEADS = 32
HD = 128
LAT_C = 16
CH = 384
VIT_W = 1024
TEXT_W = 768
VOCAB = 24704
PROMPT = 77
STEPS = 16
FRAMES = 32
TOKENS = 3072


def backdrop(key):
    canvas = jnp.clip(jax.random.normal(key, (TOKENS, HEADS * HD), jnp.float32), -6.0, 6.0)
    return canvas


def draw_queries(key, part):
    canvas = backdrop(jax.random.fold_in(key, 11))
    return canvas.astype(jnp.bfloat16)


def draw_keys(key, part):
    canvas = backdrop(jax.random.fold_in(key, 12))
    return canvas.astype(jnp.bfloat16)


def touch_ends(drawn, own_key, least, largest):
    longest = drawn.shape.index(max(drawn.shape))
    spots = []
    for shift in (0, 1):
        where = [jax.random.randint(jax.random.fold_in(own_key, axis), (), 0, length) for axis, length in enumerate(drawn.shape)]
        where[longest] = (where[longest] + shift) % drawn.shape[longest]
        spots.append(tuple(where))
    return drawn.at[spots[0]].set(least).at[spots[1]].set(largest)


def block_levels(key, shape, cuts, smallest, high):
    loudness = 1.0
    for axis_at, shards_of in cuts:
        draws = jax.random.uniform(jax.random.fold_in(jax.random.fold_in(key, 6), axis_at), (shards_of,), jnp.float32, smallest / len(cuts), high / len(cuts))
        loudness = loudness * jnp.repeat(jnp.exp(draws), shape[axis_at] // shards_of).reshape((-1,) + (1,) * (len(shape) - 1 - axis_at))
    return loudness


def scatter_about(own_key, dims, deviation, limit, shards=(), held_as=jnp.bfloat16):
    gain = block_levels(own_key, dims, shards, -0.22, 0.18) if shards else 1.0
    drawn = jax.random.normal(own_key, dims, jnp.float32) * deviation * gain
    return jnp.minimum(jnp.maximum(drawn, -limit), limit).astype(held_as)


def setup_inputs(seed: int = 0, part: int = 0) -> dict:
    key_list = jax.random.split(jax.random.key(seed), 21)
    own_keys = jax.random.split(jax.random.fold_in(key_list[20], part), 21)
    queries = draw_queries(jax.random.fold_in(jax.random.fold_in(key_list[20], part), 71), part)
    keys = draw_keys(jax.random.fold_in(jax.random.fold_in(key_list[20], part), 71), part)
    values = scatter_about(own_keys[2], (TOKENS, HEADS * HD), 1.0, 6.0, ((0, 16),))
    latent_in = scatter_about(own_keys[3], (TOKENS, 4 * LAT_C), 1.0, 6.0, ((0, 16),), jnp.float32)
    mod_table = scatter_about(key_list[4], (STEPS, 2, HEADS * HD), 0.5, 3.0, (), jnp.float32)
    step_size = jnp.clip(jax.random.uniform(key_list[5], (STEPS,), jnp.float32, 0.25, 1.0), 0.25, 1.0)
    timestep = touch_ends(jax.random.randint(own_keys[6], (FRAMES,), 0, STEPS), jax.random.fold_in(own_keys[6], 1), 0, STEPS - 1).astype(jnp.int32)
    head_weight = scatter_about(key_list[7], (HEADS * HD, 4 * LAT_C), (HEADS * HD) ** -0.5, 0.09375, (), jnp.float32)
    conv_in_weight = scatter_about(key_list[8], (27, LAT_C, CH), (27 * LAT_C) ** -0.5, 0.3125)
    conv_in_bias = scatter_about(key_list[9], (CH,), 0.5, 3.0, (), jnp.float32)
    norm_gain = jnp.clip(1.0 + 0.18 * jax.random.normal(key_list[10], (CH,), jnp.float32), 0.1, 1.9)
    conv_weight = scatter_about(key_list[11], (27, CH, CH), (27 * CH) ** -0.5, 0.0625)
    conv_bias = scatter_about(key_list[12], (CH,), 0.5, 3.0, (), jnp.float32)
    patch_weight = scatter_about(key_list[13], (4 * CH, VIT_W), (4 * CH) ** -0.5, 0.15625)
    patch_gain = jnp.clip(1.0 + 0.18 * jax.random.normal(key_list[14], (VIT_W,), jnp.float32), 0.1, 1.9)
    post_gain = jnp.clip(1.0 + 0.18 * jax.random.normal(key_list[15], (VIT_W,), jnp.float32), 0.1, 1.9)
    proj_weight = scatter_about(key_list[16], (VIT_W, TEXT_W), VIT_W ** -0.5, 0.1875, (), jnp.float32)
    text_table = scatter_about(key_list[17], (VOCAB, TEXT_W), 1.0, 6.0, ((1, 16),))
    prompt_ids = touch_ends(jax.random.randint(own_keys[18], (PROMPT,), 0, VOCAB), jax.random.fold_in(own_keys[18], 1), 0, VOCAB - 1).astype(jnp.int32)
    frame_order = jax.random.permutation(own_keys[19], FRAMES).astype(jnp.int32)
    return dict(queries=queries, keys=keys, values=values, latent_in=latent_in, mod_table=mod_table, step_size=step_size, timestep=timestep, head_weight=head_weight, conv_in_weight=conv_in_weight, conv_in_bias=conv_in_bias, norm_gain=norm_gain, conv_weight=conv_weight, conv_bias=conv_bias, patch_weight=patch_weight, patch_gain=patch_gain, post_gain=post_gain, proj_weight=proj_weight, text_table=text_table, prompt_ids=prompt_ids, frame_order=frame_order)


highest = lax.Precision.HIGHEST

def lookup(mod_table, step_size, timestep):
    onehot = (jnp.arange(mod_table.shape[0], dtype=jnp.int32)[None, :] == timestep[:, None]).astype(jnp.float32)
    modulation = jnp.dot(onehot, mod_table.reshape(mod_table.shape[0], -1), precision=highest)
    return (modulation[:, :HEADS * HD], modulation[:, HEADS * HD:], lax.optimization_barrier(jnp.sum(onehot * step_size[None, :], axis=1)))

def attend(queries, keys, values):
    length = queries.shape[0]
    block_rows = 512 if length % 512 == 0 else length

    def split_heads(matrix):
        return matrix.reshape(length, HEADS, HD).transpose(1, 0, 2)

    def one_head(triple):
        head_q, head_k, head_v = triple

        def one_block(rows_q):
            logits = jnp.dot(rows_q, head_k.T, preferred_element_type=jnp.float32) * HD ** (-0.5)
            row_peak = lax.optimization_barrier(jnp.max(logits, axis=-1, keepdims=True))
            exponent = jnp.exp(logits - row_peak)
            weights = (exponent / lax.optimization_barrier(jnp.sum(exponent, axis=-1, keepdims=True))).astype(jnp.bfloat16)
            return jnp.dot(weights, head_v, preferred_element_type=jnp.float32).astype(jnp.bfloat16)
        return lax.map(one_block, head_q.reshape(length // block_rows, block_rows, HD)).reshape(length, HD)
    heads_out = lax.map(one_head, (split_heads(queries), split_heads(keys), split_heads(values)))
    return heads_out.transpose(1, 0, 2).reshape(length, HEADS * HD)

def predict(attended, mod_shift, mod_scale, head_weight):
    frames_n = mod_shift.shape[0]
    attended_f = attended.astype(jnp.float32)
    meansq = lax.optimization_barrier(jnp.mean(attended_f * attended_f, axis=-1, keepdims=True))
    normed = (attended_f * lax.rsqrt(meansq + 1e-06)).reshape(frames_n, -1, attended.shape[1])
    normed = normed * (1.0 + mod_scale[:, None, :]) + mod_shift[:, None, :]
    return jnp.dot(normed.reshape(attended.shape[0], -1), head_weight, precision=highest)

def advance(latent_in, step_dt, prediction):
    frames_n = step_dt.shape[0]
    shaped = latent_in.reshape(frames_n, -1, latent_in.shape[1]) + step_dt[:, None, None] * prediction.reshape(frames_n, -1, latent_in.shape[1])
    return shaped.reshape(latent_in.shape)

def to_frames(latent):
    shaped = latent.reshape(-1, GRID_H, GRID_W, 2, 2, LAT_C).transpose(0, 1, 3, 2, 4, 5)
    return shaped.reshape(-1, 2 * GRID_H, 2 * GRID_W, LAT_C)

def causal_conv(padded, weight):
    frames_n = padded.shape[0] - 2
    rows_h = padded.shape[1]
    cols_w = padded.shape[2]
    spaced = jnp.pad(padded, ((0, 0), (1, 1), (1, 1), (0, 0)))
    summed = jnp.zeros((frames_n * rows_h * cols_w, weight.shape[2]), jnp.float32)
    for lag_t in range(3):
        for row_off in range(3):
            for col_off in range(3):
                window = spaced[lag_t:lag_t + frames_n, row_off:row_off + rows_h, col_off:col_off + cols_w]
                window = window.reshape(-1, spaced.shape[3])
                summed = summed + jnp.dot(window, weight[lag_t * 9 + row_off * 3 + col_off], preferred_element_type=jnp.float32)
    return summed.reshape(frames_n, rows_h, cols_w, weight.shape[2])

def activate(first_out, norm_gain):
    first_f = first_out.astype(jnp.float32)
    meansq = lax.optimization_barrier(jnp.mean(first_f * first_f, axis=-1, keepdims=True))
    return jax.nn.silu(first_f * lax.rsqrt(meansq + 1e-06) * norm_gain).astype(jnp.bfloat16)

def to_patches(decoded):
    shaped = decoded.reshape(-1, GRID_H, 2, GRID_W, 2, CH).transpose(0, 1, 3, 2, 4, 5)
    return shaped.reshape(-1, GRID_H * GRID_W, 4 * CH)

def embed(patches, patch_weight):
    flat_rows = patches.reshape(-1, patches.shape[2])
    product = jnp.dot(flat_rows, patch_weight, preferred_element_type=jnp.float32)
    return product.reshape(patches.shape[0], patches.shape[1], -1).astype(jnp.bfloat16)

def layer_norm(matrix, gain_vec):
    centered = matrix - lax.optimization_barrier(jnp.mean(matrix, axis=-1, keepdims=True))
    variance = lax.optimization_barrier(jnp.mean(centered * centered, axis=-1, keepdims=True))
    return centered * lax.rsqrt(variance + 1e-05) * gain_vec

def describe(embedded, patch_gain, post_gain, proj_weight):
    pooled = lax.optimization_barrier(jnp.mean(layer_norm(embedded.astype(jnp.float32), patch_gain), axis=-2))
    return jnp.dot(layer_norm(pooled, post_gain), proj_weight, precision=highest)

def rate(image_vec, text_vector):
    inner = lax.optimization_barrier(jnp.sum(image_vec * text_vector[None, :], axis=-1))
    image_rms = jnp.sqrt(lax.optimization_barrier(jnp.mean(image_vec * image_vec, axis=-1)) + 1e-06)
    text_rms = jnp.sqrt(jnp.mean(text_vector * text_vector) + 1e-06)
    return 100.0 * inner / (TEXT_W * image_rms * text_rms)

def reference(queries, keys, values, latent_in, mod_table, step_size, timestep, head_weight, conv_in_weight, conv_in_bias, norm_gain, conv_weight, conv_bias, patch_weight, patch_gain, post_gain, proj_weight, text_table, prompt_ids, frame_order):
    mod_shift, mod_scale, step_dt = lookup(mod_table, step_size, timestep)
    attended = attend(queries, keys, values)
    latent_next = advance(latent_in, step_dt, predict(attended, mod_shift, mod_scale, head_weight))
    frames = to_frames(latent_next).astype(jnp.bfloat16)
    zeros_lat = jnp.zeros((2,) + frames.shape[1:], jnp.bfloat16)
    first_out = (causal_conv(jnp.concatenate([zeros_lat, frames], axis=0), conv_in_weight) + conv_in_bias).astype(jnp.bfloat16)
    activated = activate(first_out, norm_gain)
    zeros_act = jnp.zeros((2,) + activated.shape[1:], jnp.bfloat16)
    branch = causal_conv(jnp.concatenate([zeros_act, activated], axis=0), conv_weight)
    decoded = (branch + conv_bias + first_out.astype(jnp.float32)).astype(jnp.bfloat16)
    image_vec = describe(embed(to_patches(decoded), patch_weight), patch_gain, post_gain, proj_weight)
    text_vector = lax.optimization_barrier(jnp.mean(jnp.take(text_table, prompt_ids, axis=0).astype(jnp.float32), axis=0))
    image_embed = jnp.take(image_vec, frame_order, axis=0)
    return (latent_next, decoded, image_embed, rate(image_embed, text_vector))
```

```python
import functools

import jax
import jax.numpy as jnp
from jax import lax
from jax.experimental import pallas as pl
from jax.experimental.pallas import tpu as pltpu
from jax.sharding import PartitionSpec as P

GRID_H = 8
GRID_W = 12
HEADS = 32
HD = 128
LAT_C = 16
CH = 384
TEXT_W = 768


highest = lax.Precision.HIGHEST


MESH = pl.DeviceIdType.MESH


def remote(src, dst, send, recv, device):
    return pltpu.make_async_remote_copy(
        src_ref=src, dst_ref=dst, send_sem=send, recv_sem=recv, device_id={"seq": device}, device_id_type=MESH
    )


def mix_kernel(
    n,
    heads_here,
    q_hbm,
    k_hbm,
    v_hbm,
    latent_ref,
    mod_hbm,
    step_ref,
    time_ref,
    weight_hbm,
    latent_out,
    frames_out,
    k_buf,
    v_buf,
    q_buf,
    att_buf,
    part_buf,
    own_buf,
    mirror_buf,
    cross_buf,
    sum_buf,
    mod_buf,
    weight_buf,
    gain_buf,
    shift_buf,
    halo_buf,
    k_send,
    k_recv,
    v_send,
    v_recv,
    q_send,
    q_recv,
    part_send,
    part_recv,
    cross_send,
    cross_recv,
    halo_send,
    halo_recv,
    local_sem,
):
    me = lax.axis_index("seq")
    half = n // 2
    rows = q_buf.shape[1]
    wide = heads_here * HD
    cols_n = latent_ref.shape[1]
    frames_dev = rows // (GRID_H * GRID_W)
    per_frame = rows // frames_dev
    first_col = pl.multiple_of(me * wide, wide)

    locals_ = [pltpu.make_async_copy(mod_hbm, mod_buf, local_sem.at[0])]
    locals_.append(pltpu.make_async_copy(weight_hbm, weight_buf, local_sem.at[1]))
    own_cp = []
    for h in range(heads_here):
        own_col = pl.ds(pl.multiple_of(me * wide + h * HD, HD), HD)
        own_cp.append(pltpu.make_async_copy(k_hbm.at[:, own_col], k_buf.at[h, me], k_recv.at[h, me]))
        own_cp.append(pltpu.make_async_copy(v_hbm.at[:, own_col], v_buf.at[h, me], v_recv.at[h, me]))
    own_cp.append(pltpu.make_async_copy(q_hbm.at[:, pl.ds(first_col, wide)], q_buf.at[me], q_recv.at[me]))

    barrier = pltpu.get_barrier_semaphore()

    def greet(x, carry):
        pl.semaphore_signal(barrier, inc=1, device_id={"seq": jnp.bitwise_xor(me, x)}, device_id_type=MESH)
        return carry

    lax.fori_loop(1, n, greet, 0)
    pl.semaphore_wait(barrier, n - 1)

    def head_copy(hbm, buf, send, recv, h, peer):
        cols = pl.ds(pl.multiple_of(peer * wide + h * HD, HD), HD)
        return remote(hbm.at[:, cols], buf.at[h, me], send.at[h, peer], recv.at[h, me], peer)

    def query_copy(peer):
        cols = pl.ds(pl.multiple_of(peer * wide, wide), wide)
        return remote(q_hbm.at[:, cols], q_buf.at[me], q_send.at[peer], q_recv.at[me], peer)

    def send_all(make):
        def far(x, carry):
            make(jnp.bitwise_xor(me, x)).start()
            return carry

        lax.fori_loop(half, n, far, 0)
        lax.fori_loop(1, half, far, 0)

    for h in range(heads_here):
        send_all(lambda peer, h=h: head_copy(k_hbm, k_buf, k_send, k_recv, h, peer))
        send_all(lambda peer, h=h: head_copy(v_hbm, v_buf, v_send, v_recv, h, peer))
    send_all(query_copy)
    for cp in locals_ + own_cp:
        cp.start()
    for cp in locals_:
        cp.wait()

    weight_own = weight_buf[pl.ds(first_col, wide), :]
    mod_own = mod_buf[:, 1, pl.ds(first_col, wide)]
    steps = mod_own.shape[0]
    step_ids = lax.broadcasted_iota(jnp.int32, (steps, cols_n), 0)

    def prepare(f, carry):
        hot = (step_ids == time_ref[f]).astype(jnp.float32)
        gain = lax.dot_general(
            mod_own, hot, (((0,), (0,)), ((), ())), precision=highest, preferred_element_type=jnp.float32
        )
        scaled = (1.0 + gain) * weight_own
        high = scaled.astype(jnp.bfloat16)
        low = (scaled - high.astype(jnp.float32)).astype(jnp.bfloat16)
        gain_buf[f] = jnp.concatenate([high, low], axis=1)
        return carry

    lax.fori_loop(0, n * frames_dev, prepare, 0)

    def one_shift(head, carry):
        cols = pl.ds(pl.multiple_of(head * HD, HD), HD)
        shifts = jnp.concatenate(
            [mod_buf[pl.ds(time_ref[me * frames_dev + f], 1), 0, cols] for f in range(frames_dev)] * (8 // frames_dev),
            axis=0,
        )
        return carry + jnp.dot(
            shifts, weight_buf[cols, :], precision=highest, preferred_element_type=jnp.float32
        )

    shift_buf[...] = lax.fori_loop(0, HEADS, one_shift, jnp.zeros(shift_buf.shape, jnp.float32))

    def arrived(buf, recv):
        def body(x, carry):
            pltpu.make_async_copy(buf.at[x], buf.at[x], recv.at[x]).wait()
            return carry

        lax.fori_loop(0, n, body, 0)

    def attend(h, src):
        head_k = k_buf[h].reshape(n * rows, HD)
        head_v = v_buf[h].reshape(n * rows, HD)
        logits = lax.dot_general(
            q_buf[src, :, h * HD : (h + 1) * HD],
            head_k,
            (((1,), (1,)), ((), ())),
            preferred_element_type=jnp.float32,
        )
        row_peak = jnp.max(logits, axis=-1, keepdims=True)
        exponent = jnp.exp2((logits - row_peak) * (HD ** (-0.5) * 1.4426950408889634))
        total = jnp.sum(exponent, axis=-1, keepdims=True)
        mixed = jnp.dot(exponent.astype(jnp.bfloat16), head_v, preferred_element_type=jnp.float32)
        att_buf[src, :, h * HD : (h + 1) * HD] = (mixed / total).astype(jnp.bfloat16)

    def project(x, src):
        rows_a = att_buf[src].astype(jnp.float32)
        squares = jnp.sum(rows_a * rows_a, axis=-1, keepdims=True)
        lane = lax.broadcasted_iota(jnp.int32, (per_frame, 2 * cols_n), 1)
        for f in range(frames_dev):
            span = slice(f * per_frame, (f + 1) * per_frame)
            both = jnp.dot(att_buf[src, span, :], gain_buf[src * frames_dev + f], preferred_element_type=jnp.float32)
            both = both + pltpu.roll(both, cols_n, 1)
            part_buf[x, span, :] = jnp.where(lane < cols_n, both, squares[span])

    for h in range(heads_here):
        arrived(k_buf.at[h], k_recv.at[h])
        arrived(v_buf.at[h], v_recv.at[h])

        def near(x, carry, h=h):
            src = jnp.bitwise_xor(me, x)
            if h == 0:
                pltpu.make_async_copy(q_buf.at[src], q_buf.at[src], q_recv.at[src]).wait()
            attend(h, src)
            if h == heads_here - 1:
                project(x, src)

                @pl.when(x > 0)
                def _():
                    remote(part_buf.at[x], own_buf.at[x], part_send.at[x], part_recv.at[x], src).start()

            return carry

        lax.fori_loop(0, half, near, 0)

    def far(x, carry):
        src = jnp.bitwise_xor(me, x)
        pltpu.make_async_copy(q_buf.at[src], q_buf.at[src], q_recv.at[src]).wait()
        for h in range(heads_here):
            attend(h, src)
        project(x, src)

        @pl.when(x > half)
        def _():
            y = x - half
            to = jnp.bitwise_xor(me, y)
            remote(part_buf.at[x], mirror_buf.at[y], part_send.at[x], part_recv.at[x], to).start()

        return carry

    lax.fori_loop(half, n, far, 0)

    def part_wait(x):
        pltpu.make_async_copy(part_buf.at[x], part_buf.at[x], part_recv.at[x]).wait()

    total = part_buf[half]
    for y in range(1, half):
        part_wait(half + y)
        total = total + mirror_buf[y]
    sum_buf[...] = total
    cross = remote(sum_buf, cross_buf, cross_send, cross_recv, jnp.bitwise_xor(me, half))
    cross.start()
    total = part_buf[0]
    for y in range(1, half):
        part_wait(y)
        total = total + own_buf[y]
    cross.wait()
    total = total + cross_buf[...]
    meansq = total[:, cols_n : cols_n + 1] / (HEADS * HD)
    prediction = total[:, :cols_n] * lax.rsqrt(meansq + 1e-06)
    pieces = []
    for f in range(frames_dev):
        span = slice(f * per_frame, (f + 1) * per_frame)
        moved = step_ref[time_ref[me * frames_dev + f]] * (prediction[span] + shift_buf[f : f + 1, :])
        pieces.append(latent_ref[span, :] + moved)
    latent_new = jnp.concatenate(pieces, axis=0)
    latent_out[...] = latent_new
    halo_buf[2] = jnp.concatenate([latent_new, jnp.zeros_like(latent_new)], axis=1).astype(jnp.bfloat16)

    for back in (1, 2):
        step_to = remote(
            halo_buf.at[2], halo_buf.at[2 - back], halo_send.at[back - 1], halo_recv.at[back - 1], me + back
        )

        @pl.when(me + back < n)
        def _(step_to=step_to):
            step_to.start()

        @pl.when(me < back)
        def _(back=back):
            halo_buf[2 - back] = jnp.zeros(halo_buf.shape[1:], jnp.bfloat16)

    for back in (1, 2):
        step_to = remote(
            halo_buf.at[2], halo_buf.at[2 - back], halo_send.at[back - 1], halo_recv.at[back - 1], me + back
        )

        @pl.when(me >= back)
        def _(step_to=step_to):
            step_to.wait_recv()

        @pl.when(me + back < n)
        def _(step_to=step_to):
            step_to.wait_send()

    frames_out[...] = halo_buf[...]

    def sent(x, carry):
        peer = jnp.bitwise_xor(me, x)
        for h in range(heads_here):
            head_copy(k_hbm, k_buf, k_send, k_recv, h, peer).wait_send()
            head_copy(v_hbm, v_buf, v_send, v_recv, h, peer).wait_send()
        query_copy(peer).wait_send()
        return carry

    lax.fori_loop(1, n, sent, 0)

    def parts_sent(x, carry):
        remote(part_buf.at[x], own_buf.at[0], part_send.at[x], part_recv.at[x], jnp.bitwise_xor(me, 1)).wait_send()
        return carry

    lax.fori_loop(1, half, parts_sent, 0)
    lax.fori_loop(half + 1, n, parts_sent, 0)


def mix(queries, keys, values, latent_in, mod_table, step_size, timestep, head_weight):
    n = lax.axis_size("seq")
    heads_here = HEADS // n
    rows, cols_n = latent_in.shape
    wide = heads_here * HD
    half = n // 2
    frames_all = timestep.shape[0]
    vmem = pltpu.VMEM
    dma = pltpu.SemaphoreType.DMA
    f32, b16 = jnp.float32, jnp.bfloat16
    anywhere = pl.BlockSpec(memory_space=pl.ANY)
    in_vmem = pl.BlockSpec(memory_space=pltpu.VMEM)
    in_smem = pl.BlockSpec(memory_space=pltpu.SMEM)
    return pl.pallas_call(
        functools.partial(mix_kernel, n, heads_here),
        out_shape=(
            jax.ShapeDtypeStruct((rows, cols_n), f32),
            jax.ShapeDtypeStruct((3, rows, 2 * cols_n), b16),
        ),
        in_specs=[anywhere, anywhere, anywhere, in_vmem, anywhere, in_smem, in_smem, anywhere],
        out_specs=(in_vmem, in_vmem),
        scratch_shapes=[
            vmem((heads_here, n, rows, HD), b16),
            vmem((heads_here, n, rows, HD), b16),
            vmem((n, rows, wide), b16),
            vmem((n, rows, wide), b16),
            vmem((n, rows, 2 * cols_n), f32),
            vmem((half, rows, 2 * cols_n), f32),
            vmem((half, rows, 2 * cols_n), f32),
            vmem((rows, 2 * cols_n), f32),
            vmem((rows, 2 * cols_n), f32),
            vmem(mod_table.shape, f32),
            vmem(head_weight.shape, f32),
            vmem((frames_all, wide, 2 * cols_n), b16),
            vmem((8, cols_n), f32),
            vmem((3, rows, 2 * cols_n), b16),
            dma((heads_here, n)),
            dma((heads_here, n)),
            dma((heads_here, n)),
            dma((heads_here, n)),
            dma((n,)),
            dma((n,)),
            dma((n,)),
            dma((n,)),
            dma,
            dma,
            dma((2,)),
            dma((2,)),
            dma((2,)),
        ],
        compiler_params=pltpu.CompilerParams(
            collective_id=0, has_side_effects=True, vmem_limit_bytes=48 << 20
        ),
        name="mix",
    )(queries, keys, values, latent_in, mod_table, step_size, timestep, head_weight)


def to_frames(latent):
    shaped = latent.reshape(-1, GRID_H, GRID_W, 2, 2, LAT_C).transpose(0, 1, 3, 2, 4, 5)
    return shaped.reshape(-1, 2 * GRID_H, 2 * GRID_W, LAT_C)


def causal_conv(padded, weight):
    frames_n = padded.shape[0] - 2
    rows_h = padded.shape[1]
    cols_w = padded.shape[2]
    spaced = jnp.pad(padded, ((0, 0), (1, 1), (1, 1), (0, 0)))
    summed = jnp.zeros((frames_n * rows_h * cols_w, weight.shape[2]), jnp.float32)
    for lag_t in range(3):
        for row_off in range(3):
            for col_off in range(3):
                window = spaced[
                    lag_t : lag_t + frames_n, row_off : row_off + rows_h, col_off : col_off + cols_w
                ]
                window = window.reshape(-1, spaced.shape[3])
                summed = summed + jnp.dot(
                    window,
                    weight[lag_t * 9 + row_off * 3 + col_off],
                    preferred_element_type=jnp.float32,
                )
    return summed.reshape(frames_n, rows_h, cols_w, weight.shape[2])


def activate(first_out, norm_gain):
    first_f = first_out.astype(jnp.float32)
    meansq = jnp.mean(first_f * first_f, axis=-1, keepdims=True)
    return jax.nn.silu(first_f * lax.rsqrt(meansq + 1e-06) * norm_gain).astype(jnp.bfloat16)


def to_patches(decoded):
    shaped = decoded.reshape(-1, GRID_H, 2, GRID_W, 2, CH).transpose(0, 1, 3, 2, 4, 5)
    return shaped.reshape(-1, GRID_H * GRID_W, 4 * CH)


def embed(patches, patch_weight):
    flat_rows = patches.reshape(-1, patches.shape[2])
    product = jnp.dot(flat_rows, patch_weight, preferred_element_type=jnp.float32)
    return product.reshape(patches.shape[0], patches.shape[1], -1).astype(jnp.bfloat16)


def layer_norm(matrix, gain_vec):
    centered = matrix - jnp.mean(matrix, axis=-1, keepdims=True)
    variance = jnp.mean(centered * centered, axis=-1, keepdims=True)
    return centered * lax.rsqrt(variance + 1e-05) * gain_vec


def describe(embedded, patch_gain, post_gain, proj_weight):
    pooled = jnp.mean(layer_norm(embedded.astype(jnp.float32), patch_gain), axis=-2)
    return jnp.dot(layer_norm(pooled, post_gain), proj_weight, precision=highest)


def rate(image_vec, text_vector):
    inner = jnp.sum(image_vec * text_vector[None, :], axis=-1)
    image_rms = jnp.sqrt(jnp.mean(image_vec * image_vec, axis=-1) + 1e-06)
    text_rms = jnp.sqrt(jnp.mean(text_vector * text_vector) + 1e-06)
    return 100.0 * inner / (TEXT_W * image_rms * text_rms)


def local(
    queries,
    keys,
    values,
    latent_in,
    mod_table,
    step_size,
    timestep,
    head_weight,
    conv_in_weight,
    conv_in_bias,
    norm_gain,
    conv_weight,
    conv_bias,
    patch_weight,
    patch_gain,
    post_gain,
    proj_weight,
    text_table,
    prompt_ids,
    frame_order,
):
    devices = lax.axis_size("seq")
    frames_dev = queries.shape[0] // (GRID_H * GRID_W)
    first_frame = lax.axis_index("seq") * frames_dev

    def exchange(matrix):
        return lax.all_to_all(matrix, "seq", split_axis=0, concat_axis=0, tiled=True)

    latent_next, halo = mix(
        queries, keys, values, latent_in, mod_table, step_size, timestep, head_weight
    )
    stacked = to_frames(halo[:, :, : latent_in.shape[1]])
    frames = stacked[-frames_dev:]
    first_wide = (causal_conv(stacked, conv_in_weight) + conv_in_bias).astype(jnp.bfloat16)
    first_out = first_wide[2:]
    frame_ids = (
        lax.axis_index("seq") * frames.shape[0]
        - 2
        + jnp.arange(frames.shape[0] + 2, dtype=jnp.int32)
    )
    widened = jnp.where(
        (frame_ids >= 0)[:, None, None, None],
        activate(first_wide, norm_gain),
        jnp.zeros((), jnp.bfloat16),
    )
    branch = causal_conv(widened, conv_weight)
    decoded = (branch + conv_bias + first_out.astype(jnp.float32)).astype(jnp.bfloat16)
    own_text = jnp.mean(jnp.take(text_table, prompt_ids, axis=0).astype(jnp.float32), axis=0)
    patches = to_patches(decoded)
    image_src = describe(embed(patches, patch_weight), patch_gain, post_gain, proj_weight)
    bundle = jnp.concatenate([image_src.reshape(-1), own_text])
    gathered = exchange(jnp.broadcast_to(bundle[None, :], (devices, bundle.shape[0])))
    images = gathered[:, : image_src.size].reshape(-1, image_src.shape[1])
    text_vector = gathered[:, image_src.size :].reshape(-1)
    order_own = lax.dynamic_slice_in_dim(frame_order, first_frame, frames_dev, 0)
    image_vec = jnp.take(images, order_own, axis=0, mode="clip")
    return (latent_next, decoded, image_vec, rate(image_vec, text_vector))


def solution(mesh):
    in_specs = (
        P(("grp", "seq"), None),
        P(("grp", "seq"), None),
        P(("grp", "seq"), None),
        P(("grp", "seq"), None),
        P(),
        P(),
        P("grp"),
        P(),
        P(),
        P(),
        P(),
        P(),
        P(),
        P(),
        P(),
        P(),
        P(),
        P(None, "seq"),
        P("grp"),
        P("grp"),
    )
    out_specs = (
        P(("grp", "seq"), None),
        P(("grp", "seq"), None, None, None),
        P(("grp", "seq"), None),
        P(("grp", "seq")),
    )
    return jax.shard_map(local, mesh=mesh, in_specs=in_specs, out_specs=out_specs, check_vma=False)
```

```python
import functools

import jax
import jax.numpy as jnp
from jax import lax
from jax.experimental import pallas as pl
from jax.experimental.pallas import tpu as pltpu
from jax.sharding import PartitionSpec as P

GRID_H = 8
GRID_W = 12
HEADS = 32
HD = 128
LAT_C = 16
CH = 384
TEXT_W = 768


highest = lax.Precision.HIGHEST


MESH = pl.DeviceIdType.MESH


def remote(src, dst, send, recv, device):
    return pltpu.make_async_remote_copy(
        src_ref=src, dst_ref=dst, send_sem=send, recv_sem=recv, device_id={"seq": device}, device_id_type=MESH
    )


def mix_kernel(
    n,
    heads_here,
    q_hbm,
    k_hbm,
    v_hbm,
    latent_ref,
    mod_hbm,
    step_ref,
    time_ref,
    weight_hbm,
    table_hbm,
    prompt_ref,
    latent_out,
    frames_out,
    text_out,
    k_buf,
    v_buf,
    q_buf,
    att_buf,
    part_buf,
    own_buf,
    mirror_buf,
    cross_buf,
    sum_buf,
    mod_buf,
    weight_buf,
    gain_buf,
    shift_buf,
    sum_rows,
    logit_even,
    logit_odd,
    peak_buf,
    halo_buf,
    table_buf,
    text_buf,
    text_all,
    k_send,
    k_recv,
    v_send,
    v_recv,
    q_send,
    q_recv,
    part_send,
    part_recv,
    cross_send,
    cross_recv,
    halo_send,
    halo_recv,
    text_send,
    text_recv,
    local_sem,
):
    me = lax.axis_index("seq")
    half = n // 2
    rows = q_buf.shape[1]
    wide = heads_here * HD
    cols_n = latent_ref.shape[0]
    frames_dev = rows // (GRID_H * GRID_W)
    per_frame = rows // frames_dev
    first_col = pl.multiple_of(me * wide, wide)

    locals_ = [pltpu.make_async_copy(mod_hbm, mod_buf, local_sem.at[0])]
    locals_.append(pltpu.make_async_copy(weight_hbm, weight_buf, local_sem.at[1]))
    own_cp = []
    for h in range(heads_here):
        own_col = pl.ds(pl.multiple_of(me * wide + h * HD, HD), HD)
        own_cp.append(pltpu.make_async_copy(k_hbm.at[:, own_col], k_buf.at[h, me], k_recv.at[h, me]))
        own_cp.append(pltpu.make_async_copy(v_hbm.at[:, own_col], v_buf.at[h, me, :, pl.ds(0, HD)], v_recv.at[h, me]))
    own_cp.append(pltpu.make_async_copy(q_hbm.at[:, pl.ds(first_col, wide)], q_buf.at[me], q_recv.at[me]))

    barrier = pltpu.get_barrier_semaphore()

    def greet(x, carry):
        pl.semaphore_signal(barrier, inc=1, device_id={"seq": jnp.bitwise_xor(me, x)}, device_id_type=MESH)
        return carry

    lax.fori_loop(1, n, greet, 0)
    pl.semaphore_wait(barrier, n - 1)

    def head_copy(hbm, buf, send, recv, h, peer):
        cols = pl.ds(pl.multiple_of(peer * wide + h * HD, HD), HD)
        return remote(
            hbm.at[:, cols], buf.at[h, me, :, pl.ds(0, HD)], send.at[h, peer], recv.at[h, me], peer
        )

    def query_copy(peer):
        cols = pl.ds(pl.multiple_of(peer * wide, wide), wide)
        return remote(q_hbm.at[:, cols], q_buf.at[me], q_send.at[peer], q_recv.at[me], peer)

    def send_some(make, first, last):
        def body(x, carry):
            make(jnp.bitwise_xor(me, x)).start()
            return carry

        lax.fori_loop(first, last, body, 0)

    def send_heads(h, first, last):
        send_some(lambda peer: head_copy(k_hbm, k_buf, k_send, k_recv, h, peer), first, last)
        send_some(lambda peer: head_copy(v_hbm, v_buf, v_send, v_recv, h, peer), first, last)

    beside_cut = jnp.logical_and(me >= half // 2, me < half + half // 2)
    send_heads(0, 1, half)
    send_some(query_copy, 1, half)
    for h in range(1, heads_here):
        send_heads(h, 1, half)
    for h in range(heads_here):
        send_heads(h, half, n)

    @pl.when(jnp.logical_not(beside_cut))
    def _():
        send_some(query_copy, half, n)

    for cp in locals_ + own_cp:
        cp.start()
    for cp in locals_:
        cp.wait()

    lanes = table_buf.shape[2]

    def table_part(i, carry):
        part = table_hbm.at[:, pl.ds(pl.multiple_of(i * lanes, lanes), lanes)]
        pltpu.make_async_copy(part, table_buf.at[i], local_sem.at[2]).start()
        return carry

    lax.fori_loop(0, table_buf.shape[0], table_part, 0)

    weight_own = weight_buf[:, pl.ds(first_col, wide)]

    def prepare(f, carry):
        gain = mod_buf[pl.ds(time_ref[f], 1), 1, pl.ds(first_col, wide)]
        scaled = (1.0 + gain) * weight_own
        high = scaled.astype(jnp.bfloat16)
        low = (scaled - high.astype(jnp.float32)).astype(jnp.bfloat16)
        gain_buf[f] = jnp.concatenate([high, low], axis=0)
        return carry

    lax.fori_loop(0, n * frames_dev, prepare, 0)

    def fill_ones(src, carry):
        for h in range(heads_here):
            v_buf[h, src, :, HD:] = jnp.ones((rows, HD), jnp.bfloat16)
        return carry

    lax.fori_loop(0, n, fill_ones, 0)

    def one_shift(head, carry):
        cols = pl.ds(pl.multiple_of(head * HD, HD), HD)
        shifts = jnp.concatenate(
            [mod_buf[pl.ds(time_ref[me * frames_dev + f], 1), 0, cols] for f in range(frames_dev)] * (8 // frames_dev),
            axis=0,
        )
        return carry + lax.dot_general(
            shifts,
            weight_buf[:, cols],
            (((1,), (1,)), ((), ())),
            precision=highest,
            preferred_element_type=jnp.float32,
        )

    shift_buf[...] = lax.fori_loop(0, HEADS, one_shift, jnp.zeros(shift_buf.shape, jnp.float32))

    words = prompt_ref.shape[0]
    width = table_buf.shape[1]
    lane_ids = lax.broadcasted_iota(jnp.int32, (width, lanes), 1)
    pltpu.make_async_copy(table_buf, table_buf, local_sem.at[2]).wait()

    def one_word(w, carry):
        word = prompt_ref[w]
        block = table_buf[word // lanes]
        return carry + jnp.where(lane_ids == word % lanes, block.astype(jnp.float32), 0.0)

    picked = lax.fori_loop(0, words, one_word, jnp.zeros((width, lanes), jnp.float32))
    text_buf[...] = jnp.broadcast_to(jnp.sum(picked, axis=-1, keepdims=True) / words, (width, lanes))

    def text_copy(peer):
        return remote(text_buf, text_all.at[me], text_send.at[peer], text_recv.at[me], peer)

    send_some(text_copy, 1, n)
    text_all[me] = text_buf[...]

    def arrived(buf, recv):
        def body(x, carry):
            block = buf.at[x, :, pl.ds(0, HD)]
            pltpu.make_async_copy(block, block, recv.at[x]).wait()
            return carry

        lax.fori_loop(0, n, body, 0)

    logit_bufs = (logit_even, logit_odd)

    def score(slot, h, src):
        logits = lax.dot_general(
            q_buf[src, :, h * HD : (h + 1) * HD],
            k_buf[h].reshape(n * rows, HD),
            (((1,), (1,)), ((), ())),
            preferred_element_type=jnp.float32,
        )
        logit_bufs[slot][...] = logits
        peak_buf[slot] = jnp.broadcast_to(jnp.max(logits, axis=-1, keepdims=True), (rows, HD))

    def weigh(slot, h, src):
        row_peak = peak_buf[slot, :, 0:1]
        exponent = jnp.exp2((logit_bufs[slot][...] - row_peak) * (HD ** (-0.5) * 1.4426950408889634))
        mixed = jnp.dot(
            exponent.astype(jnp.bfloat16),
            v_buf[h].reshape(n * rows, 2 * HD),
            preferred_element_type=jnp.float32,
        )
        att_buf[src, :, h * HD : (h + 1) * HD] = (mixed[:, :HD] / mixed[:, HD:]).astype(jnp.bfloat16)

    def in_turn(first, heads, waits, done):
        count = half * len(heads)
        unroll = 2 if len(heads) == 1 else len(heads)

        def place(t):
            x = first + lax.rem(t // len(heads), half)
            return x, jnp.bitwise_xor(me, x)

        def begin(t, p, guard):
            x, src = place(t)
            h = heads[p % len(heads)]
            if waits and p % len(heads) == 0:

                @pl.when(guard)
                def _():
                    pltpu.make_async_copy(q_buf.at[src], q_buf.at[src], q_recv.at[src]).wait()

            score(p % 2, h, src)

        begin(0, 0, me >= 0)

        def body(i, carry):
            for p in range(unroll):
                t = i * unroll + p
                begin(t + 1, p + 1, t + 1 < count)
                x, src = place(t)
                weigh(p % 2, heads[p % len(heads)], src)
                if p % len(heads) == len(heads) - 1:
                    done(x, src)
            return carry

        lax.fori_loop(0, count // unroll, body, 0)

    lane = lax.broadcasted_iota(jnp.int32, (per_frame, frames_dev * cols_n), 1)
    ones = jnp.ones((8, wide), jnp.bfloat16)
    turned = (((1,), (1,)), ((), ()))

    def project(x, src):
        packed = None
        for f in range(frames_dev):
            rows_a = att_buf[src, f * per_frame : (f + 1) * per_frame, :]
            both = lax.dot_general(
                rows_a, gain_buf[src * frames_dev + f], turned, preferred_element_type=jnp.float32
            )
            both = both + pltpu.roll(both, cols_n, 1)
            packed = both if packed is None else jnp.where(lane < f * cols_n, packed, both)
            rows_f = rows_a.astype(jnp.float32)
            squares = lax.dot_general(
                ones, (rows_f * rows_f).astype(jnp.bfloat16), turned, preferred_element_type=jnp.float32
            )
            sum_rows[x % 2, f * 8 : (f + 1) * 8, :per_frame] = squares
        part_buf[x, :per_frame, :] = packed.astype(jnp.bfloat16)
        part_buf[x, per_frame:, :] = sum_rows[x % 2].astype(jnp.bfloat16)

    for h in range(heads_here):
        arrived(k_buf.at[h], k_recv.at[h])
        arrived(v_buf.at[h], v_recv.at[h])
        if h == heads_here - 1:

            @pl.when(beside_cut)
            def _():
                send_some(query_copy, half, n)

        def near_done(x, src, h=h):
            if h == heads_here - 1:
                project(x, src)

                @pl.when(x > 0)
                def _():
                    remote(part_buf.at[x], own_buf.at[x], part_send.at[x], part_recv.at[x], src).start()

        in_turn(0, [h], h == 0, near_done)

    def far_done(x, src):
        project(x, src)

        @pl.when(x > half)
        def _():
            y = x - half
            to = jnp.bitwise_xor(me, y)
            remote(part_buf.at[x], mirror_buf.at[y], part_send.at[x], part_recv.at[x], to).start()

    in_turn(half, list(range(heads_here)), True, far_done)

    def part_wait(x):
        pltpu.make_async_copy(part_buf.at[x], part_buf.at[x], part_recv.at[x]).wait()

    total = part_buf[half].astype(jnp.float32)
    for y in range(1, half):
        part_wait(half + y)
        total = total + mirror_buf[y].astype(jnp.float32)
    sum_buf[...] = total.astype(jnp.bfloat16)
    cross = remote(sum_buf, cross_buf, cross_send, cross_recv, jnp.bitwise_xor(me, half))
    cross.start()
    total = part_buf[0].astype(jnp.float32)
    for y in range(1, half):
        part_wait(y)
        total = total + own_buf[y].astype(jnp.float32)
    cross.wait()
    total = total + cross_buf[...].astype(jnp.float32)
    diagonal = lax.broadcasted_iota(jnp.int32, (per_frame, per_frame), 0) == lax.broadcasted_iota(
        jnp.int32, (per_frame, per_frame), 1
    )
    latent_rows = jnp.transpose(latent_ref[...])
    pieces = []
    for f in range(frames_dev):
        row_sums = total[per_frame + f * 8 : per_frame + f * 8 + 1, :per_frame]
        meansq = jnp.sum(jnp.where(diagonal, row_sums, 0.0), axis=-1, keepdims=True) / (HEADS * HD)
        prediction = total[:per_frame, f * cols_n : (f + 1) * cols_n] * lax.rsqrt(meansq + 1e-06)
        moved = step_ref[time_ref[me * frames_dev + f]] * (prediction + shift_buf[f : f + 1, :])
        pieces.append(latent_rows[f * per_frame : (f + 1) * per_frame, :] + moved)
    latent_new = jnp.concatenate(pieces, axis=0)
    latent_wide = jnp.concatenate([latent_new, latent_new], axis=1)
    halo_buf[2] = latent_wide.astype(jnp.bfloat16)

    for back in (1, 2):
        step_to = remote(
            halo_buf.at[2], halo_buf.at[2 - back], halo_send.at[back - 1], halo_recv.at[back - 1], me + back
        )

        @pl.when(me + back < n)
        def _(step_to=step_to):
            step_to.start()

        @pl.when(me < back)
        def _(back=back):
            halo_buf[2 - back] = jnp.zeros(halo_buf.shape[1:], jnp.bfloat16)

    latent_out[...] = jnp.transpose(latent_new)

    def text_came(x, carry):
        src = jnp.bitwise_xor(me, x)
        pltpu.make_async_copy(text_all.at[src], text_all.at[src], text_recv.at[src]).wait()
        return carry

    lax.fori_loop(1, n, text_came, 0)
    text_out[...] = text_all[:, :, 0:8]

    for back in (1, 2):
        step_to = remote(
            halo_buf.at[2], halo_buf.at[2 - back], halo_send.at[back - 1], halo_recv.at[back - 1], me + back
        )

        @pl.when(me >= back)
        def _(step_to=step_to):
            step_to.wait_recv()

        @pl.when(me + back < n)
        def _(step_to=step_to):
            step_to.wait_send()

    frames_out[...] = halo_buf[...]

    def sent(x, carry):
        peer = jnp.bitwise_xor(me, x)
        for h in range(heads_here):
            head_copy(k_hbm, k_buf, k_send, k_recv, h, peer).wait_send()
            head_copy(v_hbm, v_buf, v_send, v_recv, h, peer).wait_send()
        query_copy(peer).wait_send()
        text_copy(peer).wait_send()
        return carry

    lax.fori_loop(1, n, sent, 0)

    def parts_sent(x, carry):
        remote(part_buf.at[x], own_buf.at[0], part_send.at[x], part_recv.at[x], jnp.bitwise_xor(me, 1)).wait_send()
        return carry

    lax.fori_loop(1, half, parts_sent, 0)
    lax.fori_loop(half + 1, n, parts_sent, 0)


def mix(queries, keys, values, latent_in, mod_table, step_size, timestep, head_weight, text_table, prompt_ids):
    n = lax.axis_size("seq")
    heads_here = HEADS // n
    rows, cols_n = latent_in.shape
    width = text_table.shape[1]
    wide = heads_here * HD
    half = n // 2
    frames_all = timestep.shape[0]
    frames_dev = frames_all // n
    part = (rows // frames_dev + 8 * frames_dev, frames_dev * cols_n)
    vmem = pltpu.VMEM
    dma = pltpu.SemaphoreType.DMA
    f32, b16 = jnp.float32, jnp.bfloat16
    anywhere = pl.BlockSpec(memory_space=pltpu.HBM)
    in_vmem = pl.BlockSpec(memory_space=pltpu.VMEM)
    in_smem = pl.BlockSpec(memory_space=pltpu.SMEM)
    return pl.pallas_call(
        functools.partial(mix_kernel, n, heads_here),
        out_shape=(
            jax.ShapeDtypeStruct((cols_n, rows), f32),
            jax.ShapeDtypeStruct((3, rows, 2 * cols_n), b16),
            jax.ShapeDtypeStruct((n, width, 8), f32),
        ),
        in_specs=[anywhere] * 3 + [in_vmem, anywhere, in_smem, in_smem, anywhere, anywhere, in_smem],
        out_specs=(in_vmem, in_vmem, in_vmem),
        scratch_shapes=[
            vmem((heads_here, n, rows, HD), b16),
            vmem((heads_here, n, rows, 2 * HD), b16),
            vmem((n, rows, wide), b16),
            vmem((n, rows, wide), b16),
            vmem((n,) + part, b16),
            vmem((half,) + part, b16),
            vmem((half,) + part, b16),
            vmem(part, b16),
            vmem(part, b16),
            vmem(mod_table.shape, f32),
            vmem((cols_n, HEADS * HD), f32),
            vmem((frames_all, 2 * cols_n, wide), b16),
            vmem((8, cols_n), f32),
            vmem((2, 8 * frames_dev, frames_dev * cols_n), f32),
            vmem((rows, n * rows), f32),
            vmem((rows, n * rows), f32),
            vmem((2, rows, HD), f32),
            vmem((3, rows, 2 * cols_n), b16),
            vmem((text_table.shape[0] // 128, width, 128), b16),
            vmem((width, 128), f32),
            vmem((n, width, 128), f32),
            dma((heads_here, n)),
            dma((heads_here, n)),
            dma((heads_here, n)),
            dma((heads_here, n)),
            dma((n,)),
            dma((n,)),
            dma((n,)),
            dma((n,)),
            dma,
            dma,
            dma((2,)),
            dma((2,)),
            dma((n,)),
            dma((n,)),
            dma((3,)),
        ],
        compiler_params=pltpu.CompilerParams(
            collective_id=0, has_side_effects=True, vmem_limit_bytes=67043328
        ),
        name="mix",
    )(
        queries,
        keys,
        values,
        latent_in.T,
        mod_table,
        step_size,
        timestep,
        head_weight.T,
        text_table.T,
        prompt_ids,
    )


TAPS = {(a, q): ((a + q - 1) % 2, (a + q - 1) // 2) for a in range(2) for q in range(3)}


def decode_kernel(
    n,
    halo_ref,
    text_ref,
    first_hbm,
    first_bias_ref,
    gain_ref,
    conv_hbm,
    conv_bias_ref,
    patch_hbm,
    patch_gain_ref,
    post_gain_ref,
    proj_hbm,
    order_ref,
    decoded_out,
    image_out,
    score_out,
    first_w,
    first_taps,
    wide_in,
    first_buf,
    window,
    conv_w,
    acc,
    pixels,
    patches,
    patch_w,
    proj_w,
    proj_pair,
    image_buf,
    image_all,
    image_send,
    image_recv,
    local_sem,
):
    me = lax.axis_index("seq")
    per_frame = GRID_H * GRID_W
    frames_dev = image_buf.shape[0]
    held = frames_dev + 2
    cols_n = halo_ref.shape[2] // 2
    lat_c = cols_n // 4
    ch = first_buf.shape[2]
    f32, b16 = jnp.float32, jnp.bfloat16

    copies = [
        pltpu.make_async_copy(src, dst, local_sem.at[i])
        for i, (src, dst) in enumerate(
            ((first_hbm, first_w), (conv_hbm, conv_w), (patch_hbm, patch_w), (proj_hbm, proj_w))
        )
    ]
    for cp in copies:
        cp.start()

    barrier = pltpu.get_barrier_semaphore()

    def greet(x, carry):
        pl.semaphore_signal(barrier, inc=1, device_id={"seq": jnp.bitwise_xor(me, x)}, device_id_type=MESH)
        return carry

    lax.fori_loop(1, n, greet, 0)

    latents = halo_ref[...].reshape(-1, 2 * cols_n).astype(f32)
    total_rows = latents.shape[0]
    token = lax.rem(lax.broadcasted_iota(jnp.int32, latents.shape, 0), per_frame)
    row_id, col_id = token // GRID_W, lax.rem(token, GRID_W)
    lane = lax.broadcasted_iota(jnp.int32, latents.shape, 1)
    for di in (-1, 0, 1):
        moved = []
        for dj in (-1, 0, 1):
            step = GRID_W * di + dj
            value = latents if step == 0 else pltpu.roll(latents, (-step) % total_rows, 0)
            keep = (row_id + di >= 0) & (row_id + di < GRID_H) & (col_id + dj >= 0) & (col_id + dj < GRID_W)
            moved.append(value if step == 0 else jnp.where(keep, value, 0.0))
        for b in range(2):
            pair = jnp.where(lane < cols_n, moved[b], moved[b + 1]).astype(b16)
            for a in range(2):
                u = di + 1 - a
                if 0 <= u < 2:
                    wide_in[2 * a + b, :, u * 2 * cols_n : (u + 1) * 2 * cols_n] = pair

    first_taps[...] = jnp.zeros_like(first_taps)
    copies[0].wait()
    for a in range(2):
        for b in range(2):
            for lag in range(3):
                for q in range(3):
                    for r in range(3):
                        (sub_a, di), (sub_b, dj) = TAPS[a, q], TAPS[b, r]
                        u, v = di + 1 - a, dj + 1 - b
                        at = ((u * 2 + v) * 4 + sub_a * 2 + sub_b) * lat_c
                        first_taps[2 * a + b, lag, at : at + lat_c, :] = first_w[lag * 9 + q * 3 + r]

    first_bias = first_bias_ref[...][None, :]
    for ab in range(4):
        summed = None
        for lag in range(3):
            term = jnp.dot(
                wide_in[ab, lag * per_frame : (lag + held) * per_frame, :],
                first_taps[ab, lag],
                preferred_element_type=f32,
            )
            summed = term if summed is None else summed + term
        first_buf[ab] = (summed + first_bias).astype(b16)

    gain = gain_ref[...][None, :]
    token = lax.broadcasted_iota(jnp.int32, (per_frame, ch), 0)
    row_id, col_id = token // GRID_W, lax.rem(token, GRID_W)

    def one_frame(f, carry):
        live = (me * frames_dev - 2 + f) >= 0
        span = pl.ds(pl.multiple_of(f * per_frame, per_frame), per_frame)
        for sub_a in range(2):
            for sub_b in range(2):
                first_f = first_buf[2 * sub_a + sub_b, span, :].astype(f32)
                meansq = jnp.mean(first_f * first_f, axis=-1, keepdims=True)
                value = jax.nn.silu(first_f * lax.rsqrt(meansq + 1e-06) * gain)
                value = jnp.where(live, value, 0.0)
                for di in (0, -1 if sub_a else 1):
                    for dj in (0, -1 if sub_b else 1):
                        step = GRID_W * di + dj
                        shifted = value
                        if step:
                            shifted = pltpu.roll(value, (-step) % per_frame, 0)
                            keep = (
                                (row_id + di >= 0)
                                & (row_id + di < GRID_H)
                                & (col_id + dj >= 0)
                                & (col_id + dj < GRID_W)
                            )
                            shifted = jnp.where(keep, shifted, 0.0)
                        shifted = shifted.astype(b16)
                        for (a, q), source_a in TAPS.items():
                            for (b, r), source_b in TAPS.items():
                                if source_a == (sub_a, di) and source_b == (sub_b, dj):
                                    tap = q * 3 + r
                                    window[f, 2 * a + b, :, tap * ch : (tap + 1) * ch] = shifted
        return carry

    lax.fori_loop(0, held, one_frame, 0)

    copies[1].wait()
    taps_n = 9
    conv_bias = conv_bias_ref[...][None, :]
    for f in range(frames_dev):
        for ab in range(4):
            own = first_buf[ab, (f + 2) * per_frame : (f + 3) * per_frame, :].astype(f32)
            acc[(f * 4 + ab) * per_frame : (f * 4 + ab + 1) * per_frame, :] = own + conv_bias

    def one_lag(lag, carry):
        rows = window[pl.ds(lag, frames_dev)].reshape(frames_dev * 4 * per_frame, taps_n * ch)
        weight = conv_w[pl.ds(lag * taps_n, taps_n)].reshape(taps_n * ch, ch)
        acc[...] += jnp.dot(rows, weight, preferred_element_type=f32)
        return carry

    lax.fori_loop(0, 3, one_lag, 0)

    for f in range(frames_dev):
        for a in range(2):
            for b in range(2):
                base = (f * 4 + 2 * a + b) * per_frame
                for i in range(GRID_H):
                    for c in range(pixels.shape[0]):
                        pixels[c, f, 2 * i + a, pl.ds(b, GRID_W, stride=2), :] = acc[
                            pl.ds(base + i * GRID_W, GRID_W), c * 128 : (c + 1) * 128
                        ]
                patches[f * per_frame : (f + 1) * per_frame, (2 * a + b) * ch : (2 * a + b + 1) * ch] = acc[
                    base : base + per_frame, :
                ].astype(b16)
    for c in range(pixels.shape[0]):
        decoded_out[:, :, :, c * 128 : (c + 1) * 128] = pixels[c].astype(b16)

    copies[2].wait()
    embedded = jnp.dot(patches[...], patch_w[...], preferred_element_type=f32).astype(b16).astype(f32)
    centered = embedded - jnp.mean(embedded, axis=-1, keepdims=True)
    variance = jnp.mean(centered * centered, axis=-1, keepdims=True)
    normed = centered * lax.rsqrt(variance + 1e-05)
    pooled = jnp.concatenate(
        [
            jnp.mean(normed[f * per_frame : (f + 1) * per_frame], axis=0, keepdims=True)
            for f in range(frames_dev)
        ],
        axis=0,
    ) * patch_gain_ref[...][None, :]
    centered = pooled - jnp.mean(pooled, axis=-1, keepdims=True)
    variance = jnp.mean(centered * centered, axis=-1, keepdims=True)
    pooled = centered * lax.rsqrt(variance + 1e-05) * post_gain_ref[...][None, :]

    copies[3].wait()
    pooled = jnp.concatenate([pooled] * (8 // frames_dev), axis=0)
    image = jnp.dot(pooled, proj_w[...], precision=highest, preferred_element_type=f32)
    for f in range(frames_dev):
        image_buf[f] = image[f : f + 1, :]

    pl.semaphore_wait(barrier, n - 1)

    def image_copy(peer):
        return remote(
            image_buf,
            image_all.at[pl.ds(me * frames_dev, frames_dev)],
            image_send.at[peer],
            image_recv.at[me],
            peer,
        )

    def spread(x, carry):
        image_copy(jnp.bitwise_xor(me, x)).start()
        return carry

    lax.fori_loop(1, n, spread, 0)
    image_all[pl.ds(me * frames_dev, frames_dev)] = image_buf[...]

    def came(x, carry):
        src = jnp.bitwise_xor(me, x)
        block = image_all.at[pl.ds(src * frames_dev, frames_dev)]
        pltpu.make_async_copy(block, block, image_recv.at[src]).wait()
        return carry

    lax.fori_loop(1, n, came, 0)
    text = text_ref[...]
    text_rms = jnp.sqrt(jnp.mean(text * text, keepdims=True) + 1e-06)
    for f in range(frames_dev):
        vector = image_all[order_ref[me * frames_dev + f]]
        image_out[f : f + 1, :] = vector
        inner = jnp.sum(vector * text, keepdims=True)
        image_rms = jnp.sqrt(jnp.mean(vector * vector, keepdims=True) + 1e-06)
        score_out[f] = (100.0 * inner / (TEXT_W * image_rms * text_rms))[0, 0]

    def gone(x, carry):
        image_copy(jnp.bitwise_xor(me, x)).wait_send()
        return carry

    lax.fori_loop(1, n, gone, 0)


def decode(
    halo,
    text_parts,
    conv_in_weight,
    conv_in_bias,
    norm_gain,
    conv_weight,
    conv_bias,
    patch_weight,
    patch_gain,
    post_gain,
    proj_weight,
    frame_order,
):
    n = lax.axis_size("seq")
    frames_dev = frame_order.shape[0] // n
    held = frames_dev + 2
    per_frame = GRID_H * GRID_W
    ch = conv_weight.shape[2]
    cols_n = halo.shape[2] // 2
    text_w = proj_weight.shape[1]
    vmem = pltpu.VMEM
    dma = pltpu.SemaphoreType.DMA
    f32, b16 = jnp.float32, jnp.bfloat16
    far = pl.BlockSpec(memory_space=pltpu.HBM)
    near = pl.BlockSpec(memory_space=pltpu.VMEM)
    scalars = pl.BlockSpec(memory_space=pltpu.SMEM)
    return pl.pallas_call(
        functools.partial(decode_kernel, n),
        out_shape=(
            jax.ShapeDtypeStruct((frames_dev, 2 * GRID_H, 2 * GRID_W, ch), b16),
            jax.ShapeDtypeStruct((frames_dev, text_w), f32),
            jax.ShapeDtypeStruct((frames_dev,), f32),
        ),
        in_specs=[near, near, far, near, near, far, near, far, near, near, far, scalars],
        out_specs=(near, near, scalars),
        scratch_shapes=[
            vmem(conv_in_weight.shape, b16),
            vmem((4, 3, 4 * cols_n, ch), b16),
            vmem((4, (held + 2) * per_frame, 4 * cols_n), b16),
            vmem((4, held * per_frame, ch), b16),
            vmem((held, 4, per_frame, 9 * ch), b16),
            vmem(conv_weight.shape, b16),
            vmem((frames_dev * 4 * per_frame, ch), f32),
            vmem((ch // 128, frames_dev, 2 * GRID_H, 2 * GRID_W, 128), f32),
            vmem((frames_dev * per_frame, 4 * ch), b16),
            vmem(patch_weight.shape, b16),
            vmem(proj_weight.shape, f32),
            vmem((8, 128), b16),
            vmem((frames_dev, 1, text_w), f32),
            vmem((n * frames_dev, 1, text_w), f32),
            dma((n,)),
            dma((n,)),
            dma((4,)),
        ],
        compiler_params=pltpu.CompilerParams(
            collective_id=1, has_side_effects=True, vmem_limit_bytes=67043328
        ),
        name="decode",
    )(
        halo,
        text_parts[:, :, 0].reshape(1, text_w),
        conv_in_weight,
        conv_in_bias,
        norm_gain,
        conv_weight,
        conv_bias,
        patch_weight,
        patch_gain,
        post_gain,
        proj_weight,
        frame_order,
    )


def local(
    queries,
    keys,
    values,
    latent_in,
    mod_table,
    step_size,
    timestep,
    head_weight,
    conv_in_weight,
    conv_in_bias,
    norm_gain,
    conv_weight,
    conv_bias,
    patch_weight,
    patch_gain,
    post_gain,
    proj_weight,
    text_table,
    prompt_ids,
    frame_order,
):
    latent_turned, halo, text_parts = mix(
        queries,
        keys,
        values,
        latent_in,
        mod_table,
        step_size,
        timestep,
        head_weight,
        text_table,
        prompt_ids,
    )
    decoded, image_vec, scores = decode(
        halo,
        text_parts,
        conv_in_weight,
        conv_in_bias,
        norm_gain,
        conv_weight,
        conv_bias,
        patch_weight,
        patch_gain,
        post_gain,
        proj_weight,
        frame_order,
    )
    return (latent_turned.T, decoded, image_vec, scores)


def solution(mesh):
    in_specs = (
        P(("grp", "seq"), None),
        P(("grp", "seq"), None),
        P(("grp", "seq"), None),
        P(("grp", "seq"), None),
        P(),
        P(),
        P("grp"),
        P(),
        P(),
        P(),
        P(),
        P(),
        P(),
        P(),
        P(),
        P(),
        P(),
        P(None, "seq"),
        P("grp"),
        P("grp"),
    )
    out_specs = (
        P(("grp", "seq"), None),
        P(("grp", "seq"), None, None, None),
        P(("grp", "seq"), None),
        P(("grp", "seq")),
    )
    return jax.shard_map(local, mesh=mesh, in_specs=in_specs, out_specs=out_specs, check_vma=False)
```

```python
import functools

import jax
import jax.numpy as jnp
from jax import lax
from jax.experimental import pallas as pl
from jax.experimental.pallas import tpu as pltpu
from jax.sharding import PartitionSpec as P

GRID_H = 8
GRID_W = 12
HEADS = 32
HD = 128
LAT_C = 16
CH = 384
TEXT_W = 768


highest = lax.Precision.HIGHEST


MESH = pl.DeviceIdType.MESH


def remote(src, dst, send, recv, device):
    return pltpu.make_async_remote_copy(
        src_ref=src, dst_ref=dst, send_sem=send, recv_sem=recv, device_id={"seq": device}, device_id_type=MESH
    )


def mix_kernel(
    n,
    heads_here,
    q_hbm,
    k_hbm,
    v_hbm,
    latent_ref,
    mod_hbm,
    step_ref,
    time_ref,
    weight_hbm,
    table_hbm,
    prompt_ref,
    early,
    idle,
    latent_out,
    text_out,
    k_buf,
    v_buf,
    q_buf,
    att_buf,
    part_buf,
    own_buf,
    mirror_buf,
    cross_buf,
    sum_buf,
    mod_buf,
    weight_buf,
    gain_buf,
    shift_buf,
    sum_rows,
    logit_even,
    logit_odd,
    peak_buf,
    halo_buf,
    table_buf,
    text_buf,
    text_all,
    k_send,
    k_recv,
    v_send,
    v_recv,
    q_send,
    q_recv,
    part_send,
    part_recv,
    cross_send,
    cross_recv,
    halo_send,
    halo_recv,
    text_send,
    text_recv,
    local_sem,
):
    me = lax.axis_index("seq")
    half = n // 2
    rows = q_buf.shape[1]
    wide = heads_here * HD
    cols_n = latent_ref.shape[0]
    frames_dev = rows // (GRID_H * GRID_W)
    per_frame = rows // frames_dev
    first_col = pl.multiple_of(me * wide, wide)

    locals_ = [pltpu.make_async_copy(mod_hbm, mod_buf, local_sem.at[0])]
    locals_.append(pltpu.make_async_copy(weight_hbm, weight_buf, local_sem.at[1]))
    own_cp = []
    for h in range(heads_here):
        own_col = pl.ds(pl.multiple_of(me * wide + h * HD, HD), HD)
        own_cp.append(pltpu.make_async_copy(k_hbm.at[:, own_col], k_buf.at[h, me], k_recv.at[h, me]))
        own_cp.append(pltpu.make_async_copy(v_hbm.at[:, own_col], v_buf.at[h, me, :, pl.ds(0, HD)], v_recv.at[h, me]))
    own_cp.append(pltpu.make_async_copy(q_hbm.at[:, pl.ds(first_col, wide)], q_buf.at[me], q_recv.at[me]))

    barrier = pltpu.get_barrier_semaphore()

    def greet(x, carry):
        pl.semaphore_signal(barrier, inc=1, device_id={"seq": jnp.bitwise_xor(me, x)}, device_id_type=MESH)
        return carry

    lax.fori_loop(1, n, greet, 0)
    pl.semaphore_wait(barrier, n - 1)

    def head_copy(hbm, buf, send, recv, h, peer):
        cols = pl.ds(pl.multiple_of(peer * wide + h * HD, HD), HD)
        return remote(
            hbm.at[:, cols], buf.at[h, me, :, pl.ds(0, HD)], send.at[h, peer], recv.at[h, me], peer
        )

    def query_copy(peer):
        cols = pl.ds(pl.multiple_of(peer * wide, wide), wide)
        return remote(q_hbm.at[:, cols], q_buf.at[me], q_send.at[peer], q_recv.at[me], peer)

    def send_some(make, first, last):
        def body(x, carry):
            make(jnp.bitwise_xor(me, x)).start()
            return carry

        lax.fori_loop(first, last, body, 0)

    def send_heads(h, first, last):
        send_some(lambda peer: head_copy(k_hbm, k_buf, k_send, k_recv, h, peer), first, last)
        send_some(lambda peer: head_copy(v_hbm, v_buf, v_send, v_recv, h, peer), first, last)


    send_heads(0, 1, n)
    send_some(query_copy, 1, half)
    for h in range(1, heads_here):
        send_heads(h, 1, n)
    send_some(query_copy, half, n)
    for cp in locals_ + own_cp:
        cp.start()
    early()
    for cp in locals_:
        cp.wait()

    lanes = table_buf.shape[2]

    def table_part(i, carry):
        part = table_hbm.at[:, pl.ds(pl.multiple_of(i * lanes, lanes), lanes)]
        pltpu.make_async_copy(part, table_buf.at[i], local_sem.at[2]).start()
        return carry

    lax.fori_loop(0, table_buf.shape[0], table_part, 0)

    weight_own = weight_buf[:, pl.ds(first_col, wide)]

    def prepare(f, carry):
        gain = mod_buf[pl.ds(time_ref[f], 1), 1, pl.ds(first_col, wide)]
        scaled = (1.0 + gain) * weight_own
        high = scaled.astype(jnp.bfloat16)
        low = (scaled - high.astype(jnp.float32)).astype(jnp.bfloat16)
        gain_buf[f] = jnp.concatenate([high, low], axis=0)
        return carry

    lax.fori_loop(0, n * frames_dev, prepare, 0)

    def fill_ones(src, carry):
        for h in range(heads_here):
            v_buf[h, src, :, HD:] = jnp.ones((rows, HD), jnp.bfloat16)
        return carry

    lax.fori_loop(0, n, fill_ones, 0)

    def one_shift(head, carry):
        cols = pl.ds(pl.multiple_of(head * HD, HD), HD)
        shifts = jnp.concatenate(
            [mod_buf[pl.ds(time_ref[me * frames_dev + f], 1), 0, cols] for f in range(frames_dev)] * (8 // frames_dev),
            axis=0,
        )
        return carry + lax.dot_general(
            shifts,
            weight_buf[:, cols],
            (((1,), (1,)), ((), ())),
            precision=highest,
            preferred_element_type=jnp.float32,
        )

    shift_buf[...] = lax.fori_loop(0, HEADS, one_shift, jnp.zeros(shift_buf.shape, jnp.float32))

    words = prompt_ref.shape[0]
    width = table_buf.shape[1]
    lane_ids = lax.broadcasted_iota(jnp.int32, (width, lanes), 1)
    pltpu.make_async_copy(table_buf, table_buf, local_sem.at[2]).wait()

    def one_word(w, carry):
        word = prompt_ref[w]
        block = table_buf[word // lanes]
        return carry + jnp.where(lane_ids == word % lanes, block.astype(jnp.float32), 0.0)

    picked = lax.fori_loop(0, words, one_word, jnp.zeros((width, lanes), jnp.float32))
    own_text = jnp.sum(picked, axis=-1, keepdims=True) / words
    place = (width, n * width)
    own_place = lax.broadcasted_iota(jnp.int32, place, 1) - me * width == lax.broadcasted_iota(
        jnp.int32, place, 0
    )
    text_buf[...] = jnp.sum(jnp.where(own_place, own_text, 0.0), axis=0, keepdims=True)

    def text_copy(peer):
        return remote(text_buf, text_all.at[me], text_send.at[peer], text_recv.at[me], peer)

    send_some(text_copy, 1, n)
    text_all[me] = text_buf[...]
    idle()

    def arrived(buf, recv):
        def body(x, carry):
            block = buf.at[x, :, pl.ds(0, HD)]
            pltpu.make_async_copy(block, block, recv.at[x]).wait()
            return carry

        lax.fori_loop(0, n, body, 0)

    logit_bufs = (logit_even, logit_odd)

    def score(slot, h, src):
        logits = lax.dot_general(
            q_buf[src, :, h * HD : (h + 1) * HD],
            k_buf[h].reshape(n * rows, HD),
            (((1,), (1,)), ((), ())),
            preferred_element_type=jnp.float32,
        )
        logit_bufs[slot][...] = logits
        peak_buf[slot] = jnp.broadcast_to(jnp.max(logits, axis=-1, keepdims=True), (rows, HD))

    def weigh(slot, h, src):
        row_peak = peak_buf[slot, :, 0:1]
        exponent = jnp.exp2((logit_bufs[slot][...] - row_peak) * (HD ** (-0.5) * 1.4426950408889634))
        mixed = jnp.dot(
            exponent.astype(jnp.bfloat16),
            v_buf[h].reshape(n * rows, 2 * HD),
            preferred_element_type=jnp.float32,
        )
        att_buf[src, :, h * HD : (h + 1) * HD] = (mixed[:, :HD] / mixed[:, HD:]).astype(jnp.bfloat16)

    def in_turn(first, heads, waits, done):
        count = half * len(heads)
        unroll = 2 if len(heads) == 1 else len(heads)

        def place(t):
            x = first + lax.rem(t // len(heads), half)
            return x, jnp.bitwise_xor(me, x)

        def begin(t, p, guard):
            x, src = place(t)
            h = heads[p % len(heads)]
            if waits and p % len(heads) == 0:

                @pl.when(guard)
                def _():
                    pltpu.make_async_copy(q_buf.at[src], q_buf.at[src], q_recv.at[src]).wait()

            score(p % 2, h, src)

        begin(0, 0, me >= 0)

        def body(i, carry):
            for p in range(unroll):
                t = i * unroll + p
                begin(t + 1, p + 1, t + 1 < count)
                x, src = place(t)
                weigh(p % 2, heads[p % len(heads)], src)
                if p % len(heads) == len(heads) - 1:
                    done(x, src)
            return carry

        lax.fori_loop(0, count // unroll, body, 0)

    lane = lax.broadcasted_iota(jnp.int32, (per_frame, frames_dev * cols_n), 1)
    ones = jnp.ones((8, wide), jnp.bfloat16)
    turned = (((1,), (1,)), ((), ()))

    def project(x, src):
        packed = None
        for f in range(frames_dev):
            rows_a = att_buf[src, f * per_frame : (f + 1) * per_frame, :]
            both = lax.dot_general(
                rows_a, gain_buf[src * frames_dev + f], turned, preferred_element_type=jnp.float32
            )
            both = both + pltpu.roll(both, cols_n, 1)
            packed = both if packed is None else jnp.where(lane < f * cols_n, packed, both)
            rows_f = rows_a.astype(jnp.float32)
            squares = lax.dot_general(
                ones, (rows_f * rows_f).astype(jnp.bfloat16), turned, preferred_element_type=jnp.float32
            )
            sum_rows[x % 2, f * 8 : (f + 1) * 8, :per_frame] = squares
        part_buf[x, :per_frame, :] = packed.astype(jnp.bfloat16)
        part_buf[x, per_frame:, :] = sum_rows[x % 2].astype(jnp.bfloat16)

    for h in range(heads_here):
        arrived(k_buf.at[h], k_recv.at[h])
        arrived(v_buf.at[h], v_recv.at[h])
        def near_done(x, src, h=h):
            if h == heads_here - 1:
                project(x, src)

                @pl.when(x > 0)
                def _():
                    remote(part_buf.at[x], own_buf.at[x], part_send.at[x], part_recv.at[x], src).start()

        in_turn(0, [h], h == 0, near_done)

    def far_done(x, src):
        project(x, src)

        @pl.when(x > half)
        def _():
            y = x - half
            to = jnp.bitwise_xor(me, y)
            remote(part_buf.at[x], mirror_buf.at[y], part_send.at[x], part_recv.at[x], to).start()

    in_turn(half, list(range(heads_here)), True, far_done)

    def part_wait(x):
        pltpu.make_async_copy(part_buf.at[x], part_buf.at[x], part_recv.at[x]).wait()

    total = part_buf[half].astype(jnp.float32)
    for y in range(1, half):
        part_wait(half + y)
        total = total + mirror_buf[y].astype(jnp.float32)
    sum_buf[...] = total.astype(jnp.bfloat16)
    cross = remote(sum_buf, cross_buf, cross_send, cross_recv, jnp.bitwise_xor(me, half))
    cross.start()
    total = part_buf[0].astype(jnp.float32)
    for y in range(1, half):
        part_wait(y)
        total = total + own_buf[y].astype(jnp.float32)
    cross.wait()
    total = total + cross_buf[...].astype(jnp.float32)
    diagonal = lax.broadcasted_iota(jnp.int32, (per_frame, per_frame), 0) == lax.broadcasted_iota(
        jnp.int32, (per_frame, per_frame), 1
    )
    latent_rows = jnp.transpose(latent_ref[...])
    pieces = []
    for f in range(frames_dev):
        row_sums = total[per_frame + f * 8 : per_frame + f * 8 + 1, :per_frame]
        meansq = jnp.sum(jnp.where(diagonal, row_sums, 0.0), axis=-1, keepdims=True) / (HEADS * HD)
        prediction = total[:per_frame, f * cols_n : (f + 1) * cols_n] * lax.rsqrt(meansq + 1e-06)
        moved = step_ref[time_ref[me * frames_dev + f]] * (prediction + shift_buf[f : f + 1, :])
        pieces.append(latent_rows[f * per_frame : (f + 1) * per_frame, :] + moved)
    latent_new = jnp.concatenate(pieces, axis=0)
    latent_wide = jnp.concatenate([latent_new, latent_new], axis=1)
    halo_buf[2] = latent_wide.astype(jnp.bfloat16)

    for back in (1, 2):
        step_to = remote(
            halo_buf.at[2], halo_buf.at[2 - back], halo_send.at[back - 1], halo_recv.at[back - 1], me + back
        )

        @pl.when(me + back < n)
        def _(step_to=step_to):
            step_to.start()

        @pl.when(me < back)
        def _(back=back):
            halo_buf[2 - back] = jnp.zeros(halo_buf.shape[1:], jnp.bfloat16)

    latent_out[...] = jnp.transpose(latent_new)

    def text_came(x, carry):
        src = jnp.bitwise_xor(me, x)
        pltpu.make_async_copy(text_all.at[src], text_all.at[src], text_recv.at[src]).wait()
        return carry

    lax.fori_loop(1, n, text_came, 0)
    text_out[...] = functools.reduce(jnp.add, [text_all[x] for x in range(n)])

    for back in (1, 2):
        step_to = remote(
            halo_buf.at[2], halo_buf.at[2 - back], halo_send.at[back - 1], halo_recv.at[back - 1], me + back
        )

        @pl.when(me >= back)
        def _(step_to=step_to):
            step_to.wait_recv()

        @pl.when(me + back < n)
        def _(step_to=step_to):
            step_to.wait_send()


    def finish():
        def sent(x, carry):
            peer = jnp.bitwise_xor(me, x)
            for h in range(heads_here):
                head_copy(k_hbm, k_buf, k_send, k_recv, h, peer).wait_send()
                head_copy(v_hbm, v_buf, v_send, v_recv, h, peer).wait_send()
            query_copy(peer).wait_send()
            text_copy(peer).wait_send()
            return carry

        lax.fori_loop(1, n, sent, 0)

        def parts_sent(x, carry):
            remote(part_buf.at[x], own_buf.at[0], part_send.at[x], part_recv.at[x], jnp.bitwise_xor(me, 1)).wait_send()
            return carry

        lax.fori_loop(1, half, parts_sent, 0)
        lax.fori_loop(half + 1, n, parts_sent, 0)

    return finish


TAPS = {(a, q): ((a + q - 1) % 2, (a + q - 1) // 2) for a in range(2) for q in range(3)}


def decode_kernel(
    n,
    halo_ref,
    text_ref,
    first_hbm,
    first_bias_ref,
    gain_ref,
    conv_hbm,
    conv_bias_ref,
    patch_hbm,
    patch_gain_ref,
    post_gain_ref,
    proj_hbm,
    order_ref,
    decoded_out,
    image_out,
    score_out,
    first_w,
    first_taps,
    wide_in,
    first_buf,
    window,
    conv_w,
    acc,
    pixels,
    patches,
    patch_w,
    proj_w,
    decoded_buf,
    image_buf,
    image_all,
    image_send,
    image_recv,
    local_sem,
):
    me = lax.axis_index("seq")
    per_frame = GRID_H * GRID_W
    frames_dev = image_buf.shape[0]
    held = frames_dev + 2
    cols_n = halo_ref.shape[2] // 2
    lat_c = cols_n // 4
    ch = first_buf.shape[2]
    f32, b16 = jnp.float32, jnp.bfloat16

    out_copy = pltpu.make_async_copy(decoded_buf, decoded_out, local_sem.at[4])
    copies = [
        pltpu.make_async_copy(src, dst, local_sem.at[i])
        for i, (src, dst) in enumerate(
            ((first_hbm, first_w), (conv_hbm, conv_w), (patch_hbm, patch_w), (proj_hbm, proj_w))
        )
    ]
    def early():
        for cp in copies:
            cp.start()

    def idle():
        first_taps[...] = jnp.zeros_like(first_taps)
        copies[0].wait()
        for a in range(2):
            for b in range(2):
                for lag in range(3):
                    for q in range(3):
                        for r in range(3):
                            (sub_a, di), (sub_b, dj) = TAPS[a, q], TAPS[b, r]
                            u, v = di + 1 - a, dj + 1 - b
                            at = ((u * 2 + v) * 4 + sub_a * 2 + sub_b) * lat_c
                            first_taps[2 * a + b, lag, at : at + lat_c, :] = first_w[lag * 9 + q * 3 + r]
        for cp in copies[1:]:
            cp.wait()

    yield early, idle

    latents = halo_ref[...].reshape(-1, 2 * cols_n).astype(f32)
    total_rows = latents.shape[0]
    token = lax.rem(lax.broadcasted_iota(jnp.int32, latents.shape, 0), per_frame)
    row_id, col_id = token // GRID_W, lax.rem(token, GRID_W)
    lane = lax.broadcasted_iota(jnp.int32, latents.shape, 1)
    for di in (-1, 0, 1):
        moved = []
        for dj in (-1, 0, 1):
            step = GRID_W * di + dj
            value = latents if step == 0 else pltpu.roll(latents, (-step) % total_rows, 0)
            keep = (row_id + di >= 0) & (row_id + di < GRID_H) & (col_id + dj >= 0) & (col_id + dj < GRID_W)
            moved.append(value if step == 0 else jnp.where(keep, value, 0.0))
        for b in range(2):
            pair = jnp.where(lane < cols_n, moved[b], moved[b + 1]).astype(b16)
            for a in range(2):
                u = di + 1 - a
                if 0 <= u < 2:
                    wide_in[2 * a + b, :, u * 2 * cols_n : (u + 1) * 2 * cols_n] = pair

    first_bias = first_bias_ref[...][None, :]
    for ab in range(4):
        summed = None
        for lag in range(3):
            term = jnp.dot(
                wide_in[ab, lag * per_frame : (lag + held) * per_frame, :],
                first_taps[ab, lag],
                preferred_element_type=f32,
            )
            summed = term if summed is None else summed + term
        first_buf[ab] = (summed + first_bias).astype(b16)

    gain = gain_ref[...][None, :]
    token = lax.broadcasted_iota(jnp.int32, (per_frame, ch), 0)
    row_id, col_id = token // GRID_W, lax.rem(token, GRID_W)

    def one_frame(f, carry):
        live = (me * frames_dev - 2 + f) >= 0
        span = pl.ds(pl.multiple_of(f * per_frame, per_frame), per_frame)
        for sub_a in range(2):
            for sub_b in range(2):
                first_f = first_buf[2 * sub_a + sub_b, span, :].astype(f32)
                meansq = jnp.mean(first_f * first_f, axis=-1, keepdims=True)
                value = jax.nn.silu(first_f * lax.rsqrt(meansq + 1e-06) * gain)
                value = jnp.where(live, value, 0.0)
                for di in (0, -1 if sub_a else 1):
                    for dj in (0, -1 if sub_b else 1):
                        step = GRID_W * di + dj
                        shifted = value
                        if step:
                            shifted = pltpu.roll(value, (-step) % per_frame, 0)
                            keep = (
                                (row_id + di >= 0)
                                & (row_id + di < GRID_H)
                                & (col_id + dj >= 0)
                                & (col_id + dj < GRID_W)
                            )
                            shifted = jnp.where(keep, shifted, 0.0)
                        shifted = shifted.astype(b16)
                        for (a, q), source_a in TAPS.items():
                            for (b, r), source_b in TAPS.items():
                                if source_a == (sub_a, di) and source_b == (sub_b, dj):
                                    tap = q * 3 + r
                                    window[f, 2 * a + b, :, tap * ch : (tap + 1) * ch] = shifted
        return carry

    lax.fori_loop(0, held, one_frame, 0)

    taps_n = 9
    conv_bias = conv_bias_ref[...][None, :]
    for f in range(frames_dev):
        for ab in range(4):
            own = first_buf[ab, (f + 2) * per_frame : (f + 3) * per_frame, :].astype(f32)
            acc[(f * 4 + ab) * per_frame : (f * 4 + ab + 1) * per_frame, :] = own + conv_bias

    def one_lag(lag, carry):
        rows = window[pl.ds(lag, frames_dev)].reshape(frames_dev * 4 * per_frame, taps_n * ch)
        weight = conv_w[pl.ds(lag * taps_n, taps_n)].reshape(taps_n * ch, ch)
        acc[...] += jnp.dot(rows, weight, preferred_element_type=f32)
        return carry

    lax.fori_loop(0, 3, one_lag, 0)

    for f in range(frames_dev):
        for a in range(2):
            for b in range(2):
                base = (f * 4 + 2 * a + b) * per_frame
                for i in range(GRID_H):
                    for c in range(pixels.shape[0]):
                        pixels[c, f, 2 * i + a, pl.ds(b, GRID_W, stride=2), :] = acc[
                            pl.ds(base + i * GRID_W, GRID_W), c * 128 : (c + 1) * 128
                        ]
                patches[f * per_frame : (f + 1) * per_frame, (2 * a + b) * ch : (2 * a + b + 1) * ch] = acc[
                    base : base + per_frame, :
                ].astype(b16)
    for c in range(pixels.shape[0]):
        decoded_buf[:, :, :, c * 128 : (c + 1) * 128] = pixels[c].astype(b16)
    out_copy.start()

    embedded = jnp.dot(patches[...], patch_w[...], preferred_element_type=f32).astype(b16).astype(f32)
    centered = embedded - jnp.mean(embedded, axis=-1, keepdims=True)
    variance = jnp.mean(centered * centered, axis=-1, keepdims=True)
    normed = centered * lax.rsqrt(variance + 1e-05)
    pooled = jnp.concatenate(
        [
            jnp.mean(normed[f * per_frame : (f + 1) * per_frame], axis=0, keepdims=True)
            for f in range(frames_dev)
        ],
        axis=0,
    ) * patch_gain_ref[...][None, :]
    centered = pooled - jnp.mean(pooled, axis=-1, keepdims=True)
    variance = jnp.mean(centered * centered, axis=-1, keepdims=True)
    pooled = centered * lax.rsqrt(variance + 1e-05) * post_gain_ref[...][None, :]

    pooled = jnp.concatenate([pooled] * (8 // frames_dev), axis=0)
    image = jnp.dot(pooled, proj_w[...], precision=highest, preferred_element_type=f32)
    for f in range(frames_dev):
        image_buf[f] = image[f : f + 1, :]

    def image_copy(peer):
        return remote(
            image_buf,
            image_all.at[pl.ds(me * frames_dev, frames_dev)],
            image_send.at[peer],
            image_recv.at[me],
            peer,
        )

    def spread(x, carry):
        image_copy(jnp.bitwise_xor(me, x)).start()
        return carry

    lax.fori_loop(1, n, spread, 0)
    image_all[pl.ds(me * frames_dev, frames_dev)] = image_buf[...]

    def came(x, carry):
        src = jnp.bitwise_xor(me, x)
        block = image_all.at[pl.ds(src * frames_dev, frames_dev)]
        pltpu.make_async_copy(block, block, image_recv.at[src]).wait()
        return carry

    lax.fori_loop(1, n, came, 0)
    text = text_ref[...]
    text_rms = jnp.sqrt(jnp.mean(text * text, keepdims=True) + 1e-06)
    for f in range(frames_dev):
        vector = image_all[order_ref[me * frames_dev + f]]
        image_out[f : f + 1, :] = vector
        inner = jnp.sum(vector * text, keepdims=True)
        image_rms = jnp.sqrt(jnp.mean(vector * vector, keepdims=True) + 1e-06)
        score_out[f] = (100.0 * inner / (TEXT_W * image_rms * text_rms))[0, 0]

    def gone(x, carry):
        image_copy(jnp.bitwise_xor(me, x)).wait_send()
        return carry

    lax.fori_loop(1, n, gone, 0)
    out_copy.wait()
    yield


MIX_IN, DECODE_IN, MIX_SCRATCH, HALO_AT = 10, 10, 36, 17


def whole_kernel(n, heads_here, *refs):
    mix_in, refs = refs[:MIX_IN], refs[MIX_IN:]
    decode_in, refs = refs[:DECODE_IN], refs[DECODE_IN:]
    (latent_out, decoded_out, image_out, score_out), refs = refs[:4], refs[4:]
    (text_full, *mix_scratch), decode_scratch = refs[: MIX_SCRATCH + 1], refs[MIX_SCRATCH + 1 :]
    halo_buf = mix_scratch[HALO_AT]
    steps = decode_kernel(n, halo_buf, text_full, *decode_in, decoded_out, image_out, score_out, *decode_scratch)
    early, idle = next(steps)
    finish = mix_kernel(n, heads_here, *mix_in, early, idle, latent_out, text_full, *mix_scratch)
    next(steps)
    finish()


def everything(
    queries,
    keys,
    values,
    latent_in,
    mod_table,
    step_size,
    timestep,
    head_weight,
    text_table,
    prompt_ids,
    conv_in_weight,
    conv_in_bias,
    norm_gain,
    conv_weight,
    conv_bias,
    patch_weight,
    patch_gain,
    post_gain,
    proj_weight,
    frame_order,
):
    n = lax.axis_size("seq")
    heads_here = HEADS // n
    rows, cols_n = latent_in.shape
    width = text_table.shape[1]
    wide = heads_here * HD
    half = n // 2
    frames_all = timestep.shape[0]
    frames_dev = frames_all // n
    per_frame = rows // frames_dev
    part = (per_frame + 8 * frames_dev, frames_dev * cols_n)
    held = frames_dev + 2
    ch = conv_weight.shape[2]
    text_w = proj_weight.shape[1]
    pixel_shape = (frames_dev, 2 * GRID_H, 2 * GRID_W, ch)
    vmem = pltpu.VMEM
    dma = pltpu.SemaphoreType.DMA
    f32, b16 = jnp.float32, jnp.bfloat16
    far = pl.BlockSpec(memory_space=pltpu.HBM)
    near = pl.BlockSpec(memory_space=pltpu.VMEM)
    scalars = pl.BlockSpec(memory_space=pltpu.SMEM)
    mix_scratch = [
        vmem((heads_here, n, rows, HD), b16),
        vmem((heads_here, n, rows, 2 * HD), b16),
        vmem((n, rows, wide), b16),
        vmem((n, rows, wide), b16),
        vmem((n,) + part, b16),
        vmem((half,) + part, b16),
        vmem((half,) + part, b16),
        vmem(part, b16),
        vmem(part, b16),
        vmem(mod_table.shape, f32),
        vmem((cols_n, HEADS * HD), f32),
        vmem((frames_all, 2 * cols_n, wide), b16),
        vmem((8, cols_n), f32),
        vmem((2, 8 * frames_dev, frames_dev * cols_n), f32),
        vmem((rows, n * rows), f32),
        vmem((rows, n * rows), f32),
        vmem((2, rows, HD), f32),
        vmem((3, rows, 2 * cols_n), b16),
        vmem((text_table.shape[0] // 128, width, 128), b16),
        vmem((1, n * width), f32),
        vmem((n, 1, n * width), f32),
        dma((heads_here, n)),
        dma((heads_here, n)),
        dma((heads_here, n)),
        dma((heads_here, n)),
        dma((n,)),
        dma((n,)),
        dma((n,)),
        dma((n,)),
        dma,
        dma,
        dma((2,)),
        dma((2,)),
        dma((n,)),
        dma((n,)),
        dma((3,)),
    ]
    decode_scratch = [
        vmem(conv_in_weight.shape, b16),
        vmem((4, 3, 4 * cols_n, ch), b16),
        vmem((4, (held + 2) * per_frame, 4 * cols_n), b16),
        vmem((4, held * per_frame, ch), b16),
        vmem((held, 4, per_frame, 9 * ch), b16),
        vmem(conv_weight.shape, b16),
        vmem((frames_dev * 4 * per_frame, ch), f32),
        vmem((ch // 128, frames_dev, 2 * GRID_H, 2 * GRID_W, 128), f32),
        vmem((frames_dev * per_frame, 4 * ch), b16),
        vmem(patch_weight.shape, b16),
        vmem(proj_weight.shape, f32),
        vmem(pixel_shape, b16),
        vmem((frames_dev, 1, text_w), f32),
        vmem((n * frames_dev, 1, text_w), f32),
        dma((n,)),
        dma((n,)),
        dma((5,)),
    ]
    assert len(mix_scratch) == MIX_SCRATCH
    results = pl.pallas_call(
        functools.partial(whole_kernel, n, heads_here),
        out_shape=(
            jax.ShapeDtypeStruct((cols_n, rows), f32),
            jax.ShapeDtypeStruct(pixel_shape, b16),
            jax.ShapeDtypeStruct((frames_dev, text_w), f32),
            jax.ShapeDtypeStruct((frames_dev,), f32),
        ),
        in_specs=[far] * 3
        + [near, far, scalars, scalars, far, far, scalars]
        + [far, near, near, far, near, far, near, near, far, scalars],
        out_specs=(near, far, near, scalars),
        scratch_shapes=[vmem((1, text_w), f32)] + mix_scratch + decode_scratch,
        compiler_params=pltpu.CompilerParams(
            collective_id=0, has_side_effects=True, vmem_limit_bytes=67043328
        ),
        name="everything",
    )(
        queries,
        keys,
        values,
        latent_in.T,
        mod_table,
        step_size,
        timestep,
        head_weight.T,
        text_table.T,
        prompt_ids,
        conv_in_weight,
        conv_in_bias,
        norm_gain,
        conv_weight,
        conv_bias,
        patch_weight,
        patch_gain,
        post_gain,
        proj_weight,
        frame_order,
    )
    return deliver(*results)


def deliver_kernel(*refs):
    count = len(refs) // 2
    for source, target in zip(refs[: count - 1], refs[count:-1]):
        target[...] = source[...]
    for f in range(refs[-1].shape[0]):
        refs[-1][f] = refs[count - 1][f]


def deliver(*arrays):
    near = pl.BlockSpec(memory_space=pltpu.VMEM)
    specs = [near] * (len(arrays) - 1) + [pl.BlockSpec(memory_space=pltpu.SMEM)]
    return pl.pallas_call(
        deliver_kernel,
        out_shape=[jax.ShapeDtypeStruct(a.shape, a.dtype) for a in arrays],
        in_specs=specs,
        out_specs=specs,
        name="deliver",
    )(*arrays)


def local(
    queries,
    keys,
    values,
    latent_in,
    mod_table,
    step_size,
    timestep,
    head_weight,
    conv_in_weight,
    conv_in_bias,
    norm_gain,
    conv_weight,
    conv_bias,
    patch_weight,
    patch_gain,
    post_gain,
    proj_weight,
    text_table,
    prompt_ids,
    frame_order,
):
    latent_turned, decoded, image_vec, scores = everything(
        queries,
        keys,
        values,
        latent_in,
        mod_table,
        step_size,
        timestep,
        head_weight,
        text_table,
        prompt_ids,
        conv_in_weight,
        conv_in_bias,
        norm_gain,
        conv_weight,
        conv_bias,
        patch_weight,
        patch_gain,
        post_gain,
        proj_weight,
        frame_order,
    )
    return (latent_turned.T, decoded, image_vec, scores)


def solution(mesh):
    in_specs = (
        P(("grp", "seq"), None),
        P(("grp", "seq"), None),
        P(("grp", "seq"), None),
        P(("grp", "seq"), None),
        P(),
        P(),
        P("grp"),
        P(),
        P(),
        P(),
        P(),
        P(),
        P(),
        P(),
        P(),
        P(),
        P(),
        P(None, "seq"),
        P("grp"),
        P("grp"),
    )
    out_specs = (
        P(("grp", "seq"), None),
        P(("grp", "seq"), None, None, None),
        P(("grp", "seq"), None),
        P(("grp", "seq")),
    )
    return jax.shard_map(local, mesh=mesh, in_specs=in_specs, out_specs=out_specs, check_vma=False)
```

```python
import functools

import jax
import jax.numpy as jnp
from jax import lax
from jax.experimental import pallas as pl
from jax.experimental.pallas import tpu as pltpu
from jax.sharding import PartitionSpec as P

GRID_H = 8
GRID_W = 12
HEADS = 32
HD = 128
LAT_C = 16
CH = 384
TEXT_W = 768


highest = lax.Precision.HIGHEST


MESH = pl.DeviceIdType.MESH
AHEAD = 4


def remote(src, dst, send, recv, device):
    return pltpu.make_async_remote_copy(
        src_ref=src, dst_ref=dst, send_sem=send, recv_sem=recv, device_id={"seq": device}, device_id_type=MESH
    )


def mix_kernel(
    n,
    heads_here,
    q_hbm,
    k_hbm,
    v_hbm,
    latent_ref,
    mod_hbm,
    step_ref,
    time_ref,
    weight_hbm,
    table_hbm,
    prompt_ref,
    early,
    idle,
    latent_out,
    text_out,
    k_buf,
    v_buf,
    q_buf,
    att_buf,
    part_buf,
    own_buf,
    mirror_buf,
    cross_buf,
    sum_buf,
    mod_buf,
    weight_buf,
    gain_buf,
    shift_buf,
    sum_rows,
    logit_even,
    logit_odd,
    peak_buf,
    halo_buf,
    table_buf,
    text_buf,
    text_all,
    k_send,
    k_recv,
    v_send,
    v_recv,
    q_send,
    q_recv,
    part_send,
    part_recv,
    cross_send,
    cross_recv,
    halo_send,
    halo_recv,
    text_send,
    text_recv,
    local_sem,
):
    me = lax.axis_index("seq")
    half = n // 2
    rows = q_buf.shape[1]
    wide = heads_here * HD
    cols_n = latent_ref.shape[0]
    frames_dev = rows // (GRID_H * GRID_W)
    per_frame = rows // frames_dev
    first_col = pl.multiple_of(me * wide, wide)

    locals_ = [pltpu.make_async_copy(mod_hbm, mod_buf, local_sem.at[0])]
    locals_.append(pltpu.make_async_copy(weight_hbm, weight_buf, local_sem.at[1]))
    own_cp = []
    for h in range(heads_here):
        own_col = pl.ds(pl.multiple_of(me * wide + h * HD, HD), HD)
        own_cp.append(pltpu.make_async_copy(k_hbm.at[:, own_col], k_buf.at[h, me], k_recv.at[h, me]))
        own_cp.append(pltpu.make_async_copy(v_hbm.at[:, own_col], v_buf.at[h, me, :, pl.ds(0, HD)], v_recv.at[h, me]))
    own_cp.append(pltpu.make_async_copy(q_hbm.at[:, pl.ds(first_col, wide)], q_buf.at[me], q_recv.at[me]))

    barrier = pltpu.get_barrier_semaphore()

    def greet(x, carry):
        pl.semaphore_signal(barrier, inc=1, device_id={"seq": jnp.bitwise_xor(me, x)}, device_id_type=MESH)
        return carry

    lax.fori_loop(1, n, greet, 0)
    pl.semaphore_wait(barrier, n - 1)

    def head_copy(hbm, buf, send, recv, h, peer):
        cols = pl.ds(pl.multiple_of(peer * wide + h * HD, HD), HD)
        return remote(
            hbm.at[:, cols], buf.at[h, me, :, pl.ds(0, HD)], send.at[h, peer], recv.at[h, me], peer
        )

    def query_copy(peer):
        cols = pl.ds(pl.multiple_of(peer * wide, wide), wide)
        return remote(q_hbm.at[:, cols], q_buf.at[me], q_send.at[peer], q_recv.at[me], peer)

    def send_some(make, first, last):
        def body(x, carry):
            make(jnp.bitwise_xor(me, x)).start()
            return carry

        lax.fori_loop(first, last, body, 0)

    phases = []
    for h in range(heads_here):
        phases.append(lambda peer, h=h: head_copy(k_hbm, k_buf, k_send, k_recv, h, peer))
        phases.append(lambda peer, h=h: head_copy(v_hbm, v_buf, v_send, v_recv, h, peer))

    def follow(phase):
        def body(x, carry):
            peer = jnp.bitwise_xor(me, x)
            phases[phase](peer).wait_send()
            if phase + 1 < len(phases):
                phases[phase + 1](peer).start()
            else:

                @pl.when(x < half + AHEAD)
                def _():
                    query_copy(peer).start()

            return carry

        lax.fori_loop(half, n, body, 0)

    def follow_query(x):
        query_copy(jnp.bitwise_xor(me, x)).wait_send()

        @pl.when(x + AHEAD < n)
        def _():
            query_copy(jnp.bitwise_xor(me, x + AHEAD)).start()

    send_some(phases[0], 1, n)
    send_some(phases[1], 1, half)
    send_some(query_copy, 1, half)
    for cp in locals_ + own_cp:
        cp.start()
    early()
    for cp in locals_:
        cp.wait()

    follow(0)
    lanes = table_buf.shape[2]

    def table_part(i, carry):
        part = table_hbm.at[:, pl.ds(pl.multiple_of(i * lanes, lanes), lanes)]
        pltpu.make_async_copy(part, table_buf.at[i], local_sem.at[2]).start()
        return carry

    lax.fori_loop(0, table_buf.shape[0], table_part, 0)

    weight_own = weight_buf[:, pl.ds(first_col, wide)]

    def prepare(f, carry):
        gain = mod_buf[pl.ds(time_ref[f], 1), 1, pl.ds(first_col, wide)]
        scaled = (1.0 + gain) * weight_own
        high = scaled.astype(jnp.bfloat16)
        low = (scaled - high.astype(jnp.float32)).astype(jnp.bfloat16)
        gain_buf[f] = jnp.concatenate([high, low], axis=0)
        return carry

    lax.fori_loop(0, n * frames_dev, prepare, 0)

    def fill_ones(src, carry):
        for h in range(heads_here):
            v_buf[h, src, :, HD:] = jnp.ones((rows, HD), jnp.bfloat16)
        return carry

    lax.fori_loop(0, n, fill_ones, 0)

    def one_shift(head, carry):
        cols = pl.ds(pl.multiple_of(head * HD, HD), HD)
        shifts = jnp.concatenate(
            [mod_buf[pl.ds(time_ref[me * frames_dev + f], 1), 0, cols] for f in range(frames_dev)] * (8 // frames_dev),
            axis=0,
        )
        return carry + lax.dot_general(
            shifts,
            weight_buf[:, cols],
            (((1,), (1,)), ((), ())),
            precision=highest,
            preferred_element_type=jnp.float32,
        )

    shift_buf[...] = lax.fori_loop(0, HEADS, one_shift, jnp.zeros(shift_buf.shape, jnp.float32))

    words = prompt_ref.shape[0]
    width = table_buf.shape[1]
    lane_ids = lax.broadcasted_iota(jnp.int32, (width, lanes), 1)
    pltpu.make_async_copy(table_buf, table_buf, local_sem.at[2]).wait()

    def one_word(w, carry):
        word = prompt_ref[w]
        block = table_buf[word // lanes]
        return carry + jnp.where(lane_ids == word % lanes, block.astype(jnp.float32), 0.0)

    picked = lax.fori_loop(0, words, one_word, jnp.zeros((width, lanes), jnp.float32))
    own_text = jnp.sum(picked, axis=-1, keepdims=True) / words
    place = (width, n * width)
    own_place = lax.broadcasted_iota(jnp.int32, place, 1) - me * width == lax.broadcasted_iota(
        jnp.int32, place, 0
    )
    text_buf[...] = jnp.sum(jnp.where(own_place, own_text, 0.0), axis=0, keepdims=True)

    def text_copy(peer):
        return remote(text_buf, text_all.at[me], text_send.at[peer], text_recv.at[me], peer)

    send_some(text_copy, 1, n)
    text_all[me] = text_buf[...]
    idle()

    def arrived(buf, recv):
        def body(x, carry):
            block = buf.at[x, :, pl.ds(0, HD)]
            pltpu.make_async_copy(block, block, recv.at[x]).wait()
            return carry

        lax.fori_loop(0, n, body, 0)

    logit_bufs = (logit_even, logit_odd)

    def score(slot, h, src):
        logits = lax.dot_general(
            q_buf[src, :, h * HD : (h + 1) * HD],
            k_buf[h].reshape(n * rows, HD),
            (((1,), (1,)), ((), ())),
            preferred_element_type=jnp.float32,
        )
        logit_bufs[slot][...] = logits
        peak_buf[slot] = jnp.broadcast_to(jnp.max(logits, axis=-1, keepdims=True), (rows, HD))

    def weigh(slot, h, src):
        row_peak = peak_buf[slot, :, 0:1]
        exponent = jnp.exp2((logit_bufs[slot][...] - row_peak) * (HD ** (-0.5) * 1.4426950408889634))
        mixed = jnp.dot(
            exponent.astype(jnp.bfloat16),
            v_buf[h].reshape(n * rows, 2 * HD),
            preferred_element_type=jnp.float32,
        )
        att_buf[src, :, h * HD : (h + 1) * HD] = (mixed[:, :HD] / mixed[:, HD:]).astype(jnp.bfloat16)

    def in_turn(first, heads, waits, done):
        count = half * len(heads)
        unroll = 2 if len(heads) == 1 else len(heads)

        def place(t):
            x = first + lax.rem(t // len(heads), half)
            return x, jnp.bitwise_xor(me, x)

        def begin(t, p, guard):
            x, src = place(t)
            h = heads[p % len(heads)]
            if waits and p % len(heads) == 0:

                @pl.when(guard)
                def _():
                    if first > 0:
                        follow_query(x)
                    pltpu.make_async_copy(q_buf.at[src], q_buf.at[src], q_recv.at[src]).wait()

            score(p % 2, h, src)

        begin(0, 0, me >= 0)

        def body(i, carry):
            for p in range(unroll):
                t = i * unroll + p
                begin(t + 1, p + 1, t + 1 < count)
                x, src = place(t)
                weigh(p % 2, heads[p % len(heads)], src)
                if p % len(heads) == len(heads) - 1:
                    done(x, src)
            return carry

        lax.fori_loop(0, count // unroll, body, 0)

    lane = lax.broadcasted_iota(jnp.int32, (per_frame, frames_dev * cols_n), 1)
    ones = jnp.ones((8, wide), jnp.bfloat16)
    turned = (((1,), (1,)), ((), ()))

    def project(x, src):
        packed = None
        for f in range(frames_dev):
            rows_a = att_buf[src, f * per_frame : (f + 1) * per_frame, :]
            both = lax.dot_general(
                rows_a, gain_buf[src * frames_dev + f], turned, preferred_element_type=jnp.float32
            )
            both = both + pltpu.roll(both, cols_n, 1)
            packed = both if packed is None else jnp.where(lane < f * cols_n, packed, both)
            rows_f = rows_a.astype(jnp.float32)
            squares = lax.dot_general(
                ones, (rows_f * rows_f).astype(jnp.bfloat16), turned, preferred_element_type=jnp.float32
            )
            sum_rows[x % 2, f * 8 : (f + 1) * 8, :per_frame] = squares
        part_buf[x, :per_frame, :] = packed.astype(jnp.bfloat16)
        part_buf[x, per_frame:, :] = sum_rows[x % 2].astype(jnp.bfloat16)

    for h in range(heads_here):
        if h > 0:
            follow(2 * h)
        if h + 1 < heads_here:
            send_some(phases[2 * h + 2], 1, half)
            send_some(phases[2 * h + 3], 1, half)
        follow(2 * h + 1)
        arrived(k_buf.at[h], k_recv.at[h])
        arrived(v_buf.at[h], v_recv.at[h])
        def near_done(x, src, h=h):
            if h == heads_here - 1:
                project(x, src)

                @pl.when(x > 0)
                def _():
                    remote(part_buf.at[x], own_buf.at[x], part_send.at[x], part_recv.at[x], src).start()

        in_turn(0, [h], h == 0, near_done)

    def far_done(x, src):
        project(x, src)

        @pl.when(x > half)
        def _():
            y = x - half
            to = jnp.bitwise_xor(me, y)
            remote(part_buf.at[x], mirror_buf.at[y], part_send.at[x], part_recv.at[x], to).start()

    in_turn(half, list(range(heads_here)), True, far_done)

    def part_wait(x):
        pltpu.make_async_copy(part_buf.at[x], part_buf.at[x], part_recv.at[x]).wait()

    total = part_buf[half].astype(jnp.float32)
    for y in range(1, half):
        part_wait(half + y)
        total = total + mirror_buf[y].astype(jnp.float32)
    sum_buf[...] = total.astype(jnp.bfloat16)
    cross = remote(sum_buf, cross_buf, cross_send, cross_recv, jnp.bitwise_xor(me, half))
    cross.start()
    total = part_buf[0].astype(jnp.float32)
    for y in range(1, half):
        part_wait(y)
        total = total + own_buf[y].astype(jnp.float32)
    cross.wait()
    total = total + cross_buf[...].astype(jnp.float32)
    diagonal = lax.broadcasted_iota(jnp.int32, (per_frame, per_frame), 0) == lax.broadcasted_iota(
        jnp.int32, (per_frame, per_frame), 1
    )
    latent_rows = jnp.transpose(latent_ref[...])
    pieces = []
    for f in range(frames_dev):
        row_sums = total[per_frame + f * 8 : per_frame + f * 8 + 1, :per_frame]
        meansq = jnp.sum(jnp.where(diagonal, row_sums, 0.0), axis=-1, keepdims=True) / (HEADS * HD)
        prediction = total[:per_frame, f * cols_n : (f + 1) * cols_n] * lax.rsqrt(meansq + 1e-06)
        moved = step_ref[time_ref[me * frames_dev + f]] * (prediction + shift_buf[f : f + 1, :])
        pieces.append(latent_rows[f * per_frame : (f + 1) * per_frame, :] + moved)
    latent_new = jnp.concatenate(pieces, axis=0)
    latent_wide = jnp.concatenate([latent_new, latent_new], axis=1)
    halo_buf[2] = latent_wide.astype(jnp.bfloat16)

    for back in (1, 2):
        step_to = remote(
            halo_buf.at[2], halo_buf.at[2 - back], halo_send.at[back - 1], halo_recv.at[back - 1], me + back
        )

        @pl.when(me + back < n)
        def _(step_to=step_to):
            step_to.start()

        @pl.when(me < back)
        def _(back=back):
            halo_buf[2 - back] = jnp.zeros(halo_buf.shape[1:], jnp.bfloat16)

    latent_out[...] = jnp.transpose(latent_new)

    def text_came(x, carry):
        src = jnp.bitwise_xor(me, x)
        pltpu.make_async_copy(text_all.at[src], text_all.at[src], text_recv.at[src]).wait()
        return carry

    lax.fori_loop(1, n, text_came, 0)
    text_out[...] = functools.reduce(jnp.add, [text_all[x] for x in range(n)])

    for back in (1, 2):
        step_to = remote(
            halo_buf.at[2], halo_buf.at[2 - back], halo_send.at[back - 1], halo_recv.at[back - 1], me + back
        )

        @pl.when(me >= back)
        def _(step_to=step_to):
            step_to.wait_recv()

        @pl.when(me + back < n)
        def _(step_to=step_to):
            step_to.wait_send()


    def finish():
        def near_sent(x, carry):
            for copy in phases + [query_copy]:
                copy(jnp.bitwise_xor(me, x)).wait_send()
            return carry

        def text_sent(x, carry):
            text_copy(jnp.bitwise_xor(me, x)).wait_send()
            return carry

        lax.fori_loop(1, half, near_sent, 0)
        lax.fori_loop(1, n, text_sent, 0)

        def parts_sent(x, carry):
            remote(part_buf.at[x], own_buf.at[0], part_send.at[x], part_recv.at[x], jnp.bitwise_xor(me, 1)).wait_send()
            return carry

        lax.fori_loop(1, half, parts_sent, 0)
        lax.fori_loop(half + 1, n, parts_sent, 0)

    return finish


TAPS = {(a, q): ((a + q - 1) % 2, (a + q - 1) // 2) for a in range(2) for q in range(3)}


def decode_kernel(
    n,
    halo_ref,
    text_ref,
    first_hbm,
    first_bias_ref,
    gain_ref,
    conv_hbm,
    conv_bias_ref,
    patch_hbm,
    patch_gain_ref,
    post_gain_ref,
    proj_hbm,
    order_ref,
    decoded_out,
    image_out,
    score_out,
    first_w,
    first_taps,
    wide_in,
    first_buf,
    window,
    conv_w,
    acc,
    pixels,
    patches,
    patch_w,
    proj_w,
    proj_high,
    proj_low,
    decoded_buf,
    image_buf,
    image_all,
    image_send,
    image_recv,
    local_sem,
):
    me = lax.axis_index("seq")
    per_frame = GRID_H * GRID_W
    frames_dev = image_buf.shape[0]
    held = frames_dev + 2
    cols_n = halo_ref.shape[2] // 2
    lat_c = cols_n // 4
    ch = first_buf.shape[2]
    f32, b16 = jnp.float32, jnp.bfloat16

    out_copy = pltpu.make_async_copy(decoded_buf, decoded_out, local_sem.at[4])
    copies = [
        pltpu.make_async_copy(src, dst, local_sem.at[i])
        for i, (src, dst) in enumerate(
            ((first_hbm, first_w), (conv_hbm, conv_w), (patch_hbm, patch_w), (proj_hbm, proj_w))
        )
    ]
    def early():
        for cp in copies:
            cp.start()

    def idle():
        first_taps[...] = jnp.zeros_like(first_taps)
        copies[0].wait()
        for a in range(2):
            for b in range(2):
                for lag in range(3):
                    for q in range(3):
                        for r in range(3):
                            (sub_a, di), (sub_b, dj) = TAPS[a, q], TAPS[b, r]
                            u, v = di + 1 - a, dj + 1 - b
                            at = ((u * 2 + v) * 4 + sub_a * 2 + sub_b) * lat_c
                            first_taps[2 * a + b, lag, at : at + lat_c, :] = first_w[lag * 9 + q * 3 + r]
        for cp in copies[1:]:
            cp.wait()
        whole = proj_w[...]
        high = whole.astype(b16)
        proj_high[...] = high
        proj_low[...] = (whole - high.astype(f32)).astype(b16)

    yield early, idle

    latents = halo_ref[...].reshape(-1, 2 * cols_n).astype(f32)
    total_rows = latents.shape[0]
    token = lax.rem(lax.broadcasted_iota(jnp.int32, latents.shape, 0), per_frame)
    row_id, col_id = token // GRID_W, lax.rem(token, GRID_W)
    lane = lax.broadcasted_iota(jnp.int32, latents.shape, 1)
    for di in (-1, 0, 1):
        moved = []
        for dj in (-1, 0, 1):
            step = GRID_W * di + dj
            value = latents if step == 0 else pltpu.roll(latents, (-step) % total_rows, 0)
            keep = (row_id + di >= 0) & (row_id + di < GRID_H) & (col_id + dj >= 0) & (col_id + dj < GRID_W)
            moved.append(value if step == 0 else jnp.where(keep, value, 0.0))
        for b in range(2):
            pair = jnp.where(lane < cols_n, moved[b], moved[b + 1]).astype(b16)
            for a in range(2):
                u = di + 1 - a
                if 0 <= u < 2:
                    wide_in[2 * a + b, :, u * 2 * cols_n : (u + 1) * 2 * cols_n] = pair

    first_bias = first_bias_ref[...][None, :]
    for ab in range(4):
        summed = None
        for lag in range(3):
            term = jnp.dot(
                wide_in[ab, lag * per_frame : (lag + held) * per_frame, :],
                first_taps[ab, lag],
                preferred_element_type=f32,
            )
            summed = term if summed is None else summed + term
        first_buf[ab] = (summed + first_bias).astype(b16)

    gain = gain_ref[...][None, :]
    token = lax.broadcasted_iota(jnp.int32, (per_frame, ch), 0)
    row_id, col_id = token // GRID_W, lax.rem(token, GRID_W)

    def one_frame(f, carry):
        live = (me * frames_dev - 2 + f) >= 0
        span = pl.ds(pl.multiple_of(f * per_frame, per_frame), per_frame)
        for sub_a in range(2):
            for sub_b in range(2):
                first_f = first_buf[2 * sub_a + sub_b, span, :].astype(f32)
                meansq = jnp.mean(first_f * first_f, axis=-1, keepdims=True)
                value = jax.nn.silu(first_f * lax.rsqrt(meansq + 1e-06) * gain)
                value = jnp.where(live, value, 0.0)
                for di in (0, -1 if sub_a else 1):
                    for dj in (0, -1 if sub_b else 1):
                        step = GRID_W * di + dj
                        shifted = value
                        if step:
                            shifted = pltpu.roll(value, (-step) % per_frame, 0)
                            keep = (
                                (row_id + di >= 0)
                                & (row_id + di < GRID_H)
                                & (col_id + dj >= 0)
                                & (col_id + dj < GRID_W)
                            )
                            shifted = jnp.where(keep, shifted, 0.0)
                        shifted = shifted.astype(b16)
                        for (a, q), source_a in TAPS.items():
                            for (b, r), source_b in TAPS.items():
                                if source_a == (sub_a, di) and source_b == (sub_b, dj):
                                    tap = q * 3 + r
                                    window[f, 2 * a + b, :, tap * ch : (tap + 1) * ch] = shifted
        return carry

    lax.fori_loop(0, held, one_frame, 0)

    taps_n = 9
    conv_bias = conv_bias_ref[...][None, :]
    for f in range(frames_dev):
        for ab in range(4):
            own = first_buf[ab, (f + 2) * per_frame : (f + 3) * per_frame, :].astype(f32)
            acc[(f * 4 + ab) * per_frame : (f * 4 + ab + 1) * per_frame, :] = own + conv_bias

    def one_lag(lag, carry):
        rows = window[pl.ds(lag, frames_dev)].reshape(frames_dev * 4 * per_frame, taps_n * ch)
        weight = conv_w[pl.ds(lag * taps_n, taps_n)].reshape(taps_n * ch, ch)
        acc[...] += jnp.dot(rows, weight, preferred_element_type=f32)
        return carry

    lax.fori_loop(0, 3, one_lag, 0)

    for f in range(frames_dev):
        for a in range(2):
            for b in range(2):
                base = (f * 4 + 2 * a + b) * per_frame
                for i in range(GRID_H):
                    for c in range(pixels.shape[0]):
                        pixels[c, f, 2 * i + a, pl.ds(b, GRID_W, stride=2), :] = acc[
                            pl.ds(base + i * GRID_W, GRID_W), c * 128 : (c + 1) * 128
                        ]
                patches[f * per_frame : (f + 1) * per_frame, (2 * a + b) * ch : (2 * a + b + 1) * ch] = acc[
                    base : base + per_frame, :
                ].astype(b16)
    for c in range(pixels.shape[0]):
        decoded_buf[:, :, :, c * 128 : (c + 1) * 128] = pixels[c].astype(b16)
    out_copy.start()

    embedded = jnp.dot(patches[...], patch_w[...], preferred_element_type=f32).astype(b16).astype(f32)
    centered = embedded - jnp.mean(embedded, axis=-1, keepdims=True)
    variance = jnp.mean(centered * centered, axis=-1, keepdims=True)
    normed = centered * lax.rsqrt(variance + 1e-05)
    pooled = jnp.concatenate(
        [
            jnp.mean(normed[f * per_frame : (f + 1) * per_frame], axis=0, keepdims=True)
            for f in range(frames_dev)
        ],
        axis=0,
    ) * patch_gain_ref[...][None, :]
    centered = pooled - jnp.mean(pooled, axis=-1, keepdims=True)
    variance = jnp.mean(centered * centered, axis=-1, keepdims=True)
    pooled = centered * lax.rsqrt(variance + 1e-05) * post_gain_ref[...][None, :]

    pooled_high = pooled.astype(b16).astype(f32)
    blank = jnp.zeros((16 - 2 * frames_dev, pooled.shape[1]), f32)
    pair = jnp.concatenate([pooled_high, pooled - pooled_high, blank], axis=0).astype(b16)
    main = jnp.dot(pair, proj_high[...], preferred_element_type=f32)
    rest = jnp.dot(pair, proj_low[...], preferred_element_type=f32)
    image = main[:frames_dev] + (main[frames_dev : 2 * frames_dev] + rest[:frames_dev])
    for f in range(frames_dev):
        image_buf[f] = image[f : f + 1, :]

    def image_copy(peer):
        return remote(
            image_buf,
            image_all.at[pl.ds(me * frames_dev, frames_dev)],
            image_send.at[peer],
            image_recv.at[me],
            peer,
        )

    def spread(x, carry):
        image_copy(jnp.bitwise_xor(me, x)).start()
        return carry

    lax.fori_loop(1, n, spread, 0)
    image_all[pl.ds(me * frames_dev, frames_dev)] = image_buf[...]

    def came(x, carry):
        src = jnp.bitwise_xor(me, x)
        block = image_all.at[pl.ds(src * frames_dev, frames_dev)]
        pltpu.make_async_copy(block, block, image_recv.at[src]).wait()
        return carry

    lax.fori_loop(1, n, came, 0)
    text = text_ref[...]
    text_rms = jnp.sqrt(jnp.mean(text * text, keepdims=True) + 1e-06)
    for f in range(frames_dev):
        vector = image_all[order_ref[me * frames_dev + f]]
        image_out[f : f + 1, :] = vector
        inner = jnp.sum(vector * text, keepdims=True)
        image_rms = jnp.sqrt(jnp.mean(vector * vector, keepdims=True) + 1e-06)
        score_out[f] = (100.0 * inner / (TEXT_W * image_rms * text_rms))[0, 0]

    def gone(x, carry):
        image_copy(jnp.bitwise_xor(me, x)).wait_send()
        return carry

    lax.fori_loop(1, n, gone, 0)
    out_copy.wait()
    yield


MIX_IN, DECODE_IN, MIX_SCRATCH, HALO_AT = 10, 10, 36, 17
SMALL_MIX, SMALL_DECODE = (3, 5, 6, 9), (1, 2, 4, 6, 7, 9)


def whole_kernel(n, heads_here, *refs):
    mix_in, refs = refs[:MIX_IN], refs[MIX_IN:]
    decode_in, refs = refs[:DECODE_IN], refs[DECODE_IN:]
    (latent_out, decoded_out, image_out, score_out), refs = refs[:4], refs[4:]
    (text_full, *mix_scratch), decode_scratch = refs[: MIX_SCRATCH + 1], refs[MIX_SCRATCH + 1 :]
    halo_buf = mix_scratch[HALO_AT]
    *decode_scratch, small_sem = decode_scratch
    small_bufs = decode_scratch[-len(SMALL_MIX) - len(SMALL_DECODE) :]
    decode_scratch = decode_scratch[: -len(small_bufs)]
    mix_in, decode_in = list(mix_in), list(decode_in)
    small_copies = []
    for group, places in ((mix_in, SMALL_MIX), (decode_in, SMALL_DECODE)):
        for place in places:
            i = len(small_copies)
            small_copies.append(pltpu.make_async_copy(group[place], small_bufs[i], small_sem.at[i]))
            small_copies[-1].start()
            group[place] = small_bufs[i]
    steps = decode_kernel(n, halo_buf, text_full, *decode_in, decoded_out, image_out, score_out, *decode_scratch)
    start_weights, idle = next(steps)

    def early():
        start_weights()
        for cp in small_copies:
            cp.wait()

    finish = mix_kernel(n, heads_here, *mix_in, early, idle, latent_out, text_full, *mix_scratch)
    next(steps)
    finish()


def everything(
    queries,
    keys,
    values,
    latent_in,
    mod_table,
    step_size,
    timestep,
    head_weight,
    text_table,
    prompt_ids,
    conv_in_weight,
    conv_in_bias,
    norm_gain,
    conv_weight,
    conv_bias,
    patch_weight,
    patch_gain,
    post_gain,
    proj_weight,
    frame_order,
):
    n = lax.axis_size("seq")
    heads_here = HEADS // n
    rows, cols_n = latent_in.shape
    width = text_table.shape[1]
    wide = heads_here * HD
    half = n // 2
    frames_all = timestep.shape[0]
    frames_dev = frames_all // n
    per_frame = rows // frames_dev
    part = (per_frame + 8 * frames_dev, frames_dev * cols_n)
    held = frames_dev + 2
    ch = conv_weight.shape[2]
    text_w = proj_weight.shape[1]
    pixel_shape = (frames_dev, 2 * GRID_H, 2 * GRID_W, ch)
    vmem = pltpu.VMEM
    dma = pltpu.SemaphoreType.DMA
    f32, b16 = jnp.float32, jnp.bfloat16
    far = pl.BlockSpec(memory_space=pltpu.HBM)
    near = pl.BlockSpec(memory_space=pltpu.VMEM)
    scalars = pl.BlockSpec(memory_space=pltpu.SMEM)
    mix_scratch = [
        vmem((heads_here, n, rows, HD), b16),
        vmem((heads_here, n, rows, 2 * HD), b16),
        vmem((n, rows, wide), b16),
        vmem((n, rows, wide), b16),
        vmem((n,) + part, b16),
        vmem((half,) + part, b16),
        vmem((half,) + part, b16),
        vmem(part, b16),
        vmem(part, b16),
        vmem(mod_table.shape, f32),
        vmem((cols_n, HEADS * HD), f32),
        vmem((frames_all, 2 * cols_n, wide), b16),
        vmem((8, cols_n), f32),
        vmem((2, 8 * frames_dev, frames_dev * cols_n), f32),
        vmem((rows, n * rows), f32),
        vmem((rows, n * rows), f32),
        vmem((2, rows, HD), f32),
        vmem((3, rows, 2 * cols_n), b16),
        vmem((text_table.shape[0] // 128, width, 128), b16),
        vmem((1, n * width), f32),
        vmem((n, 1, n * width), f32),
        dma((heads_here, n)),
        dma((heads_here, n)),
        dma((heads_here, n)),
        dma((heads_here, n)),
        dma((n,)),
        dma((n,)),
        dma((n,)),
        dma((n,)),
        dma,
        dma,
        dma((2,)),
        dma((2,)),
        dma((n,)),
        dma((n,)),
        dma((3,)),
    ]
    decode_scratch = [
        vmem(conv_in_weight.shape, b16),
        vmem((4, 3, 4 * cols_n, ch), b16),
        vmem((4, (held + 2) * per_frame, 4 * cols_n), b16),
        vmem((4, held * per_frame, ch), b16),
        vmem((held, 4, per_frame, 9 * ch), b16),
        vmem(conv_weight.shape, b16),
        vmem((frames_dev * 4 * per_frame, ch), f32),
        vmem((ch // 128, frames_dev, 2 * GRID_H, 2 * GRID_W, 128), f32),
        vmem((frames_dev * per_frame, 4 * ch), b16),
        vmem(patch_weight.shape, b16),
        vmem(proj_weight.shape, f32),
        vmem(proj_weight.shape, b16),
        vmem(proj_weight.shape, b16),
        vmem(pixel_shape, b16),
        vmem((frames_dev, 1, text_w), f32),
        vmem((n * frames_dev, 1, text_w), f32),
        dma((n,)),
        dma((n,)),
        dma((5,)),
        vmem((cols_n, rows), f32),
        pltpu.SMEM(step_size.shape, f32),
        pltpu.SMEM(timestep.shape, jnp.int32),
        pltpu.SMEM(prompt_ids.shape, jnp.int32),
        vmem(conv_in_bias.shape, f32),
        vmem(norm_gain.shape, f32),
        vmem(conv_bias.shape, f32),
        vmem(patch_gain.shape, f32),
        vmem(post_gain.shape, f32),
        pltpu.SMEM(frame_order.shape, jnp.int32),
        dma((len(SMALL_MIX) + len(SMALL_DECODE),)),
    ]
    assert len(mix_scratch) == MIX_SCRATCH
    results = pl.pallas_call(
        functools.partial(whole_kernel, n, heads_here),
        out_shape=(
            jax.ShapeDtypeStruct((cols_n, rows), f32),
            jax.ShapeDtypeStruct(pixel_shape, b16),
            jax.ShapeDtypeStruct((frames_dev, text_w), f32),
            jax.ShapeDtypeStruct((frames_dev,), f32),
        ),
        in_specs=[far] * (MIX_IN + DECODE_IN),
        out_specs=(near, far, near, scalars),
        scratch_shapes=[vmem((1, text_w), f32)] + mix_scratch + decode_scratch,
        compiler_params=pltpu.CompilerParams(
            collective_id=0, has_side_effects=True, vmem_limit_bytes=67043328
        ),
        name="everything",
    )(
        queries,
        keys,
        values,
        latent_in.T,
        mod_table,
        step_size,
        timestep,
        head_weight.T,
        text_table.T,
        prompt_ids,
        conv_in_weight,
        conv_in_bias,
        norm_gain,
        conv_weight,
        conv_bias,
        patch_weight,
        patch_gain,
        post_gain,
        proj_weight,
        frame_order,
    )
    return deliver(*results)


def deliver_kernel(*refs):
    count = len(refs) // 2
    for source, target in zip(refs[: count - 1], refs[count:-1]):
        target[...] = source[...]
    for f in range(refs[-1].shape[0]):
        refs[-1][f] = refs[count - 1][f]


def deliver(*arrays):
    near = pl.BlockSpec(memory_space=pltpu.VMEM)
    specs = [near] * (len(arrays) - 1) + [pl.BlockSpec(memory_space=pltpu.SMEM)]
    return pl.pallas_call(
        deliver_kernel,
        out_shape=[jax.ShapeDtypeStruct(a.shape, a.dtype) for a in arrays],
        in_specs=specs,
        out_specs=specs,
        name="deliver",
    )(*arrays)


def local(
    queries,
    keys,
    values,
    latent_in,
    mod_table,
    step_size,
    timestep,
    head_weight,
    conv_in_weight,
    conv_in_bias,
    norm_gain,
    conv_weight,
    conv_bias,
    patch_weight,
    patch_gain,
    post_gain,
    proj_weight,
    text_table,
    prompt_ids,
    frame_order,
):
    latent_turned, decoded, image_vec, scores = everything(
        queries,
        keys,
        values,
        latent_in,
        mod_table,
        step_size,
        timestep,
        head_weight,
        text_table,
        prompt_ids,
        conv_in_weight,
        conv_in_bias,
        norm_gain,
        conv_weight,
        conv_bias,
        patch_weight,
        patch_gain,
        post_gain,
        proj_weight,
        frame_order,
    )
    return (latent_turned.T, decoded, image_vec, scores)


def solution(mesh):
    in_specs = (
        P(("grp", "seq"), None),
        P(("grp", "seq"), None),
        P(("grp", "seq"), None),
        P(("grp", "seq"), None),
        P(),
        P(),
        P("grp"),
        P(),
        P(),
        P(),
        P(),
        P(),
        P(),
        P(),
        P(),
        P(),
        P(),
        P(None, "seq"),
        P("grp"),
        P("grp"),
    )
    out_specs = (
        P(("grp", "seq"), None),
        P(("grp", "seq"), None, None, None),
        P(("grp", "seq"), None),
        P(("grp", "seq")),
    )
    return jax.shard_map(local, mesh=mesh, in_specs=in_specs, out_specs=out_specs, check_vma=False)
```

```python
import functools

import jax
import jax.numpy as jnp
from jax import lax
from jax.experimental import pallas as pl
from jax.experimental.pallas import tpu as pltpu
from jax.sharding import PartitionSpec as P

GRID_H = 8
GRID_W = 12
HEADS = 32
HD = 128
LAT_C = 16
CH = 384
TEXT_W = 768


highest = lax.Precision.HIGHEST


MESH = pl.DeviceIdType.MESH
AHEAD = 4


def remote(src, dst, send, recv, device):
    return pltpu.make_async_remote_copy(
        src_ref=src, dst_ref=dst, send_sem=send, recv_sem=recv, device_id={"seq": device}, device_id_type=MESH
    )


def mix_kernel(
    n,
    heads_here,
    q_hbm,
    k_hbm,
    v_hbm,
    latent_ref,
    mod_hbm,
    step_ref,
    time_ref,
    weight_hbm,
    table_hbm,
    prompt_ref,
    early,
    idle,
    latent_out,
    text_out,
    k_buf,
    v_buf,
    q_buf,
    part_buf,
    own_buf,
    mirror_buf,
    cross_buf,
    sum_buf,
    mod_buf,
    weight_buf,
    gain_buf,
    shift_buf,
    sum_rows,
    logit_even,
    logit_odd,
    peak_buf,
    halo_buf,
    table_buf,
    text_buf,
    text_all,
    k_send,
    k_recv,
    v_send,
    v_recv,
    q_send,
    q_recv,
    part_send,
    part_recv,
    cross_send,
    cross_recv,
    halo_send,
    halo_recv,
    text_send,
    text_recv,
    local_sem,
):
    me = lax.axis_index("seq")
    half = n // 2
    rows = q_buf.shape[1]
    wide = heads_here * HD
    cols_n = latent_ref.shape[0]
    frames_dev = rows // (GRID_H * GRID_W)
    per_frame = rows // frames_dev
    first_col = pl.multiple_of(me * wide, wide)

    locals_ = [pltpu.make_async_copy(mod_hbm, mod_buf, local_sem.at[0])]
    locals_.append(pltpu.make_async_copy(weight_hbm, weight_buf, local_sem.at[1]))
    own_cp = []
    for h in range(heads_here):
        own_col = pl.ds(pl.multiple_of(me * wide + h * HD, HD), HD)
        own_cp.append(pltpu.make_async_copy(k_hbm.at[:, own_col], k_buf.at[h, me], k_recv.at[h, me]))
        own_cp.append(pltpu.make_async_copy(v_hbm.at[:, own_col], v_buf.at[h, me, :, pl.ds(0, HD)], v_recv.at[h, me]))
    own_cp.append(pltpu.make_async_copy(q_hbm.at[:, pl.ds(first_col, wide)], q_buf.at[me], q_recv.at[me]))

    barrier = pltpu.get_barrier_semaphore()

    def greet(x, carry):
        pl.semaphore_signal(barrier, inc=1, device_id={"seq": jnp.bitwise_xor(me, x)}, device_id_type=MESH)
        return carry

    lax.fori_loop(1, n, greet, 0)
    pl.semaphore_wait(barrier, n - 1)

    def head_copy(hbm, buf, send, recv, h, peer):
        cols = pl.ds(pl.multiple_of(peer * wide + h * HD, HD), HD)
        return remote(
            hbm.at[:, cols], buf.at[h, me, :, pl.ds(0, HD)], send.at[h, peer], recv.at[h, me], peer
        )

    def query_copy(peer):
        cols = pl.ds(pl.multiple_of(peer * wide, wide), wide)
        return remote(q_hbm.at[:, cols], q_buf.at[me], q_send.at[peer], q_recv.at[me], peer)

    def send_some(make, first, last):
        def body(x, carry):
            make(jnp.bitwise_xor(me, x)).start()
            return carry

        lax.fori_loop(first, last, body, 0)

    phases = []
    for h in range(heads_here):
        phases.append(lambda peer, h=h: head_copy(k_hbm, k_buf, k_send, k_recv, h, peer))
        phases.append(lambda peer, h=h: head_copy(v_hbm, v_buf, v_send, v_recv, h, peer))

    def follow(phase):
        def body(x, carry):
            peer = jnp.bitwise_xor(me, x)
            phases[phase](peer).wait_send()
            if phase + 1 < len(phases):
                phases[phase + 1](peer).start()
            else:

                @pl.when(x < half + AHEAD)
                def _():
                    query_copy(peer).start()

            return carry

        lax.fori_loop(half, n, body, 0)

    def follow_query(x):
        query_copy(jnp.bitwise_xor(me, x)).wait_send()

        @pl.when(x + AHEAD < n)
        def _():
            query_copy(jnp.bitwise_xor(me, x + AHEAD)).start()

    send_some(phases[0], 1, n)
    send_some(phases[1], 1, half)
    send_some(query_copy, 1, half)
    for cp in locals_ + own_cp:
        cp.start()
    early()
    for cp in locals_:
        cp.wait()

    follow(0)
    lanes = table_buf.shape[2]

    def table_part(i, carry):
        part = table_hbm.at[:, pl.ds(pl.multiple_of(i * lanes, lanes), lanes)]
        pltpu.make_async_copy(part, table_buf.at[i], local_sem.at[2]).start()
        return carry

    lax.fori_loop(0, table_buf.shape[0], table_part, 0)

    weight_own = weight_buf[:, pl.ds(first_col, wide)]

    def prepare(f, carry):
        gain = mod_buf[pl.ds(time_ref[f], 1), 1, pl.ds(first_col, wide)]
        scaled = (1.0 + gain) * weight_own
        high = scaled.astype(jnp.bfloat16)
        low = (scaled - high.astype(jnp.float32)).astype(jnp.bfloat16)
        gain_buf[f] = jnp.concatenate([high, low], axis=0)
        return carry

    lax.fori_loop(0, n * frames_dev, prepare, 0)

    def fill_ones(src, carry):
        for h in range(heads_here):
            v_buf[h, src, :, HD:] = jnp.ones((rows, HD), jnp.bfloat16)
        return carry

    lax.fori_loop(0, n, fill_ones, 0)

    def one_shift(head, carry):
        cols = pl.ds(pl.multiple_of(head * HD, HD), HD)
        shifts = jnp.concatenate(
            [mod_buf[pl.ds(time_ref[me * frames_dev + f], 1), 0, cols] for f in range(frames_dev)] * (8 // frames_dev),
            axis=0,
        )
        return carry + lax.dot_general(
            shifts,
            weight_buf[:, cols],
            (((1,), (1,)), ((), ())),
            precision=highest,
            preferred_element_type=jnp.float32,
        )

    shift_buf[...] = lax.fori_loop(0, HEADS, one_shift, jnp.zeros(shift_buf.shape, jnp.float32))

    words = prompt_ref.shape[0]
    width = table_buf.shape[1]
    lane_ids = lax.broadcasted_iota(jnp.int32, (width, lanes), 1)
    pltpu.make_async_copy(table_buf, table_buf, local_sem.at[2]).wait()

    def one_word(w, carry):
        word = prompt_ref[w]
        block = table_buf[word // lanes]
        return carry + jnp.where(lane_ids == word % lanes, block.astype(jnp.float32), 0.0)

    picked = lax.fori_loop(0, words, one_word, jnp.zeros((width, lanes), jnp.float32))
    own_text = jnp.sum(picked, axis=-1, keepdims=True) / words
    place = (width, n * width)
    own_place = lax.broadcasted_iota(jnp.int32, place, 1) - me * width == lax.broadcasted_iota(
        jnp.int32, place, 0
    )
    text_buf[...] = jnp.sum(jnp.where(own_place, own_text, 0.0), axis=0, keepdims=True)

    def text_copy(peer):
        return remote(text_buf, text_all.at[me], text_send.at[peer], text_recv.at[me], peer)

    send_some(text_copy, 1, n)
    text_all[me] = text_buf[...]
    idle()

    def arrived(buf, recv):
        def body(x, carry):
            block = buf.at[x, :, pl.ds(0, HD)]
            pltpu.make_async_copy(block, block, recv.at[x]).wait()
            return carry

        lax.fori_loop(0, n, body, 0)

    logit_bufs = (logit_even, logit_odd)

    def score(slot, h, src):
        logits = lax.dot_general(
            q_buf[src, :, h * HD : (h + 1) * HD],
            k_buf[h].reshape(n * rows, HD),
            (((1,), (1,)), ((), ())),
            preferred_element_type=jnp.float32,
        )
        logit_bufs[slot][...] = logits
        peak_buf[slot] = jnp.broadcast_to(jnp.max(logits, axis=-1, keepdims=True), (rows, HD))

    def weigh(slot, h, src):
        row_peak = peak_buf[slot, :, 0:1]
        exponent = jnp.exp2((logit_bufs[slot][...] - row_peak) * (HD ** (-0.5) * 1.4426950408889634))
        mixed = jnp.dot(
            exponent.astype(jnp.bfloat16),
            v_buf[h].reshape(n * rows, 2 * HD),
            preferred_element_type=jnp.float32,
        )
        q_buf[src, :, h * HD : (h + 1) * HD] = (mixed[:, :HD] / mixed[:, HD:]).astype(jnp.bfloat16)

    def in_turn(first, heads, waits, done):
        count = half * len(heads)
        unroll = 2 if len(heads) == 1 else len(heads)

        def place(t):
            x = first + lax.rem(t // len(heads), half)
            return x, jnp.bitwise_xor(me, x)

        def begin(t, p, guard):
            x, src = place(t)
            h = heads[p % len(heads)]
            if waits and p % len(heads) == 0:

                @pl.when(guard)
                def _():
                    if first > 0:
                        follow_query(x)
                    pltpu.make_async_copy(q_buf.at[src], q_buf.at[src], q_recv.at[src]).wait()

            score(p % 2, h, src)

        begin(0, 0, me >= 0)

        def body(i, carry):
            for p in range(unroll):
                t = i * unroll + p
                begin(t + 1, p + 1, t + 1 < count)
                x, src = place(t)
                weigh(p % 2, heads[p % len(heads)], src)
                if p % len(heads) == len(heads) - 1:
                    done(x, src)
            return carry

        lax.fori_loop(0, count // unroll, body, 0)

    lane = lax.broadcasted_iota(jnp.int32, (per_frame, frames_dev * cols_n), 1)
    ones = jnp.ones((8, wide), jnp.bfloat16)
    turned = (((1,), (1,)), ((), ()))

    def project(x, src):
        packed = None
        for f in range(frames_dev):
            rows_a = q_buf[src, f * per_frame : (f + 1) * per_frame, :]
            both = lax.dot_general(
                rows_a, gain_buf[src * frames_dev + f], turned, preferred_element_type=jnp.float32
            )
            both = both + pltpu.roll(both, cols_n, 1)
            packed = both if packed is None else jnp.where(lane < f * cols_n, packed, both)
            rows_f = rows_a.astype(jnp.float32)
            squares = lax.dot_general(
                ones, (rows_f * rows_f).astype(jnp.bfloat16), turned, preferred_element_type=jnp.float32
            )
            sum_rows[x % 2, f * 8 : (f + 1) * 8, :per_frame] = squares
        part_buf[x, :per_frame, :] = packed.astype(jnp.bfloat16)
        part_buf[x, per_frame:, :] = sum_rows[x % 2].astype(jnp.bfloat16)

    for h in range(heads_here):
        if h > 0:
            follow(2 * h)
        if h + 1 < heads_here:
            send_some(phases[2 * h + 2], 1, half)
            send_some(phases[2 * h + 3], 1, half)
        follow(2 * h + 1)
        arrived(k_buf.at[h], k_recv.at[h])
        arrived(v_buf.at[h], v_recv.at[h])
        def near_done(x, src, h=h):
            if h == heads_here - 1:
                project(x, src)

                @pl.when(x > 0)
                def _():
                    remote(part_buf.at[x], own_buf.at[x], part_send.at[x], part_recv.at[x], src).start()

        in_turn(0, [h], h == 0, near_done)

    def far_done(x, src):
        project(x, src)

        @pl.when(x > half)
        def _():
            y = x - half
            to = jnp.bitwise_xor(me, y)
            remote(part_buf.at[x], mirror_buf.at[y], part_send.at[x], part_recv.at[x], to).start()

    in_turn(half, list(range(heads_here)), True, far_done)

    def part_wait(x):
        pltpu.make_async_copy(part_buf.at[x], part_buf.at[x], part_recv.at[x]).wait()

    total = part_buf[half].astype(jnp.float32)
    for y in range(1, half):
        part_wait(half + y)
        total = total + mirror_buf[y].astype(jnp.float32)
    sum_buf[...] = total.astype(jnp.bfloat16)
    cross = remote(sum_buf, cross_buf, cross_send, cross_recv, jnp.bitwise_xor(me, half))
    cross.start()
    total = part_buf[0].astype(jnp.float32)
    for y in range(1, half):
        part_wait(y)
        total = total + own_buf[y].astype(jnp.float32)
    cross.wait()
    total = total + cross_buf[...].astype(jnp.float32)
    diagonal = lax.broadcasted_iota(jnp.int32, (per_frame, per_frame), 0) == lax.broadcasted_iota(
        jnp.int32, (per_frame, per_frame), 1
    )
    latent_rows = jnp.transpose(latent_ref[...])
    pieces = []
    for f in range(frames_dev):
        row_sums = total[per_frame + f * 8 : per_frame + f * 8 + 1, :per_frame]
        meansq = jnp.sum(jnp.where(diagonal, row_sums, 0.0), axis=-1, keepdims=True) / (HEADS * HD)
        prediction = total[:per_frame, f * cols_n : (f + 1) * cols_n] * lax.rsqrt(meansq + 1e-06)
        moved = step_ref[time_ref[me * frames_dev + f]] * (prediction + shift_buf[f : f + 1, :])
        pieces.append(latent_rows[f * per_frame : (f + 1) * per_frame, :] + moved)
    latent_new = jnp.concatenate(pieces, axis=0)
    latent_wide = jnp.concatenate([latent_new, latent_new], axis=1)
    halo_buf[2] = latent_wide.astype(jnp.bfloat16)

    for back in (1, 2):
        step_to = remote(
            halo_buf.at[2], halo_buf.at[2 - back], halo_send.at[back - 1], halo_recv.at[back - 1], me + back
        )

        @pl.when(me + back < n)
        def _(step_to=step_to):
            step_to.start()

        @pl.when(me < back)
        def _(back=back):
            halo_buf[2 - back] = jnp.zeros(halo_buf.shape[1:], jnp.bfloat16)

    latent_out[...] = jnp.transpose(latent_new)

    def text_came(x, carry):
        src = jnp.bitwise_xor(me, x)
        pltpu.make_async_copy(text_all.at[src], text_all.at[src], text_recv.at[src]).wait()
        return carry

    lax.fori_loop(1, n, text_came, 0)
    text_out[...] = functools.reduce(jnp.add, [text_all[x] for x in range(n)])

    for back in (1, 2):
        step_to = remote(
            halo_buf.at[2], halo_buf.at[2 - back], halo_send.at[back - 1], halo_recv.at[back - 1], me + back
        )

        @pl.when(me >= back)
        def _(step_to=step_to):
            step_to.wait_recv()

        @pl.when(me + back < n)
        def _(step_to=step_to):
            step_to.wait_send()


    def finish():
        def near_sent(x, carry):
            for copy in phases + [query_copy]:
                copy(jnp.bitwise_xor(me, x)).wait_send()
            return carry

        def text_sent(x, carry):
            text_copy(jnp.bitwise_xor(me, x)).wait_send()
            return carry

        lax.fori_loop(1, half, near_sent, 0)
        lax.fori_loop(1, n, text_sent, 0)

        def parts_sent(x, carry):
            remote(part_buf.at[x], own_buf.at[0], part_send.at[x], part_recv.at[x], jnp.bitwise_xor(me, 1)).wait_send()
            return carry

        lax.fori_loop(1, half, parts_sent, 0)
        lax.fori_loop(half + 1, n, parts_sent, 0)

    return finish


TAPS = {(a, q): ((a + q - 1) % 2, (a + q - 1) // 2) for a in range(2) for q in range(3)}


def decode_kernel(
    n,
    halo_ref,
    text_ref,
    first_hbm,
    first_bias_ref,
    gain_ref,
    conv_hbm,
    conv_bias_ref,
    patch_hbm,
    patch_gain_ref,
    post_gain_ref,
    proj_hbm,
    order_ref,
    decoded_out,
    image_out,
    score_out,
    first_w,
    first_taps,
    wide_in,
    first_buf,
    window,
    conv_w,
    acc,
    pixels,
    patches,
    patch_w,
    proj_w,
    proj_high,
    proj_low,
    decoded_buf,
    image_buf,
    image_all,
    image_send,
    image_recv,
    local_sem,
):
    me = lax.axis_index("seq")
    per_frame = GRID_H * GRID_W
    frames_dev = image_buf.shape[0]
    held = frames_dev + 2
    cols_n = halo_ref.shape[2] // 2
    lat_c = cols_n // 4
    ch = first_buf.shape[2]
    f32, b16 = jnp.float32, jnp.bfloat16

    out_copy = pltpu.make_async_copy(decoded_buf, decoded_out, local_sem.at[4])
    copies = [
        pltpu.make_async_copy(src, dst, local_sem.at[i])
        for i, (src, dst) in enumerate(
            ((first_hbm, first_w), (conv_hbm, conv_w), (patch_hbm, patch_w), (proj_hbm, proj_w))
        )
    ]
    def early():
        for cp in copies:
            cp.start()

    def idle():
        first_taps[...] = jnp.zeros_like(first_taps)
        copies[0].wait()
        for a in range(2):
            for b in range(2):
                for lag in range(3):
                    for q in range(3):
                        for r in range(3):
                            (sub_a, di), (sub_b, dj) = TAPS[a, q], TAPS[b, r]
                            u, v = di + 1 - a, dj + 1 - b
                            at = ((u * 2 + v) * 4 + sub_a * 2 + sub_b) * lat_c
                            first_taps[2 * a + b, lag, at : at + lat_c, :] = first_w[lag * 9 + q * 3 + r]
        for cp in copies[1:]:
            cp.wait()
        whole = proj_w[...]
        high = whole.astype(b16)
        proj_high[...] = high
        proj_low[...] = (whole - high.astype(f32)).astype(b16)

    yield early, idle

    latents = halo_ref[...].reshape(-1, 2 * cols_n).astype(f32)
    total_rows = latents.shape[0]
    token = lax.rem(lax.broadcasted_iota(jnp.int32, latents.shape, 0), per_frame)
    row_id, col_id = token // GRID_W, lax.rem(token, GRID_W)
    lane = lax.broadcasted_iota(jnp.int32, latents.shape, 1)
    for di in (-1, 0, 1):
        moved = []
        for dj in (-1, 0, 1):
            step = GRID_W * di + dj
            value = latents if step == 0 else pltpu.roll(latents, (-step) % total_rows, 0)
            keep = (row_id + di >= 0) & (row_id + di < GRID_H) & (col_id + dj >= 0) & (col_id + dj < GRID_W)
            moved.append(value if step == 0 else jnp.where(keep, value, 0.0))
        for b in range(2):
            pair = jnp.where(lane < cols_n, moved[b], moved[b + 1]).astype(b16)
            for a in range(2):
                u = di + 1 - a
                if 0 <= u < 2:
                    wide_in[2 * a + b, :, u * 2 * cols_n : (u + 1) * 2 * cols_n] = pair

    first_bias = first_bias_ref[...][None, :]
    for ab in range(4):
        summed = None
        for lag in range(3):
            term = jnp.dot(
                wide_in[ab, lag * per_frame : (lag + held) * per_frame, :],
                first_taps[ab, lag],
                preferred_element_type=f32,
            )
            summed = term if summed is None else summed + term
        first_buf[ab] = (summed + first_bias).astype(b16)

    gain = gain_ref[...][None, :]
    token = lax.broadcasted_iota(jnp.int32, (per_frame, ch), 0)
    row_id, col_id = token // GRID_W, lax.rem(token, GRID_W)

    def one_frame(f):
        live = (me * frames_dev - 2 + f) >= 0
        span = slice(f * per_frame, (f + 1) * per_frame)
        for sub_a in range(2):
            for sub_b in range(2):
                first_f = first_buf[2 * sub_a + sub_b, span, :].astype(f32)
                meansq = jnp.mean(first_f * first_f, axis=-1, keepdims=True)
                value = jax.nn.silu(first_f * lax.rsqrt(meansq + 1e-06) * gain)
                value = jnp.where(live, value, 0.0)
                for di in (0, -1 if sub_a else 1):
                    for dj in (0, -1 if sub_b else 1):
                        step = GRID_W * di + dj
                        shifted = value
                        if step:
                            shifted = pltpu.roll(value, (-step) % per_frame, 0)
                            keep = (
                                (row_id + di >= 0)
                                & (row_id + di < GRID_H)
                                & (col_id + dj >= 0)
                                & (col_id + dj < GRID_W)
                            )
                            shifted = jnp.where(keep, shifted, 0.0)
                        shifted = shifted.astype(b16)
                        for (a, q), source_a in TAPS.items():
                            for (b, r), source_b in TAPS.items():
                                if source_a == (sub_a, di) and source_b == (sub_b, dj):
                                    tap = q * 3 + r
                                    window[f, 2 * a + b, :, tap * ch : (tap + 1) * ch] = shifted

    taps_n = 9
    conv_bias = conv_bias_ref[...][None, :]
    for f in range(frames_dev):
        for ab in range(4):
            own = first_buf[ab, (f + 2) * per_frame : (f + 3) * per_frame, :].astype(f32)
            acc[(f * 4 + ab) * per_frame : (f * 4 + ab + 1) * per_frame, :] = own + conv_bias

    frame_rows = 4 * per_frame
    side_at = ch // 256 * 256

    def one_lag(lag):
        rows = window[lag : lag + frames_dev].reshape(frames_dev * frame_rows, taps_n * ch)
        weight = conv_w[lag * taps_n : (lag + 1) * taps_n, :, :side_at].reshape(taps_n * ch, side_at)
        acc[:, :side_at] += jnp.dot(rows, weight, preferred_element_type=f32)

    def one_side(f):
        rows = window[f].reshape(frame_rows, taps_n * ch)
        lags = [lag for lag in range(3) if 0 <= f - lag < frames_dev]
        while lags:
            now, lags = lags[:2], lags[2:]
            weight = jnp.concatenate(
                [
                    conv_w[lag * taps_n : (lag + 1) * taps_n, :, side_at:].reshape(taps_n * ch, ch - side_at)
                    for lag in now
                ],
                axis=1,
            )
            both = jnp.dot(rows, weight, preferred_element_type=f32)
            for i, lag in enumerate(now):
                to = slice((f - lag) * frame_rows, (f - lag + 1) * frame_rows)
                acc[to, side_at:] += both[:, i * (ch - side_at) : (i + 1) * (ch - side_at)]

    for f in range(frames_dev):
        one_frame(f)
    for lag in range(3):
        if lag + frames_dev < held:
            one_frame(lag + frames_dev)
        one_lag(lag)
        one_side(lag)
    for f in range(3, held):
        one_side(f)

    for f in range(frames_dev):
        for a in range(2):
            for b in range(2):
                base = (f * 4 + 2 * a + b) * per_frame
                for i in range(GRID_H):
                    for c in range(pixels.shape[0]):
                        pixels[c, f, 2 * i + a, pl.ds(b, GRID_W, stride=2), :] = acc[
                            pl.ds(base + i * GRID_W, GRID_W), c * 128 : (c + 1) * 128
                        ]
                patches[f * per_frame : (f + 1) * per_frame, (2 * a + b) * ch : (2 * a + b + 1) * ch] = acc[
                    base : base + per_frame, :
                ].astype(b16)
    for c in range(pixels.shape[0]):
        decoded_buf[:, :, :, c * 128 : (c + 1) * 128] = pixels[c].astype(b16)
    out_copy.start()

    embedded = jnp.dot(patches[...], patch_w[...], preferred_element_type=f32).astype(b16).astype(f32)
    centered = embedded - jnp.mean(embedded, axis=-1, keepdims=True)
    variance = jnp.mean(centered * centered, axis=-1, keepdims=True)
    normed = centered * lax.rsqrt(variance + 1e-05)
    pooled = jnp.concatenate(
        [
            jnp.mean(normed[f * per_frame : (f + 1) * per_frame], axis=0, keepdims=True)
            for f in range(frames_dev)
        ],
        axis=0,
    ) * patch_gain_ref[...][None, :]
    centered = pooled - jnp.mean(pooled, axis=-1, keepdims=True)
    variance = jnp.mean(centered * centered, axis=-1, keepdims=True)
    pooled = centered * lax.rsqrt(variance + 1e-05) * post_gain_ref[...][None, :]

    pooled_high = pooled.astype(b16).astype(f32)
    blank = jnp.zeros((16 - 2 * frames_dev, pooled.shape[1]), f32)
    pair = jnp.concatenate([pooled_high, pooled - pooled_high, blank], axis=0).astype(b16)
    main = jnp.dot(pair, proj_high[...], preferred_element_type=f32)
    rest = jnp.dot(pair, proj_low[...], preferred_element_type=f32)
    image = main[:frames_dev] + (main[frames_dev : 2 * frames_dev] + rest[:frames_dev])
    for f in range(frames_dev):
        image_buf[f] = image[f : f + 1, :]

    def image_copy(peer):
        return remote(
            image_buf,
            image_all.at[pl.ds(me * frames_dev, frames_dev)],
            image_send.at[peer],
            image_recv.at[me],
            peer,
        )

    def spread(x, carry):
        image_copy(jnp.bitwise_xor(me, x)).start()
        return carry

    lax.fori_loop(1, n, spread, 0)
    image_all[pl.ds(me * frames_dev, frames_dev)] = image_buf[...]

    def came(x, carry):
        src = jnp.bitwise_xor(me, x)
        block = image_all.at[pl.ds(src * frames_dev, frames_dev)]
        pltpu.make_async_copy(block, block, image_recv.at[src]).wait()
        return carry

    lax.fori_loop(1, n, came, 0)
    text = text_ref[...]
    text_rms = jnp.sqrt(jnp.mean(text * text, keepdims=True) + 1e-06)
    for f in range(frames_dev):
        vector = image_all[order_ref[me * frames_dev + f]]
        image_out[f : f + 1, :] = vector
        inner = jnp.sum(vector * text, keepdims=True)
        image_rms = jnp.sqrt(jnp.mean(vector * vector, keepdims=True) + 1e-06)
        score_out[f] = (100.0 * inner / (TEXT_W * image_rms * text_rms))[0, 0]

    def gone(x, carry):
        image_copy(jnp.bitwise_xor(me, x)).wait_send()
        return carry

    lax.fori_loop(1, n, gone, 0)
    out_copy.wait()
    yield


MIX_IN, DECODE_IN, MIX_SCRATCH, HALO_AT = 10, 10, 35, 16
SMALL_MIX, SMALL_DECODE = (3, 5, 6, 9), (1, 2, 4, 6, 7, 9)


def whole_kernel(n, heads_here, *refs):
    mix_in, refs = refs[:MIX_IN], refs[MIX_IN:]
    decode_in, refs = refs[:DECODE_IN], refs[DECODE_IN:]
    (latent_out, decoded_out, image_out, score_out), refs = refs[:4], refs[4:]
    (text_full, *mix_scratch), decode_scratch = refs[: MIX_SCRATCH + 1], refs[MIX_SCRATCH + 1 :]
    halo_buf = mix_scratch[HALO_AT]
    *decode_scratch, small_sem = decode_scratch
    small_bufs = decode_scratch[-len(SMALL_MIX) - len(SMALL_DECODE) :]
    decode_scratch = decode_scratch[: -len(small_bufs)]
    mix_in, decode_in = list(mix_in), list(decode_in)
    small_copies = []
    for group, places in ((mix_in, SMALL_MIX), (decode_in, SMALL_DECODE)):
        for place in places:
            i = len(small_copies)
            small_copies.append(pltpu.make_async_copy(group[place], small_bufs[i], small_sem.at[i]))
            small_copies[-1].start()
            group[place] = small_bufs[i]
    steps = decode_kernel(n, halo_buf, text_full, *decode_in, decoded_out, image_out, score_out, *decode_scratch)
    start_weights, idle = next(steps)

    def early():
        start_weights()
        for cp in small_copies:
            cp.wait()

    finish = mix_kernel(n, heads_here, *mix_in, early, idle, latent_out, text_full, *mix_scratch)
    next(steps)
    finish()


def everything(
    queries,
    keys,
    values,
    latent_in,
    mod_table,
    step_size,
    timestep,
    head_weight,
    text_table,
    prompt_ids,
    conv_in_weight,
    conv_in_bias,
    norm_gain,
    conv_weight,
    conv_bias,
    patch_weight,
    patch_gain,
    post_gain,
    proj_weight,
    frame_order,
):
    n = lax.axis_size("seq")
    heads_here = HEADS // n
    rows, cols_n = latent_in.shape
    width = text_table.shape[1]
    wide = heads_here * HD
    half = n // 2
    frames_all = timestep.shape[0]
    frames_dev = frames_all // n
    per_frame = rows // frames_dev
    part = (per_frame + 8 * frames_dev, frames_dev * cols_n)
    held = frames_dev + 2
    ch = conv_weight.shape[2]
    text_w = proj_weight.shape[1]
    pixel_shape = (frames_dev, 2 * GRID_H, 2 * GRID_W, ch)
    vmem = pltpu.VMEM
    dma = pltpu.SemaphoreType.DMA
    f32, b16 = jnp.float32, jnp.bfloat16
    far = pl.BlockSpec(memory_space=pltpu.HBM)
    near = pl.BlockSpec(memory_space=pltpu.VMEM)
    scalars = pl.BlockSpec(memory_space=pltpu.SMEM)
    mix_scratch = [
        vmem((heads_here, n, rows, HD), b16),
        vmem((heads_here, n, rows, 2 * HD), b16),
        vmem((n, rows, wide), b16),
        vmem((n,) + part, b16),
        vmem((half,) + part, b16),
        vmem((half,) + part, b16),
        vmem(part, b16),
        vmem(part, b16),
        vmem(mod_table.shape, f32),
        vmem((cols_n, HEADS * HD), f32),
        vmem((frames_all, 2 * cols_n, wide), b16),
        vmem((8, cols_n), f32),
        vmem((2, 8 * frames_dev, frames_dev * cols_n), f32),
        vmem((rows, n * rows), f32),
        vmem((rows, n * rows), f32),
        vmem((2, rows, HD), f32),
        vmem((3, rows, 2 * cols_n), b16),
        vmem((text_table.shape[0] // 128, width, 128), b16),
        vmem((1, n * width), f32),
        vmem((n, 1, n * width), f32),
        dma((heads_here, n)),
        dma((heads_here, n)),
        dma((heads_here, n)),
        dma((heads_here, n)),
        dma((n,)),
        dma((n,)),
        dma((n,)),
        dma((n,)),
        dma,
        dma,
        dma((2,)),
        dma((2,)),
        dma((n,)),
        dma((n,)),
        dma((3,)),
    ]
    decode_scratch = [
        vmem(conv_in_weight.shape, b16),
        vmem((4, 3, 4 * cols_n, ch), b16),
        vmem((4, (held + 2) * per_frame, 4 * cols_n), b16),
        vmem((4, held * per_frame, ch), b16),
        vmem((held, 4, per_frame, 9 * ch), b16),
        vmem(conv_weight.shape, b16),
        vmem((frames_dev * 4 * per_frame, ch), f32),
        vmem((ch // 128, frames_dev, 2 * GRID_H, 2 * GRID_W, 128), f32),
        vmem((frames_dev * per_frame, 4 * ch), b16),
        vmem(patch_weight.shape, b16),
        vmem(proj_weight.shape, f32),
        vmem(proj_weight.shape, b16),
        vmem(proj_weight.shape, b16),
        vmem(pixel_shape, b16),
        vmem((frames_dev, 1, text_w), f32),
        vmem((n * frames_dev, 1, text_w), f32),
        dma((n,)),
        dma((n,)),
        dma((5,)),
        vmem((cols_n, rows), f32),
        pltpu.SMEM(step_size.shape, f32),
        pltpu.SMEM(timestep.shape, jnp.int32),
        pltpu.SMEM(prompt_ids.shape, jnp.int32),
        vmem(conv_in_bias.shape, f32),
        vmem(norm_gain.shape, f32),
        vmem(conv_bias.shape, f32),
        vmem(patch_gain.shape, f32),
        vmem(post_gain.shape, f32),
        pltpu.SMEM(frame_order.shape, jnp.int32),
        dma((len(SMALL_MIX) + len(SMALL_DECODE),)),
    ]
    assert len(mix_scratch) == MIX_SCRATCH
    results = pl.pallas_call(
        functools.partial(whole_kernel, n, heads_here),
        out_shape=(
            jax.ShapeDtypeStruct((cols_n, rows), f32),
            jax.ShapeDtypeStruct(pixel_shape, b16),
            jax.ShapeDtypeStruct((frames_dev, text_w), f32),
            jax.ShapeDtypeStruct((frames_dev,), f32),
        ),
        in_specs=[far] * (MIX_IN + DECODE_IN),
        out_specs=(near, far, near, scalars),
        scratch_shapes=[vmem((1, text_w), f32)] + mix_scratch + decode_scratch,
        compiler_params=pltpu.CompilerParams(
            collective_id=0, has_side_effects=True, vmem_limit_bytes=67043328
        ),
        name="everything",
    )(
        queries,
        keys,
        values,
        latent_in.T,
        mod_table,
        step_size,
        timestep,
        head_weight.T,
        text_table.T,
        prompt_ids,
        conv_in_weight,
        conv_in_bias,
        norm_gain,
        conv_weight,
        conv_bias,
        patch_weight,
        patch_gain,
        post_gain,
        proj_weight,
        frame_order,
    )
    return deliver(*results)


def deliver_kernel(*refs):
    count = len(refs) // 2
    for source, target in zip(refs[: count - 1], refs[count:-1]):
        target[...] = source[...]
    for f in range(refs[-1].shape[0]):
        refs[-1][f] = refs[count - 1][f]


def deliver(*arrays):
    near = pl.BlockSpec(memory_space=pltpu.VMEM)
    specs = [near] * (len(arrays) - 1) + [pl.BlockSpec(memory_space=pltpu.SMEM)]
    return pl.pallas_call(
        deliver_kernel,
        out_shape=[jax.ShapeDtypeStruct(a.shape, a.dtype) for a in arrays],
        in_specs=specs,
        out_specs=specs,
        name="deliver",
    )(*arrays)


def local(
    queries,
    keys,
    values,
    latent_in,
    mod_table,
    step_size,
    timestep,
    head_weight,
    conv_in_weight,
    conv_in_bias,
    norm_gain,
    conv_weight,
    conv_bias,
    patch_weight,
    patch_gain,
    post_gain,
    proj_weight,
    text_table,
    prompt_ids,
    frame_order,
):
    latent_turned, decoded, image_vec, scores = everything(
        queries,
        keys,
        values,
        latent_in,
        mod_table,
        step_size,
        timestep,
        head_weight,
        text_table,
        prompt_ids,
        conv_in_weight,
        conv_in_bias,
        norm_gain,
        conv_weight,
        conv_bias,
        patch_weight,
        patch_gain,
        post_gain,
        proj_weight,
        frame_order,
    )
    return (latent_turned.T, decoded, image_vec, scores)


def solution(mesh):
    in_specs = (
        P(("grp", "seq"), None),
        P(("grp", "seq"), None),
        P(("grp", "seq"), None),
        P(("grp", "seq"), None),
        P(),
        P(),
        P("grp"),
        P(),
        P(),
        P(),
        P(),
        P(),
        P(),
        P(),
        P(),
        P(),
        P(),
        P(None, "seq"),
        P("grp"),
        P("grp"),
    )
    out_specs = (
        P(("grp", "seq"), None),
        P(("grp", "seq"), None, None, None),
        P(("grp", "seq"), None),
        P(("grp", "seq")),
    )
    return jax.shard_map(local, mesh=mesh, in_specs=in_specs, out_specs=out_specs, check_vma=False)
```

```python
import functools

import jax
import jax.numpy as jnp
from jax import lax
from jax.experimental import pallas as pl
from jax.experimental.pallas import tpu as pltpu
from jax.sharding import PartitionSpec as P

GRID_H = 8
GRID_W = 12
HEADS = 32
HD = 128
LAT_C = 16
CH = 384
TEXT_W = 768


highest = lax.Precision.HIGHEST


MESH = pl.DeviceIdType.MESH
AHEAD = 4


def remote(src, dst, send, recv, device):
    return pltpu.make_async_remote_copy(
        src_ref=src, dst_ref=dst, send_sem=send, recv_sem=recv, device_id={"seq": device}, device_id_type=MESH
    )


def mix_kernel(
    n,
    heads_here,
    q_hbm,
    k_hbm,
    v_hbm,
    latent_ref,
    mod_hbm,
    step_ref,
    time_ref,
    weight_hbm,
    table_hbm,
    prompt_ref,
    early,
    idle,
    latent_out,
    text_out,
    k_buf,
    v_buf,
    q_buf,
    part_buf,
    own_buf,
    mirror_buf,
    cross_buf,
    sum_buf,
    mod_buf,
    weight_buf,
    gain_buf,
    shift_buf,
    sum_rows,
    logit_even,
    logit_odd,
    peak_buf,
    halo_buf,
    table_buf,
    text_buf,
    text_all,
    k_send,
    k_recv,
    v_send,
    v_recv,
    q_send,
    q_recv,
    part_send,
    part_recv,
    cross_send,
    cross_recv,
    halo_send,
    halo_recv,
    text_send,
    text_recv,
    local_sem,
):
    me = lax.axis_index("seq")
    half = n // 2
    rows = q_buf.shape[1]
    wide = heads_here * HD
    cols_n = latent_ref.shape[0]
    frames_dev = rows // (GRID_H * GRID_W)
    per_frame = rows // frames_dev
    first_col = pl.multiple_of(me * wide, wide)

    locals_ = [pltpu.make_async_copy(mod_hbm, mod_buf, local_sem.at[0])]
    locals_.append(pltpu.make_async_copy(weight_hbm, weight_buf, local_sem.at[1]))
    own_cp = []
    for h in range(heads_here):
        own_col = pl.ds(pl.multiple_of(me * wide + h * HD, HD), HD)
        own_cp.append(pltpu.make_async_copy(k_hbm.at[:, own_col], k_buf.at[h, me], k_recv.at[h, me]))
        own_cp.append(pltpu.make_async_copy(v_hbm.at[:, own_col], v_buf.at[h, me, :, pl.ds(0, HD)], v_recv.at[h, me]))
    own_cp.append(pltpu.make_async_copy(q_hbm.at[:, pl.ds(first_col, wide)], q_buf.at[me], q_recv.at[me]))

    barrier = pltpu.get_barrier_semaphore()

    def greet(x, carry):
        pl.semaphore_signal(barrier, inc=1, device_id={"seq": jnp.bitwise_xor(me, x)}, device_id_type=MESH)
        return carry

    lax.fori_loop(1, n, greet, 0)
    pl.semaphore_wait(barrier, n - 1)

    def head_copy(hbm, buf, send, recv, h, peer):
        cols = pl.ds(pl.multiple_of(peer * wide + h * HD, HD), HD)
        return remote(
            hbm.at[:, cols], buf.at[h, me, :, pl.ds(0, HD)], send.at[h, peer], recv.at[h, me], peer
        )

    def query_copy(peer):
        cols = pl.ds(pl.multiple_of(peer * wide, wide), wide)
        return remote(q_hbm.at[:, cols], q_buf.at[me], q_send.at[peer], q_recv.at[me], peer)

    def send_some(make, first, last):
        def body(x, carry):
            make(jnp.bitwise_xor(me, x)).start()
            return carry

        lax.fori_loop(first, last, body, 0)

    phases = []
    for h in range(heads_here):
        phases.append(lambda peer, h=h: head_copy(k_hbm, k_buf, k_send, k_recv, h, peer))
        phases.append(lambda peer, h=h: head_copy(v_hbm, v_buf, v_send, v_recv, h, peer))

    def follow(phase):
        def body(x, carry):
            peer = jnp.bitwise_xor(me, x)
            phases[phase](peer).wait_send()
            if phase + 1 < len(phases):
                phases[phase + 1](peer).start()
            else:

                @pl.when(x < half + AHEAD)
                def _():
                    query_copy(peer).start()

            return carry

        lax.fori_loop(half, n, body, 0)

    def follow_query(x):
        query_copy(jnp.bitwise_xor(me, x)).wait_send()

        @pl.when(x + AHEAD < n)
        def _():
            query_copy(jnp.bitwise_xor(me, x + AHEAD)).start()

    send_some(phases[0], 1, n)
    send_some(phases[1], 1, half)
    send_some(query_copy, 1, half)
    for cp in locals_ + own_cp:
        cp.start()
    early()
    for cp in locals_:
        cp.wait()

    lanes = table_buf.shape[2]

    def table_part(i, carry):
        part = table_hbm.at[:, pl.ds(pl.multiple_of(i * lanes, lanes), lanes)]
        pltpu.make_async_copy(part, table_buf.at[i], local_sem.at[2]).start()
        return carry

    lax.fori_loop(0, table_buf.shape[0], table_part, 0)

    weight_own = weight_buf[:, pl.ds(first_col, wide)]

    def prepare(f, carry):
        gain = mod_buf[pl.ds(time_ref[f], 1), 1, pl.ds(first_col, wide)]
        scaled = (1.0 + gain) * weight_own
        high = scaled.astype(jnp.bfloat16)
        low = (scaled - high.astype(jnp.float32)).astype(jnp.bfloat16)
        gain_buf[f] = jnp.concatenate([high, low], axis=0)
        return carry

    lax.fori_loop(0, n * frames_dev, prepare, 0)

    def fill_ones(src, carry):
        for h in range(heads_here):
            v_buf[h, src, :, HD:] = jnp.ones((rows, HD), jnp.bfloat16)
        return carry

    lax.fori_loop(0, n, fill_ones, 0)

    def one_shift(head, carry):
        cols = pl.ds(pl.multiple_of(head * HD, HD), HD)
        shifts = jnp.concatenate(
            [mod_buf[pl.ds(time_ref[me * frames_dev + f], 1), 0, cols] for f in range(frames_dev)] * (8 // frames_dev),
            axis=0,
        )
        return carry + lax.dot_general(
            shifts,
            weight_buf[:, cols],
            (((1,), (1,)), ((), ())),
            precision=highest,
            preferred_element_type=jnp.float32,
        )

    shift_buf[...] = lax.fori_loop(0, HEADS, one_shift, jnp.zeros(shift_buf.shape, jnp.float32))

    words = prompt_ref.shape[0]
    width = table_buf.shape[1]
    lane_ids = lax.broadcasted_iota(jnp.int32, (width, lanes), 1)
    pltpu.make_async_copy(table_buf, table_buf, local_sem.at[2]).wait()

    def one_word(w, carry):
        word = prompt_ref[w]
        block = table_buf[word // lanes]
        return carry + jnp.where(lane_ids == word % lanes, block.astype(jnp.float32), 0.0)

    picked = lax.fori_loop(0, words, one_word, jnp.zeros((width, lanes), jnp.float32))
    own_text = jnp.sum(picked, axis=-1, keepdims=True) / words
    place = (width, n * width)
    own_place = lax.broadcasted_iota(jnp.int32, place, 1) - me * width == lax.broadcasted_iota(
        jnp.int32, place, 0
    )
    text_buf[...] = jnp.sum(jnp.where(own_place, own_text, 0.0), axis=0, keepdims=True)

    def text_copy(peer):
        return remote(text_buf, text_all.at[me], text_send.at[peer], text_recv.at[me], peer)

    send_some(text_copy, 1, n)
    text_all[me] = text_buf[...]
    idle()

    def arrived(buf, recv):
        def body(x, carry):
            block = buf.at[x, :, pl.ds(0, HD)]
            pltpu.make_async_copy(block, block, recv.at[x]).wait()
            return carry

        lax.fori_loop(0, n, body, 0)

    logit_bufs = (logit_even, logit_odd)

    def score(slot, h, src):
        logits = lax.dot_general(
            q_buf[src, :, h * HD : (h + 1) * HD],
            k_buf[h].reshape(n * rows, HD),
            (((1,), (1,)), ((), ())),
            preferred_element_type=jnp.float32,
        )
        logit_bufs[slot][...] = logits
        peak_buf[slot] = jnp.broadcast_to(jnp.max(logits, axis=-1, keepdims=True), (rows, HD))

    def weigh(slot, h, src):
        row_peak = peak_buf[slot, :, 0:1]
        exponent = jnp.exp2((logit_bufs[slot][...] - row_peak) * (HD ** (-0.5) * 1.4426950408889634))
        mixed = jnp.dot(
            exponent.astype(jnp.bfloat16),
            v_buf[h].reshape(n * rows, 2 * HD),
            preferred_element_type=jnp.float32,
        )
        q_buf[src, :, h * HD : (h + 1) * HD] = (mixed[:, :HD] / mixed[:, HD:]).astype(jnp.bfloat16)

    def in_turn(first, heads, waits, done):
        count = half * len(heads)
        unroll = 2 if len(heads) == 1 else len(heads)

        def place(t):
            x = first + lax.rem(t // len(heads), half)
            return x, jnp.bitwise_xor(me, x)

        def begin(t, p, guard):
            x, src = place(t)
            h = heads[p % len(heads)]
            if waits and p % len(heads) == 0:

                @pl.when(guard)
                def _():
                    if first > 0:
                        follow_query(x)
                    pltpu.make_async_copy(q_buf.at[src], q_buf.at[src], q_recv.at[src]).wait()

            score(p % 2, h, src)

        begin(0, 0, me >= 0)

        def body(i, carry):
            for p in range(unroll):
                t = i * unroll + p
                begin(t + 1, p + 1, t + 1 < count)
                x, src = place(t)
                weigh(p % 2, heads[p % len(heads)], src)
                if p % len(heads) == len(heads) - 1:
                    done(x, src)
            return carry

        lax.fori_loop(0, count // unroll, body, 0)

    lane = lax.broadcasted_iota(jnp.int32, (per_frame, frames_dev * cols_n), 1)
    ones = jnp.ones((8, wide), jnp.bfloat16)
    turned = (((1,), (1,)), ((), ()))

    def project(x, src):
        packed = None
        for f in range(frames_dev):
            rows_a = q_buf[src, f * per_frame : (f + 1) * per_frame, :]
            both = lax.dot_general(
                rows_a, gain_buf[src * frames_dev + f], turned, preferred_element_type=jnp.float32
            )
            both = both + pltpu.roll(both, cols_n, 1)
            packed = both if packed is None else jnp.where(lane < f * cols_n, packed, both)
            rows_f = rows_a.astype(jnp.float32)
            squares = lax.dot_general(
                ones, (rows_f * rows_f).astype(jnp.bfloat16), turned, preferred_element_type=jnp.float32
            )
            sum_rows[x % 2, f * 8 : (f + 1) * 8, :per_frame] = squares
        part_buf[x, :per_frame, :] = packed.astype(jnp.bfloat16)
        part_buf[x, per_frame:, :] = sum_rows[x % 2].astype(jnp.bfloat16)

    for h in range(heads_here):
        follow(2 * h)
        if h + 1 < heads_here:
            send_some(phases[2 * h + 2], 1, half)
            send_some(phases[2 * h + 3], 1, half)
        follow(2 * h + 1)
        arrived(k_buf.at[h], k_recv.at[h])
        arrived(v_buf.at[h], v_recv.at[h])
        def near_done(x, src, h=h):
            if h == heads_here - 1:
                project(x, src)

                @pl.when(x > 0)
                def _():
                    remote(part_buf.at[x], own_buf.at[x], part_send.at[x], part_recv.at[x], src).start()

        in_turn(0, [h], h == 0, near_done)

    def far_done(x, src):
        project(x, src)

        @pl.when(x > half)
        def _():
            y = x - half
            to = jnp.bitwise_xor(me, y)
            remote(part_buf.at[x], mirror_buf.at[y], part_send.at[x], part_recv.at[x], to).start()

    in_turn(half, list(range(heads_here)), True, far_done)

    def part_wait(x):
        pltpu.make_async_copy(part_buf.at[x], part_buf.at[x], part_recv.at[x]).wait()

    total = part_buf[half].astype(jnp.float32)
    for y in range(1, half):
        part_wait(half + y)
        total = total + mirror_buf[y].astype(jnp.float32)
    sum_buf[...] = total.astype(jnp.bfloat16)
    cross = remote(sum_buf, cross_buf, cross_send, cross_recv, jnp.bitwise_xor(me, half))
    cross.start()
    total = part_buf[0].astype(jnp.float32)
    for y in range(1, half):
        part_wait(y)
        total = total + own_buf[y].astype(jnp.float32)
    cross.wait()
    total = total + cross_buf[...].astype(jnp.float32)
    diagonal = lax.broadcasted_iota(jnp.int32, (per_frame, per_frame), 0) == lax.broadcasted_iota(
        jnp.int32, (per_frame, per_frame), 1
    )
    latent_rows = jnp.transpose(latent_ref[...])
    pieces = []
    for f in range(frames_dev):
        row_sums = total[per_frame + f * 8 : per_frame + f * 8 + 1, :per_frame]
        meansq = jnp.sum(jnp.where(diagonal, row_sums, 0.0), axis=-1, keepdims=True) / (HEADS * HD)
        prediction = total[:per_frame, f * cols_n : (f + 1) * cols_n] * lax.rsqrt(meansq + 1e-06)
        moved = step_ref[time_ref[me * frames_dev + f]] * (prediction + shift_buf[f : f + 1, :])
        pieces.append(latent_rows[f * per_frame : (f + 1) * per_frame, :] + moved)
    latent_new = jnp.concatenate(pieces, axis=0)
    latent_wide = jnp.concatenate([latent_new, latent_new], axis=1)
    halo_buf[2] = latent_wide.astype(jnp.bfloat16)

    for back in (1, 2):
        step_to = remote(
            halo_buf.at[2], halo_buf.at[2 - back], halo_send.at[back - 1], halo_recv.at[back - 1], me + back
        )

        @pl.when(me + back < n)
        def _(step_to=step_to):
            step_to.start()

        @pl.when(me < back)
        def _(back=back):
            halo_buf[2 - back] = jnp.zeros(halo_buf.shape[1:], jnp.bfloat16)

    latent_out[...] = jnp.transpose(latent_new)

    def text_came(x, carry):
        src = jnp.bitwise_xor(me, x)
        pltpu.make_async_copy(text_all.at[src], text_all.at[src], text_recv.at[src]).wait()
        return carry

    lax.fori_loop(1, n, text_came, 0)
    text_out[...] = functools.reduce(jnp.add, [text_all[x] for x in range(n)])

    for back in (1, 2):
        step_to = remote(
            halo_buf.at[2], halo_buf.at[2 - back], halo_send.at[back - 1], halo_recv.at[back - 1], me + back
        )

        @pl.when(me >= back)
        def _(step_to=step_to):
            step_to.wait_recv()

        @pl.when(me + back < n)
        def _(step_to=step_to):
            step_to.wait_send()


    def finish():
        def near_sent(x, carry):
            for copy in phases + [query_copy]:
                copy(jnp.bitwise_xor(me, x)).wait_send()
            return carry

        def text_sent(x, carry):
            text_copy(jnp.bitwise_xor(me, x)).wait_send()
            return carry

        lax.fori_loop(1, half, near_sent, 0)
        lax.fori_loop(1, n, text_sent, 0)

        def parts_sent(x, carry):
            remote(part_buf.at[x], own_buf.at[0], part_send.at[x], part_recv.at[x], jnp.bitwise_xor(me, 1)).wait_send()
            return carry

        lax.fori_loop(1, half, parts_sent, 0)
        lax.fori_loop(half + 1, n, parts_sent, 0)

    return finish


TAPS = {(a, q): ((a + q - 1) % 2, (a + q - 1) // 2) for a in range(2) for q in range(3)}


def decode_kernel(
    n,
    halo_ref,
    text_ref,
    first_hbm,
    first_bias_ref,
    gain_ref,
    conv_hbm,
    conv_bias_ref,
    patch_hbm,
    patch_gain_ref,
    post_gain_ref,
    proj_hbm,
    order_ref,
    decoded_out,
    image_out,
    score_out,
    first_w,
    first_taps,
    wide_in,
    first_buf,
    window,
    conv_w,
    acc,
    pixels,
    patches,
    patch_w,
    proj_w,
    proj_high,
    proj_low,
    decoded_buf,
    image_buf,
    image_all,
    image_send,
    image_recv,
    local_sem,
):
    me = lax.axis_index("seq")
    per_frame = GRID_H * GRID_W
    frames_dev = image_buf.shape[0]
    held = frames_dev + 2
    cols_n = halo_ref.shape[2] // 2
    lat_c = cols_n // 4
    ch = first_buf.shape[2]
    f32, b16 = jnp.float32, jnp.bfloat16

    out_copy = pltpu.make_async_copy(decoded_buf, decoded_out, local_sem.at[4])
    copies = [
        pltpu.make_async_copy(src, dst, local_sem.at[i])
        for i, (src, dst) in enumerate(
            ((first_hbm, first_w), (conv_hbm, conv_w), (patch_hbm, patch_w), (proj_hbm, proj_w))
        )
    ]
    def early():
        for cp in copies:
            cp.start()

    def idle():
        first_taps[...] = jnp.zeros_like(first_taps)
        copies[0].wait()
        for a in range(2):
            for b in range(2):
                for lag in range(3):
                    for q in range(3):
                        for r in range(3):
                            (sub_a, di), (sub_b, dj) = TAPS[a, q], TAPS[b, r]
                            u, v = di + 1 - a, dj + 1 - b
                            at = ((u * 2 + v) * 4 + sub_a * 2 + sub_b) * lat_c
                            first_taps[2 * a + b, lag, at : at + lat_c, :] = first_w[lag * 9 + q * 3 + r]
        for cp in copies[1:]:
            cp.wait()
        whole = proj_w[...]
        high = whole.astype(b16)
        proj_high[...] = high
        proj_low[...] = (whole - high.astype(f32)).astype(b16)

    yield early, idle

    latents = halo_ref[...].reshape(-1, 2 * cols_n).astype(f32)
    total_rows = latents.shape[0]
    token = lax.rem(lax.broadcasted_iota(jnp.int32, latents.shape, 0), per_frame)
    row_id, col_id = token // GRID_W, lax.rem(token, GRID_W)
    lane = lax.broadcasted_iota(jnp.int32, latents.shape, 1)
    for di in (-1, 0, 1):
        moved = []
        for dj in (-1, 0, 1):
            step = GRID_W * di + dj
            value = latents if step == 0 else pltpu.roll(latents, (-step) % total_rows, 0)
            keep = (row_id + di >= 0) & (row_id + di < GRID_H) & (col_id + dj >= 0) & (col_id + dj < GRID_W)
            moved.append(value if step == 0 else jnp.where(keep, value, 0.0))
        for b in range(2):
            pair = jnp.where(lane < cols_n, moved[b], moved[b + 1]).astype(b16)
            for a in range(2):
                u = di + 1 - a
                if 0 <= u < 2:
                    wide_in[2 * a + b, :, u * 2 * cols_n : (u + 1) * 2 * cols_n] = pair

    first_bias = first_bias_ref[...][None, :]
    for ab in range(4):
        summed = None
        for lag in range(3):
            term = jnp.dot(
                wide_in[ab, lag * per_frame : (lag + held) * per_frame, :],
                first_taps[ab, lag],
                preferred_element_type=f32,
            )
            summed = term if summed is None else summed + term
        first_buf[ab] = (summed + first_bias).astype(b16)

    gain = gain_ref[...][None, :]
    token = lax.broadcasted_iota(jnp.int32, (per_frame, ch), 0)
    row_id, col_id = token // GRID_W, lax.rem(token, GRID_W)

    def one_frame(f):
        live = (me * frames_dev - 2 + f) >= 0
        span = slice(f * per_frame, (f + 1) * per_frame)
        for sub_a in range(2):
            for sub_b in range(2):
                first_f = first_buf[2 * sub_a + sub_b, span, :].astype(f32)
                meansq = jnp.mean(first_f * first_f, axis=-1, keepdims=True)
                value = jax.nn.silu(first_f * lax.rsqrt(meansq + 1e-06) * gain)
                value = jnp.where(live, value, 0.0)
                for di in (0, -1 if sub_a else 1):
                    for dj in (0, -1 if sub_b else 1):
                        step = GRID_W * di + dj
                        shifted = value
                        if step:
                            shifted = pltpu.roll(value, (-step) % per_frame, 0)
                            keep = (
                                (row_id + di >= 0)
                                & (row_id + di < GRID_H)
                                & (col_id + dj >= 0)
                                & (col_id + dj < GRID_W)
                            )
                            shifted = jnp.where(keep, shifted, 0.0)
                        shifted = shifted.astype(b16)
                        for (a, q), source_a in TAPS.items():
                            for (b, r), source_b in TAPS.items():
                                if source_a == (sub_a, di) and source_b == (sub_b, dj):
                                    tap = q * 3 + r
                                    window[f, 2 * a + b, :, tap * ch : (tap + 1) * ch] = shifted

    taps_n = 9
    conv_bias = conv_bias_ref[...][None, :]
    for f in range(frames_dev):
        for ab in range(4):
            own = first_buf[ab, (f + 2) * per_frame : (f + 3) * per_frame, :].astype(f32)
            acc[(f * 4 + ab) * per_frame : (f * 4 + ab + 1) * per_frame, :] = own + conv_bias

    frame_rows = 4 * per_frame
    side_at = ch // 256 * 256

    def one_lag(lag):
        rows = window[lag : lag + frames_dev].reshape(frames_dev * frame_rows, taps_n * ch)
        weight = conv_w[lag * taps_n : (lag + 1) * taps_n, :, :side_at].reshape(taps_n * ch, side_at)
        acc[:, :side_at] += jnp.dot(rows, weight, preferred_element_type=f32)

    def one_side(f):
        rows = window[f].reshape(frame_rows, taps_n * ch)
        lags = [lag for lag in range(3) if 0 <= f - lag < frames_dev]
        while lags:
            now, lags = lags[:2], lags[2:]
            weight = jnp.concatenate(
                [
                    conv_w[lag * taps_n : (lag + 1) * taps_n, :, side_at:].reshape(taps_n * ch, ch - side_at)
                    for lag in now
                ],
                axis=1,
            )
            both = jnp.dot(rows, weight, preferred_element_type=f32)
            for i, lag in enumerate(now):
                to = slice((f - lag) * frame_rows, (f - lag + 1) * frame_rows)
                acc[to, side_at:] += both[:, i * (ch - side_at) : (i + 1) * (ch - side_at)]

    for f in range(frames_dev):
        one_frame(f)
    for lag in range(3):
        if lag + frames_dev < held:
            one_frame(lag + frames_dev)
        one_lag(lag)
        one_side(lag)
    for f in range(3, held):
        one_side(f)

    for f in range(frames_dev):
        for a in range(2):
            for b in range(2):
                base = (f * 4 + 2 * a + b) * per_frame
                for i in range(GRID_H):
                    for c in range(pixels.shape[0]):
                        pixels[c, f, 2 * i + a, pl.ds(b, GRID_W, stride=2), :] = acc[
                            pl.ds(base + i * GRID_W, GRID_W), c * 128 : (c + 1) * 128
                        ]
                patches[f * per_frame : (f + 1) * per_frame, (2 * a + b) * ch : (2 * a + b + 1) * ch] = acc[
                    base : base + per_frame, :
                ].astype(b16)
    for c in range(pixels.shape[0]):
        decoded_buf[:, :, :, c * 128 : (c + 1) * 128] = pixels[c].astype(b16)
    out_copy.start()

    embedded = jnp.dot(patches[...], patch_w[...], preferred_element_type=f32).astype(b16).astype(f32)
    centered = embedded - jnp.mean(embedded, axis=-1, keepdims=True)
    variance = jnp.mean(centered * centered, axis=-1, keepdims=True)
    normed = centered * lax.rsqrt(variance + 1e-05)
    pooled = jnp.concatenate(
        [
            jnp.mean(normed[f * per_frame : (f + 1) * per_frame], axis=0, keepdims=True)
            for f in range(frames_dev)
        ],
        axis=0,
    ) * patch_gain_ref[...][None, :]
    centered = pooled - jnp.mean(pooled, axis=-1, keepdims=True)
    variance = jnp.mean(centered * centered, axis=-1, keepdims=True)
    pooled = centered * lax.rsqrt(variance + 1e-05) * post_gain_ref[...][None, :]

    pooled_high = pooled.astype(b16).astype(f32)
    blank = jnp.zeros((16 - 2 * frames_dev, pooled.shape[1]), f32)
    pair = jnp.concatenate([pooled_high, pooled - pooled_high, blank], axis=0).astype(b16)
    main = jnp.dot(pair, proj_high[...], preferred_element_type=f32)
    rest = jnp.dot(pair, proj_low[...], preferred_element_type=f32)
    image = main[:frames_dev] + (main[frames_dev : 2 * frames_dev] + rest[:frames_dev])
    for f in range(frames_dev):
        image_buf[f] = image[f : f + 1, :]

    def image_copy(peer):
        return remote(
            image_buf,
            image_all.at[pl.ds(me * frames_dev, frames_dev)],
            image_send.at[peer],
            image_recv.at[me],
            peer,
        )

    def spread(x, carry):
        image_copy(jnp.bitwise_xor(me, x)).start()
        return carry

    lax.fori_loop(1, n, spread, 0)
    image_all[pl.ds(me * frames_dev, frames_dev)] = image_buf[...]

    def came(x, carry):
        src = jnp.bitwise_xor(me, x)
        block = image_all.at[pl.ds(src * frames_dev, frames_dev)]
        pltpu.make_async_copy(block, block, image_recv.at[src]).wait()
        return carry

    lax.fori_loop(1, n, came, 0)
    text = text_ref[...]
    text_rms = jnp.sqrt(jnp.mean(text * text, keepdims=True) + 1e-06)
    for f in range(frames_dev):
        vector = image_all[order_ref[me * frames_dev + f]]
        image_out[f : f + 1, :] = vector
        inner = jnp.sum(vector * text, keepdims=True)
        image_rms = jnp.sqrt(jnp.mean(vector * vector, keepdims=True) + 1e-06)
        score_out[f] = (100.0 * inner / (TEXT_W * image_rms * text_rms))[0, 0]

    def gone(x, carry):
        image_copy(jnp.bitwise_xor(me, x)).wait_send()
        return carry

    lax.fori_loop(1, n, gone, 0)
    out_copy.wait()
    yield


MIX_IN, DECODE_IN, MIX_SCRATCH, HALO_AT = 10, 10, 35, 16
SMALL_MIX, SMALL_DECODE = (3, 5, 6, 9), (1, 2, 4, 6, 7, 9)


def whole_kernel(n, heads_here, *refs):
    mix_in, refs = refs[:MIX_IN], refs[MIX_IN:]
    decode_in, refs = refs[:DECODE_IN], refs[DECODE_IN:]
    (latent_out, decoded_out, image_out, score_out), refs = refs[:4], refs[4:]
    (text_full, *mix_scratch), decode_scratch = refs[: MIX_SCRATCH + 1], refs[MIX_SCRATCH + 1 :]
    halo_buf = mix_scratch[HALO_AT]
    *decode_scratch, small_sem = decode_scratch
    small_bufs = decode_scratch[-len(SMALL_MIX) - len(SMALL_DECODE) :]
    decode_scratch = decode_scratch[: -len(small_bufs)]
    mix_in, decode_in = list(mix_in), list(decode_in)
    small_copies = []
    for group, places in ((mix_in, SMALL_MIX), (decode_in, SMALL_DECODE)):
        for place in places:
            i = len(small_copies)
            small_copies.append(pltpu.make_async_copy(group[place], small_bufs[i], small_sem.at[i]))
            small_copies[-1].start()
            group[place] = small_bufs[i]
    steps = decode_kernel(n, halo_buf, text_full, *decode_in, decoded_out, image_out, score_out, *decode_scratch)
    start_weights, idle = next(steps)

    def early():
        start_weights()
        for cp in small_copies:
            cp.wait()

    finish = mix_kernel(n, heads_here, *mix_in, early, idle, latent_out, text_full, *mix_scratch)
    next(steps)
    finish()


def everything(
    queries,
    keys,
    values,
    latent_in,
    mod_table,
    step_size,
    timestep,
    head_weight,
    text_table,
    prompt_ids,
    conv_in_weight,
    conv_in_bias,
    norm_gain,
    conv_weight,
    conv_bias,
    patch_weight,
    patch_gain,
    post_gain,
    proj_weight,
    frame_order,
):
    n = lax.axis_size("seq")
    heads_here = HEADS // n
    rows, cols_n = latent_in.shape
    width = text_table.shape[1]
    wide = heads_here * HD
    half = n // 2
    frames_all = timestep.shape[0]
    frames_dev = frames_all // n
    per_frame = rows // frames_dev
    part = (per_frame + 8 * frames_dev, frames_dev * cols_n)
    held = frames_dev + 2
    ch = conv_weight.shape[2]
    text_w = proj_weight.shape[1]
    pixel_shape = (frames_dev, 2 * GRID_H, 2 * GRID_W, ch)
    vmem = pltpu.VMEM
    dma = pltpu.SemaphoreType.DMA
    f32, b16 = jnp.float32, jnp.bfloat16
    far = pl.BlockSpec(memory_space=pltpu.HBM)
    near = pl.BlockSpec(memory_space=pltpu.VMEM)
    scalars = pl.BlockSpec(memory_space=pltpu.SMEM)
    mix_scratch = [
        vmem((heads_here, n, rows, HD), b16),
        vmem((heads_here, n, rows, 2 * HD), b16),
        vmem((n, rows, wide), b16),
        vmem((n,) + part, b16),
        vmem((half,) + part, b16),
        vmem((half,) + part, b16),
        vmem(part, b16),
        vmem(part, b16),
        vmem(mod_table.shape, f32),
        vmem((cols_n, HEADS * HD), f32),
        vmem((frames_all, 2 * cols_n, wide), b16),
        vmem((8, cols_n), f32),
        vmem((2, 8 * frames_dev, frames_dev * cols_n), f32),
        vmem((rows, n * rows), f32),
        vmem((rows, n * rows), f32),
        vmem((2, rows, HD), f32),
        vmem((3, rows, 2 * cols_n), b16),
        vmem((text_table.shape[0] // 128, width, 128), b16),
        vmem((1, n * width), f32),
        vmem((n, 1, n * width), f32),
        dma((heads_here, n)),
        dma((heads_here, n)),
        dma((heads_here, n)),
        dma((heads_here, n)),
        dma((n,)),
        dma((n,)),
        dma((n,)),
        dma((n,)),
        dma,
        dma,
        dma((2,)),
        dma((2,)),
        dma((n,)),
        dma((n,)),
        dma((3,)),
    ]
    decode_scratch = [
        vmem(conv_in_weight.shape, b16),
        vmem((4, 3, 4 * cols_n, ch), b16),
        vmem((4, (held + 2) * per_frame, 4 * cols_n), b16),
        vmem((4, held * per_frame, ch), b16),
        vmem((held, 4, per_frame, 9 * ch), b16),
        vmem(conv_weight.shape, b16),
        vmem((frames_dev * 4 * per_frame, ch), f32),
        vmem((ch // 128, frames_dev, 2 * GRID_H, 2 * GRID_W, 128), f32),
        vmem((frames_dev * per_frame, 4 * ch), b16),
        vmem(patch_weight.shape, b16),
        vmem(proj_weight.shape, f32),
        vmem(proj_weight.shape, b16),
        vmem(proj_weight.shape, b16),
        vmem(pixel_shape, b16),
        vmem((frames_dev, 1, text_w), f32),
        vmem((n * frames_dev, 1, text_w), f32),
        dma((n,)),
        dma((n,)),
        dma((5,)),
        vmem((cols_n, rows), f32),
        pltpu.SMEM(step_size.shape, f32),
        pltpu.SMEM(timestep.shape, jnp.int32),
        pltpu.SMEM(prompt_ids.shape, jnp.int32),
        vmem(conv_in_bias.shape, f32),
        vmem(norm_gain.shape, f32),
        vmem(conv_bias.shape, f32),
        vmem(patch_gain.shape, f32),
        vmem(post_gain.shape, f32),
        pltpu.SMEM(frame_order.shape, jnp.int32),
        dma((len(SMALL_MIX) + len(SMALL_DECODE),)),
    ]
    assert len(mix_scratch) == MIX_SCRATCH
    results = pl.pallas_call(
        functools.partial(whole_kernel, n, heads_here),
        out_shape=(
            jax.ShapeDtypeStruct((cols_n, rows), f32),
            jax.ShapeDtypeStruct(pixel_shape, b16),
            jax.ShapeDtypeStruct((frames_dev, text_w), f32),
            jax.ShapeDtypeStruct((frames_dev,), f32),
        ),
        in_specs=[far] * (MIX_IN + DECODE_IN),
        out_specs=(near, far, near, scalars),
        scratch_shapes=[vmem((1, text_w), f32)] + mix_scratch + decode_scratch,
        compiler_params=pltpu.CompilerParams(
            collective_id=0, has_side_effects=True, vmem_limit_bytes=67043328
        ),
        name="everything",
    )(
        queries,
        keys,
        values,
        latent_in.T,
        mod_table,
        step_size,
        timestep,
        head_weight.T,
        text_table.T,
        prompt_ids,
        conv_in_weight,
        conv_in_bias,
        norm_gain,
        conv_weight,
        conv_bias,
        patch_weight,
        patch_gain,
        post_gain,
        proj_weight,
        frame_order,
    )
    return deliver(*results)


def deliver_kernel(*refs):
    count = len(refs) // 2
    for source, target in zip(refs[: count - 1], refs[count:-1]):
        target[...] = source[...]
    for f in range(refs[-1].shape[0]):
        refs[-1][f] = refs[count - 1][f]


def deliver(*arrays):
    near = pl.BlockSpec(memory_space=pltpu.VMEM)
    specs = [near] * (len(arrays) - 1) + [pl.BlockSpec(memory_space=pltpu.SMEM)]
    return pl.pallas_call(
        deliver_kernel,
        out_shape=[jax.ShapeDtypeStruct(a.shape, a.dtype) for a in arrays],
        in_specs=specs,
        out_specs=specs,
        name="deliver",
    )(*arrays)


def local(
    queries,
    keys,
    values,
    latent_in,
    mod_table,
    step_size,
    timestep,
    head_weight,
    conv_in_weight,
    conv_in_bias,
    norm_gain,
    conv_weight,
    conv_bias,
    patch_weight,
    patch_gain,
    post_gain,
    proj_weight,
    text_table,
    prompt_ids,
    frame_order,
):
    latent_turned, decoded, image_vec, scores = everything(
        queries,
        keys,
        values,
        latent_in,
        mod_table,
        step_size,
        timestep,
        head_weight,
        text_table,
        prompt_ids,
        conv_in_weight,
        conv_in_bias,
        norm_gain,
        conv_weight,
        conv_bias,
        patch_weight,
        patch_gain,
        post_gain,
        proj_weight,
        frame_order,
    )
    return (latent_turned.T, decoded, image_vec, scores)


def solution(mesh):
    in_specs = (
        P(("grp", "seq"), None),
        P(("grp", "seq"), None),
        P(("grp", "seq"), None),
        P(("grp", "seq"), None),
        P(),
        P(),
        P("grp"),
        P(),
        P(),
        P(),
        P(),
        P(),
        P(),
        P(),
        P(),
        P(),
        P(),
        P(None, "seq"),
        P("grp"),
        P("grp"),
    )
    out_specs = (
        P(("grp", "seq"), None),
        P(("grp", "seq"), None, None, None),
        P(("grp", "seq"), None),
        P(("grp", "seq")),
    )
    return jax.shard_map(local, mesh=mesh, in_specs=in_specs, out_specs=out_specs, check_vma=False)
```
